32 devices in a mesh: parts: 2 (over y), row: 4 (over x, core), dp: 4 (over z).
Axes of the slice: x: 2, y: 2, z: 4, core: 2. Of those that a mesh axis runs over, the one named last changes fastest.
Arguments:
- activations: bfloat16 [1024, 13312], P(('parts', 'dp'), 'row'), parts along dimension 0, may hold values from -6 to 6
- cotangent: bfloat16 [1024, 8192], P(('parts', 'dp'), 'row'), parts along dimension 0, may hold values from -0.19921875 to 0.19921875
- forget_labels: int32 [1024], P(('parts', 'dp')), parts along dimension 0, may hold values 0 or 1
- kept_blocks: bfloat16 [4, 256, 128, 128], P('row', 'dp'), may hold values from -0.09375 to 0.09375
- block_ids: int32 [4, 256], P('row', 'dp'), may hold values from -1 to 1663, as said below
- adapter_a: bfloat16 [13312, 64], P('row'), may hold values from -0.0546875 to 0.0546875
- output_adapter: bfloat16 [64, 8192], P(None, 'row'), may hold values from -0.75 to 0.75
Outputs:
- projected: bfloat16 [1024, 8192], P(('parts', 'dp'), 'row'), parts along dimension 0
- input_adapter_gradient: float32 [26624, 64], P(('parts', 'row')), parts along dimension 0
- output_adapter_gradient: float32 [128, 8192], P('parts', 'row'), parts along dimension 0
The draws below stay inside these ranges and needn't reach their ends.
There are 2 independent parts, one for each index of `parts`. The reference program is written for one: setup_inputs(seed, part) draws one part's arguments, and reference() takes and returns one part's arrays. A program takes and returns all parts, laid end to end along the dimension named above; an argument that names none is the same for every part. Nothing has to cross between parts.
Inputs may be any that keep to these rules, and one draw needn't show every extreme that they name: Each row of block_ids names distinct blocks of its row shard, live slots first and -1 after them; one row shard fills all 256 slots and the emptiest fills half of them; every row shard holds its last block.
All inputs are finite; a program needn't handle non-finite values. No bound on the sum of `forget_labels` on one device may be relied on, other than what follows from the above.
Results may differ from the reference program's by a relative error of at most 0.0048.
Values may be sent and summed in bfloat16 or wider, within the bound.
No kernel may reach another device: no remote copies, remote signals or barrier semaphores. Data moves between devices by JAX's collectives and lax.ppermute only.
A program may use at most 192 MiB of HBM per device.

```python
import jax
import jax.numpy as jnp
from jax import lax

D = 8192
FF_DEV = 3328
RANK = 64
BLK = 128
CAP_DEV = 64
FF = 13312
TOKENS = 512
SLOTS = 256
N_ROW = 4
N_DP = 4


def shard_picks(single, tile_count, slots, live):
    key_perm, key_spot = jax.random.split(single)
    order = jax.random.permutation(key_perm, tile_count)
    where_last = jnp.argmax(order == tile_count - 1).astype(jnp.int32)
    spot = jax.random.randint(key_spot, (), 0, live).astype(jnp.int32)
    moved = order[spot]
    order = order.at[where_last].set(moved)
    order = order.at[spot].set(tile_count - 1)
    return order[:slots]


def draw_block_ids(key, part):
    tile_count = FF_DEV // BLK * (D // BLK)
    slots = N_DP * CAP_DEV
    key_rank, key_pick = jax.random.split(jax.random.fold_in(key, 7))
    ranking = jax.random.permutation(key_rank, N_ROW)
    least = slots // 2
    counts = least + (slots - least) * ranking // max(N_ROW - 1, 1)
    picks = jax.vmap(lambda single, live: shard_picks(single, tile_count, slots, live))(jax.random.split(key_pick, N_ROW), counts)
    position = jnp.arange(slots)[None, :]
    return jnp.where(position < counts[:, None], picks, -1).astype(jnp.int32)


def with_ends(drawn, own_key, low, top_value):
    spot = [jax.random.randint(jax.random.fold_in(own_key, axis), (), 0, length) for axis, length in enumerate(drawn.shape)]
    main_axis = drawn.shape.index(max(drawn.shape))
    next_to = spot[:main_axis] + [(spot[main_axis] + 1) % drawn.shape[main_axis]] + spot[main_axis + 1:]
    return drawn.at[tuple(spot)].set(low).at[tuple(next_to)].set(top_value)


def block_scale(own_key, dims, pieces, low, largest):
    level, own = 1.0, jax.random.fold_in(own_key, 6)
    for dim, shards_of in pieces:
        steps = jnp.exp(jax.random.uniform(jax.random.fold_in(own, dim), (shards_of,), jnp.float32, low / len(pieces), largest / len(pieces)))
        level = level * jnp.repeat(steps, dims[dim] // shards_of).reshape([-1 if axis == dim else 1 for axis in range(len(dims))])
    return level


def bell_draw(stream_key, dims, scale, bound, cuts=(), held_as=jnp.bfloat16):
    array = jax.random.normal(stream_key, dims, jnp.float32) * scale
    if len(cuts) > 0:
        array = block_scale(stream_key, dims, cuts, -0.22, 0.18) * array
    return jnp.clip(array, min=-bound, max=bound).astype(held_as)


def setup_inputs(seed: int = 0, part: int = 0) -> dict:
    key_of = jax.random.split(jax.random.key(seed), 8)
    part_splits = jax.random.split(jax.random.fold_in(key_of[7], part), 8)
    return {
        "activations": bell_draw(part_splits[0], (TOKENS, FF), 1.0, 6.0, ((0, 4), (1, 4))),
        "cotangent": bell_draw(part_splits[1], (TOKENS, D), 0.03125, 0.19921875, ((0, 4), (1, 4))),
        "forget_labels": with_ends((jax.random.randint(part_splits[2], (TOKENS,), 0, 4) < 1).astype(jnp.int32), jax.random.fold_in(part_splits[2], 1), 0, 1),
        "kept_blocks": bell_draw(key_of[3], (N_ROW, SLOTS, BLK, BLK), (FF * 3 // 10) ** -0.5, 0.09375, ((0, 4), (1, 4))),
        "block_ids": draw_block_ids(jax.random.fold_in(key_of[7], 71), part),
        "adapter_a": bell_draw(key_of[5], (FF, RANK), FF ** -0.5, 0.0546875, ((0, 4),)),
        "output_adapter": bell_draw(key_of[6], (RANK, D), RANK ** -0.5, 0.75, ((1, 4),)),
    }


adapter_scale = 2.0


def reference(activations, cotangent, forget_labels, kept_blocks, block_ids, adapter_a, output_adapter):
    row_blocks = FF_DEV // BLK
    col_blocks = D // BLK
    shards = activations.reshape(TOKENS, N_ROW, FF_DEV).transpose(1, 0, 2)

    def add_shard(total, item):
        shard_rows, shard_blocks, shard_ids = item
        slots = jnp.where(shard_ids >= 0, shard_ids, row_blocks * col_blocks).astype(jnp.int32)
        dense = jnp.zeros((row_blocks * col_blocks, BLK, BLK), shard_blocks.dtype)
        dense = dense.at[slots].set(shard_blocks, mode="drop")
        dense = dense.reshape(row_blocks, col_blocks, BLK, BLK).transpose(0, 2, 1, 3).reshape(FF_DEV, D)
        return total + jnp.dot(shard_rows, dense, preferred_element_type=jnp.float32), None

    frozen_product, unused = lax.scan(add_shard, jnp.zeros((TOKENS, D), jnp.float32), (shards, kept_blocks, block_ids))
    low = jnp.dot(activations, adapter_a, preferred_element_type=jnp.float32)
    low_rank_output = low.astype(jnp.bfloat16)
    projected = (frozen_product + adapter_scale * jnp.dot(low_rank_output, output_adapter, preferred_element_type=jnp.float32)).astype(jnp.bfloat16)
    signs = (1 - 2 * forget_labels).astype(cotangent.dtype)
    signed_cotangent = cotangent * signs[:, None]
    output_adapter_gradient = adapter_scale * jnp.dot(low_rank_output.T, signed_cotangent, preferred_element_type=jnp.float32)
    back = jnp.dot(signed_cotangent, output_adapter.T, preferred_element_type=jnp.float32)
    backward_output_adapter = back.astype(jnp.bfloat16)
    input_adapter_gradient = adapter_scale * jnp.dot(activations.T, backward_output_adapter, preferred_element_type=jnp.float32)
    return projected, input_adapter_gradient, output_adapter_gradient
```

```python
import functools

import jax
import jax.numpy as jnp
from jax import lax
from jax.experimental import pallas as pl
from jax.experimental.pallas import tpu as pltpu
from jax.sharding import PartitionSpec as P

D = 8192

adapter_scale = 2.0

F32 = jnp.float32
BF16 = jnp.bfloat16


def fill_tiles(tiles_ref, own_ref, mate_ref):
    row_blocks, _, tile = tiles_ref.shape
    tokens = own_ref.shape[0]
    for i in range(row_blocks):
        tiles_ref[i, :tokens, :] = own_ref[:, i * tile:(i + 1) * tile]
        tiles_ref[i, tokens:, :] = mate_ref[:, i * tile:(i + 1) * tile]


def add_blocks(sum_ref, tiles_ref, blocks_ref, ids_ref, base, col_blocks, unroll):
    count = blocks_ref.shape[0]

    def one(step, carry):
        for u in range(unroll):
            k = step * unroll + u
            ident = ids_ref[base + k]
            live = ident >= 0
            row = jnp.where(live, ident, 0) // col_blocks
            col = jnp.where(live, ident % col_blocks, col_blocks)
            sum_ref[col] += jnp.dot(tiles_ref[row], blocks_ref[k], preferred_element_type=F32)
        return carry

    lax.fori_loop(0, count // unroll, one, 0)


def first_kernel(ids_ref, own_ref, mate_ref, blocks_ref, total_ref, tiles_ref, sum_ref, *, col_blocks):
    sum_ref[...] = jnp.zeros_like(sum_ref)
    fill_tiles(tiles_ref, own_ref, mate_ref)
    add_blocks(sum_ref, tiles_ref, blocks_ref, ids_ref, 0, col_blocks, 8)
    total_ref[...] = sum_ref[:col_blocks]


def more_kernel(base_ref, ids_ref, own_ref, mate_ref, total_in_ref, *rest, col_blocks, count):
    blocks, (total_ref, tiles_ref, sum_ref) = rest[:count], rest[count:]
    fill_tiles(tiles_ref, own_ref, mate_ref)
    sum_ref[:col_blocks] = total_in_ref[...]
    for j, blocks_ref in enumerate(blocks):
        add_blocks(sum_ref, tiles_ref, blocks_ref, ids_ref, base_ref[j], col_blocks, blocks_ref.shape[0])
    total_ref[...] = sum_ref[:col_blocks]


def last_kernel(base_ref, ids_ref, own_ref, mate_ref, total_in_ref, *rest, col_blocks, count):
    blocks, (send_mate, keep_mate, send_own, keep_own, tiles_ref, sum_ref) = rest[:count], rest[count:]
    tokens = own_ref.shape[0]
    chips, share = keep_own.shape[0], keep_own.shape[1]
    fill_tiles(tiles_ref, own_ref, mate_ref)
    sum_ref[:col_blocks] = total_in_ref[...]
    for j, blocks_ref in enumerate(blocks):
        add_blocks(sum_ref, tiles_ref, blocks_ref, ids_ref, base_ref[j], col_blocks, blocks_ref.shape[0])
    core = base_ref[count]
    for chip in range(chips):
        mine = (2 * chip + core) * share
        other = (2 * chip + 1 - core) * share
        for q in range(share):
            send_mate[chip, q] = sum_ref[other + q, tokens:, :].astype(BF16)
            keep_mate[chip, q] = sum_ref[mine + q, tokens:, :]
            send_own[chip, q] = sum_ref[other + q, :tokens, :].astype(BF16)
            keep_own[chip, q] = sum_ref[mine + q, :tokens, :]


def final_kernel(low_ref, adapter_ref, keep_ref, core_ref, *rest):
    pieces, out_ref = rest[:-1], rest[-1]
    share, _, tile = keep_ref.shape
    for q in range(share):
        total = keep_ref[q] + core_ref[q].astype(F32)
        for piece in pieces:
            total += piece[q].astype(F32)
        cols = slice(q * tile, (q + 1) * tile)
        extra = jnp.dot(low_ref[...], adapter_ref[:, cols], preferred_element_type=F32)
        out_ref[:, cols] = (total + adapter_scale * extra).astype(BF16)


VMEM_LIMIT = 48 * 1024 * 1024
smem = functools.partial(pl.BlockSpec, memory_space=pltpu.SMEM)
vmem = functools.partial(pl.BlockSpec, memory_space=pltpu.VMEM)


def call(kernel, outs, scratch, scalars, arrays):
    return pl.pallas_call(
        kernel,
        out_shape=outs,
        in_specs=[smem()] * len(scalars) + [vmem()] * len(arrays),
        out_specs=jax.tree.map(lambda _: vmem(), outs),
        scratch_shapes=scratch,
        compiler_params=pltpu.CompilerParams(vmem_limit_bytes=VMEM_LIMIT),
    )(*scalars, *arrays)


def make_body(n_parts, n_row, n_dp):
    chips = n_row // 2
    group = n_dp // 2

    def core_swap(value):
        return lax.ppermute(value, "row", [(i, i ^ 1) for i in range(n_row)])

    def chip_shift(value, d):
        pairs = [(2 * a + c, 2 * ((a + d) % chips) + c) for a in range(chips) for c in range(2)]
        return lax.ppermute(value, "row", pairs)

    def mate_swap(value):
        return lax.ppermute(value, "dp", [(i, i ^ 1) for i in range(n_dp)])

    def group_shift(value, d):
        pairs = [(2 * a + h, 2 * ((a + d) % group) + h) for a in range(group) for h in range(2)]
        return lax.ppermute(value, "dp", pairs)

    def part_shift(value, d):
        return lax.ppermute(value, "parts", [(i, (i + d) % n_parts) for i in range(n_parts)])

    def body(activations, cotangent, forget_labels, kept_blocks, block_ids, adapter_a, output_adapter):
        tokens, shard_rows = activations.shape
        rank = adapter_a.shape[1]
        feats = cotangent.shape[1]
        tile = kept_blocks.shape[-1]
        slots = kept_blocks.shape[1]
        row_blocks = shard_rows // tile
        col_blocks = D // tile
        share = col_blocks // n_row
        part = lax.axis_index("parts")
        row_index = lax.axis_index("row")
        dp_index = lax.axis_index("dp")
        core, chip = row_index % 2, row_index // 2
        half_bit = dp_index % 2
        blocks = kept_blocks[0]
        ids = block_ids[0]

        held = slots // n_parts
        chunks = 4
        size = held // chunks
        own_share = lax.dynamic_slice_in_dim(blocks, part * held, held, axis=0)
        mate_activations = mate_swap(activations)
        far_ids = [group_shift(ids, d) for d in range(1, group)]
        arrivals = []
        for d in range(1, group):
            for i in range(chunks):
                direct = group_shift(own_share[i * size:(i + 1) * size], d)
                arrivals.append((direct, d, 0, i))
        direct_last = arrivals[-1][0]
        for direct, d, _, i in list(arrivals):
            for e in range(1, n_parts):
                arrivals.append((part_shift(direct, e), d, e, i))

        signs = (1 - 2 * forget_labels).astype(F32)[:, None]
        low_part = jnp.dot(activations, adapter_a, preferred_element_type=F32)
        back_part = signs * lax.dot_general(
            cotangent, output_adapter, (((1,), (1,)), ((), ())), preferred_element_type=F32
        )
        both = jnp.concatenate([low_part, back_part], axis=1)
        both = both + core_swap(both)
        pieces = jnp.zeros((chips,) + both.shape, F32)
        pieces = lax.dynamic_update_index_in_dim(pieces, both, chip, 0)
        for d in range(1, chips):
            pieces = lax.dynamic_update_index_in_dim(pieces, chip_shift(both, d), (chip - d) % chips, 0)
        both = pieces.sum(axis=0).astype(BF16)
        low_b, back_b = both[:, :rank], both[:, rank:]
        mate_back_b = mate_swap(back_b)

        contract_tokens = (((0,), (0,)), ((), ()))
        in_grad = adapter_scale * (
            lax.dot_general(back_b, activations, contract_tokens, preferred_element_type=F32)
            + lax.dot_general(mate_back_b, mate_activations, contract_tokens, preferred_element_type=F32)
        )
        out_grad = adapter_scale * lax.dot_general(
            low_b * signs.astype(BF16), cotangent, contract_tokens, preferred_element_type=F32
        )
        in_half, out_half = shard_rows // 2, feats // 2
        in_mine = lax.dynamic_slice_in_dim(in_grad, half_bit * in_half, in_half, axis=1)
        out_mine = lax.dynamic_slice_in_dim(out_grad, half_bit * out_half, out_half, axis=1)
        out_other = lax.dynamic_slice_in_dim(out_grad, (1 - half_bit) * out_half, out_half, axis=1)
        out_mine = out_mine + mate_swap(out_other)
        grads = jnp.concatenate([in_mine, out_mine], axis=1).astype(BF16)
        grads, direct_last = lax.optimization_barrier((grads, direct_last))
        arrivals = [
            (direct_last,) + item[1:] if (item[1], item[2], item[3]) == (group - 1, 0, chunks - 1) else item
            for item in arrivals
        ]
        pieces = jnp.zeros((group,) + grads.shape, BF16)
        pieces = lax.dynamic_update_index_in_dim(pieces, grads, dp_index // 2, 0)
        for d in range(1, group):
            pieces = lax.dynamic_update_index_in_dim(
                pieces, group_shift(grads, d), (dp_index // 2 - d) % group, 0
            )
        grads = pieces.astype(F32).sum(axis=0)
        mate_grads = mate_swap(grads)
        low_side = jnp.where(half_bit == 0, grads, mate_grads)
        high_side = jnp.where(half_bit == 0, mate_grads, grads)
        input_adapter_gradient = jnp.concatenate([low_side[:, :in_half], high_side[:, :in_half]], axis=1).T
        output_adapter_gradient = jnp.concatenate([low_side[:, in_half:], high_side[:, in_half:]], axis=1)

        both_tokens = 2 * tokens
        scratch = [
            pltpu.VMEM((row_blocks, both_tokens, tile), BF16),
            pltpu.VMEM((col_blocks + 1, both_tokens, tile), F32),
        ]
        total_shape = jax.ShapeDtypeStruct((col_blocks, both_tokens, tile), F32)
        total = call(
            functools.partial(first_kernel, col_blocks=col_blocks),
            total_shape, scratch, (ids,), (activations, mate_activations, blocks),
        )
        all_ids = jnp.concatenate(far_ids)

        def bases(items, *more):
            starts = [(d - 1) * slots + ((part - e) % n_parts) * held + i * size for _, d, e, i in items]
            return jnp.stack(starts + list(more)).astype(jnp.int32)

        late = [item for item in arrivals if item[2] > 0 and item[1] == group - 1 and item[3] >= chunks - 2]
        late.insert(0, arrivals[(group - 1) * chunks - 1])
        late_keys = [item[1:] for item in late]
        early = [item for item in arrivals if item[1:] not in late_keys]
        total = call(
            functools.partial(more_kernel, col_blocks=col_blocks, count=len(early)),
            total_shape, scratch, (bases(early), all_ids),
            (activations, mate_activations, total) + tuple(item[0] for item in early),
        )
        piece = (chips, share, tokens, tile)
        send_mate, keep_mate, send_own, keep_own = call(
            functools.partial(last_kernel, col_blocks=col_blocks, count=len(late)),
            tuple(jax.ShapeDtypeStruct(piece, t) for t in (BF16, F32, BF16, F32)),
            scratch, (bases(late, core), all_ids),
            (activations, mate_activations, total) + tuple(item[0] for item in late),
        )

        def at(value, where):
            return lax.dynamic_index_in_dim(value, where % chips, 0, keepdims=False)

        core_mate = core_swap(send_mate)
        core_own = core_swap(send_own)

        def over_chips(keep, got):
            result = []
            for d in range(1, chips):
                sent = (at(keep, chip + d) + at(got, chip + d).astype(F32)).astype(BF16)
                result.append(chip_shift(sent, d))
            return result

        mate_total = at(keep_mate, chip) + at(core_mate, chip).astype(F32)
        for piece_got in over_chips(keep_mate, core_mate):
            mate_total += piece_got.astype(F32)
        own_pieces = over_chips(keep_own, core_own)
        from_mate = mate_swap(mate_total.astype(BF16))
        projected = call(
            final_kernel,
            jax.ShapeDtypeStruct((tokens, feats), BF16), [], (),
            (low_b, output_adapter, at(keep_own, chip), at(core_own, chip)) + tuple(own_pieces) + (from_mate,),
        )
        return projected, input_adapter_gradient, output_adapter_gradient

    return body


def solution(mesh):
    placed = (
        P(("parts", "dp"), "row"),
        P(("parts", "dp"), "row"),
        P(("parts", "dp")),
        P("row", "dp", None, None),
        P("row", "dp"),
        P("row", None),
        P(None, "row"),
    )
    return jax.shard_map(
        make_body(mesh.shape["parts"], mesh.shape["row"], mesh.shape["dp"]),
        mesh=mesh,
        in_specs=placed,
        out_specs=(P(("parts", "dp"), "row"), P(("parts", "row"), None), P("parts", "row")),
        check_vma=False,
    )
```

```python
import functools

import jax
import jax.numpy as jnp
from jax import lax
from jax.experimental import pallas as pl
from jax.experimental.pallas import tpu as pltpu
from jax.sharding import PartitionSpec as P

D = 8192

adapter_scale = 2.0

F32 = jnp.float32
BF16 = jnp.bfloat16


def add_blocks(total_ref, tiles_ref, blocks_ref, ids_ref, base, col_blocks, unroll):
    count = blocks_ref.shape[0]

    def one(step, carry):
        for u in range(unroll):
            k = step * unroll + u
            ident = ids_ref[base + k]
            known = jnp.maximum(ident, 0)
            row = lax.div(known, col_blocks)
            col = jnp.where(ident >= 0, lax.rem(known, col_blocks), col_blocks)
            total_ref[col] += jnp.dot(tiles_ref[row], blocks_ref[k], preferred_element_type=F32)
        return carry

    lax.fori_loop(0, count // unroll, one, 0)


def first_kernel(ids_ref, own_ref, mate_ref, blocks_ref, total_ref, tiles_ref, *, col_blocks):
    row_blocks, _, tile = tiles_ref.shape
    tokens = own_ref.shape[0]
    total_ref[...] = jnp.zeros_like(total_ref)
    for i in range(row_blocks):
        tiles_ref[i, :tokens, :] = own_ref[:, i * tile:(i + 1) * tile]
        tiles_ref[i, tokens:, :] = mate_ref[:, i * tile:(i + 1) * tile]
    add_blocks(total_ref, tiles_ref, blocks_ref, ids_ref, 0, col_blocks, 8)


def add_arrivals(where_ref, ids_ref, tiles_ref, blocks, total_ref, places, parts, held, col_blocks):
    for blocks_ref, (offset, shift, start) in zip(blocks, places):
        source = lax.rem(where_ref[0] + (parts - shift), parts)
        base = offset + source * held + start
        add_blocks(total_ref, tiles_ref, blocks_ref, ids_ref, base, col_blocks, 4)


def more_kernel(where_ref, ids_ref, tiles_ref, old_ref, *rest, **plan):
    add_arrivals(where_ref, ids_ref, tiles_ref, rest[:-1], rest[-1], **plan)


def last_kernel(where_ref, ids_ref, tiles_ref, old_ref, *rest, **plan):
    blocks, (total_ref, send_mate, send_own) = rest[:-3], rest[-3:]
    add_arrivals(where_ref, ids_ref, tiles_ref, blocks, total_ref, **plan)
    chips, share, tokens, _ = send_mate.shape
    for chip in range(chips):
        other = (2 * chip + 1 - where_ref[1]) * share
        for q in range(share):
            send_mate[chip, q] = total_ref[other + q, tokens:, :].astype(BF16)
            send_own[chip, q] = total_ref[other + q, :tokens, :].astype(BF16)


def chip_kernel(where_ref, total_ref, core_ref, leaving_ref, *, first):
    chips, share, tokens, _ = core_ref.shape
    for d in range(1, chips):
        to_chip = lax.rem(where_ref[2] + d, chips)
        mine = (2 * to_chip + where_ref[1]) * share
        for q in range(share):
            value = total_ref[mine + q, first:first + tokens, :] + core_ref[to_chip, q].astype(F32)
            leaving_ref[d - 1, q] = value.astype(BF16)


def mate_kernel(where_ref, total_ref, core_ref, *rest):
    pieces, out_ref = rest[:-1], rest[-1]
    _, share, tokens, _ = core_ref.shape
    chip = where_ref[2]
    mine = (2 * chip + where_ref[1]) * share
    for q in range(share):
        value = total_ref[mine + q, tokens:, :] + core_ref[chip, q].astype(F32)
        for piece in pieces:
            value += piece[q].astype(F32)
        out_ref[q] = value.astype(BF16)


def final_kernel(where_ref, low_ref, adapter_ref, total_ref, core_ref, *rest):
    pieces, out_ref = rest[:-1], rest[-1]
    _, share, tokens, tile = core_ref.shape
    chip = where_ref[2]
    mine = (2 * chip + where_ref[1]) * share
    for q in range(share):
        value = total_ref[mine + q, :tokens, :] + core_ref[chip, q].astype(F32)
        for piece in pieces:
            value += piece[q].astype(F32)
        cols = slice(q * tile, (q + 1) * tile)
        extra = jnp.dot(low_ref[...], adapter_ref[:, cols], preferred_element_type=F32)
        out_ref[:, cols] = (value + adapter_scale * extra).astype(BF16)


def call(kernel, outs, scalars, arrays, flops, aliases=None):
    smem = pl.BlockSpec(memory_space=pltpu.SMEM)
    vmem = pl.BlockSpec(memory_space=pltpu.VMEM)
    return pl.pallas_call(
        kernel,
        out_shape=outs,
        in_specs=[smem] * len(scalars) + [vmem] * len(arrays),
        out_specs=tuple(vmem for _ in outs),
        input_output_aliases=aliases or {},
        cost_estimate=pl.CostEstimate(flops=flops, transcendentals=0, bytes_accessed=1 << 20),
        compiler_params=pltpu.CompilerParams(vmem_limit_bytes=4 * 1024 * 1024),
    )(*scalars, *arrays)


def on_chip(value):
    return pltpu.with_memory_space_constraint(value, pltpu.VMEM)


def after(value, *needed):
    return lax.optimization_barrier((value,) + needed)[0]


def make_body(n_parts, n_row, n_dp):
    chips = n_row // 2
    group = n_dp // 2

    def core_swap(value):
        return lax.ppermute(value, "row", [(i, i ^ 1) for i in range(n_row)])

    def chip_shift(value, d):
        pairs = [(2 * a + c, 2 * ((a + d) % chips) + c) for a in range(chips) for c in range(2)]
        return lax.ppermute(value, "row", pairs)

    def mate_swap(value):
        return lax.ppermute(value, "dp", [(i, i ^ 1) for i in range(n_dp)])

    def group_shift(value, d):
        pairs = [(2 * a + h, 2 * ((a + d) % group) + h) for a in range(group) for h in range(2)]
        return lax.ppermute(value, "dp", pairs)

    def part_shift(value, d):
        return lax.ppermute(value, "parts", [(i, (i + d) % n_parts) for i in range(n_parts)])

    def in_order_sum(own, received, place, count):
        if count == 2:
            return own.astype(F32) + received[0].astype(F32)
        stack = jnp.zeros((count,) + own.shape, own.dtype)
        stack = lax.dynamic_update_index_in_dim(stack, own, place, 0)
        for d, value in enumerate(received, 1):
            stack = lax.dynamic_update_index_in_dim(stack, value, lax.rem(place + (count - d), count), 0)
        return stack.astype(F32).sum(axis=0)

    def body(activations, cotangent, forget_labels, kept_blocks, block_ids, adapter_a, output_adapter):
        tokens, shard_rows = activations.shape
        rank = adapter_a.shape[1]
        feats = cotangent.shape[1]
        slots, tile = kept_blocks.shape[1], kept_blocks.shape[-1]
        row_blocks = shard_rows // tile
        col_blocks = D // tile
        share = col_blocks // n_row
        part = lax.axis_index("parts")
        row_index = lax.axis_index("row")
        dp_index = lax.axis_index("dp")
        core, chip = lax.rem(row_index, 2), lax.div(row_index, 2)
        half_bit, place = lax.rem(dp_index, 2), lax.div(dp_index, 2)
        where = jnp.stack([part, core, chip]).astype(jnp.int32)
        blocks = kept_blocks[0]
        ids = block_ids[0]

        far_ids = [group_shift(ids, d) for d in range(1, group)]
        mate_activations = mate_swap(activations)
        held = slots // n_parts
        sizes = [held * k // 32 for k in (12, 12, 8)]
        starts = [sum(sizes[:k]) for k in range(len(sizes))]
        own_share = lax.dynamic_slice_in_dim(blocks, part * held, held, axis=0)
        all_ids = far_ids[0] if group == 2 else jnp.concatenate(far_ids)
        direct = []
        for d in range(1, group):
            for start, size in zip(starts, sizes):
                leaving = own_share[start:start + size]
                if start > 0:
                    leaving = after(leaving, all_ids)
                direct.append((group_shift(leaving, d), ((d - 1) * slots, 0, start)))

        adapter_early = after(adapter_a, all_ids)
        signs = (1 - 2 * forget_labels).astype(F32)[:, None]
        low_part = jnp.dot(activations, adapter_early, preferred_element_type=F32)
        back_part = signs * lax.dot_general(
            cotangent, after(output_adapter, all_ids), (((1,), (1,)), ((), ())), preferred_element_type=F32
        )
        both = jnp.concatenate([low_part, back_part], axis=1)
        both = both + core_swap(both)
        both = in_order_sum(both, [chip_shift(both, d) for d in range(1, chips)], chip, chips).astype(BF16)
        low_b, back_b = both[:, :rank], both[:, rank:]
        contract_tokens = (((0,), (0,)), ((), ()))
        out_grad = adapter_scale * lax.dot_general(
            low_b * signs.astype(BF16), cotangent, contract_tokens, preferred_element_type=F32
        )
        in_half, out_half = shard_rows // 2, feats // 2
        out_mine = lax.dynamic_slice_in_dim(out_grad, half_bit * out_half, out_half, axis=1)
        out_other = lax.dynamic_slice_in_dim(out_grad, (1 - half_bit) * out_half, out_half, axis=1)
        mate_pack = mate_swap(jnp.concatenate([out_other, back_b.astype(F32).T], axis=1))

        both_tokens = 2 * tokens
        per_block = 2 * both_tokens * tile * tile
        total_shape = pltpu.VMEM((col_blocks + 1, both_tokens, tile), F32)
        total, tiles = call(
            functools.partial(first_kernel, col_blocks=col_blocks),
            (total_shape, pltpu.VMEM((row_blocks, both_tokens, tile), BF16)),
            (ids,), (activations, mate_activations, blocks), slots * per_block,
        )
        swapped = []
        for k, (value, (offset, _, start)) in enumerate(direct):
            if k == len(direct) - 1:
                value = after(value, total)
            for e in range(1, n_parts):
                swapped.append((part_shift(value, e), (offset, e, start)))

        gate = direct[-2][0]
        mate_pack = after(mate_pack, gate)
        mate_out, mate_back_b = mate_pack[:, :out_half], mate_pack[:, out_half:].astype(BF16)
        in_grad = adapter_scale * (
            lax.dot_general(back_b, activations, contract_tokens, preferred_element_type=F32)
            + jnp.dot(mate_back_b, mate_activations, preferred_element_type=F32)
        )
        in_mine = lax.dynamic_slice_in_dim(in_grad, half_bit * in_half, in_half, axis=1)
        grads = jnp.concatenate([in_mine, out_mine + mate_out], axis=1).astype(BF16)
        grads = after(grads, direct[-1][0])
        far_grads = [group_shift(grads, d) for d in range(1, group)]

        late = [direct[-1]] + swapped[-2 * (n_parts - 1):]
        early = direct[:-1] + swapped[:-2 * (n_parts - 1)]

        def plan(items):
            return dict(places=[item[1] for item in items], parts=n_parts, held=held, col_blocks=col_blocks)

        def work(items):
            return sum(item[0].shape[0] for item in items) * per_block

        (total,) = call(
            functools.partial(more_kernel, **plan(early)), (total_shape,), (where, all_ids),
            (on_chip(tiles), on_chip(total)) + tuple(item[0] for item in early), work(early), {3: 0},
        )
        send = pltpu.VMEM((chips, share, tokens, tile), BF16)
        total, send_mate, send_own = call(
            functools.partial(last_kernel, **plan(late)), (total_shape, send, send), (where, all_ids),
            (on_chip(tiles), on_chip(total)) + tuple(item[0] for item in late), work(late), {3: 0},
        )

        def for_chips(first, core_got, *needed):
            (leaving,) = call(
                functools.partial(chip_kernel, first=first),
                (pltpu.VMEM((chips - 1, share, tokens, tile), BF16),), (where,), (on_chip(total), core_got), 0,
            )
            if needed:
                leaving = after(leaving, *needed)
            return leaving, [chip_shift(leaving[d - 1], d) for d in range(1, chips)]

        core_mate = core_swap(send_mate)
        core_own = core_swap(send_own)
        leaving, mate_pieces = for_chips(tokens, core_mate)
        far_grads = [after(value, leaving) for value in far_grads]
        grads = in_order_sum(grads, far_grads, place, group)
        mate_grads = mate_swap(grads)
        (mate_total,) = call(
            mate_kernel, (pltpu.VMEM((share, tokens, tile), BF16),), (where,),
            (on_chip(total), core_mate) + tuple(mate_pieces), 0,
        )
        from_mate = mate_swap(mate_total)
        _, own_pieces = for_chips(0, core_own, mate_total)
        mate_grads = after(mate_grads, mate_total)
        low_side = jnp.where(half_bit == 0, grads, mate_grads)
        high_side = jnp.where(half_bit == 0, mate_grads, grads)
        input_adapter_gradient = jnp.concatenate([low_side[:, :in_half], high_side[:, :in_half]], axis=1).T
        output_adapter_gradient = jnp.concatenate([low_side[:, in_half:], high_side[:, in_half:]], axis=1)
        (projected,) = call(
            final_kernel, (jax.ShapeDtypeStruct((tokens, feats), BF16),), (where,),
            (low_b, output_adapter, on_chip(total), core_own) + tuple(own_pieces) + (from_mate,),
            2 * tokens * rank * feats,
        )
        return projected, input_adapter_gradient, output_adapter_gradient

    return body


def solution(mesh):
    placed = (
        P(("parts", "dp"), "row"),
        P(("parts", "dp"), "row"),
        P(("parts", "dp")),
        P("row", "dp", None, None),
        P("row", "dp"),
        P("row", None),
        P(None, "row"),
    )
    return jax.shard_map(
        make_body(mesh.shape["parts"], mesh.shape["row"], mesh.shape["dp"]),
        mesh=mesh,
        in_specs=placed,
        out_specs=(P(("parts", "dp"), "row"), P(("parts", "row"), None), P("parts", "row")),
        check_vma=False,
    )
```

```python
import functools

import jax
import jax.numpy as jnp
from jax import lax
from jax.experimental import pallas as pl
from jax.experimental.pallas import tpu as pltpu
from jax.sharding import PartitionSpec as P

D = 8192

adapter_scale = 2.0

F32 = jnp.float32
BF16 = jnp.bfloat16


def add_blocks(total_ref, tiles_ref, blocks_ref, ids_ref, base, col_blocks, unroll):
    count = blocks_ref.shape[0]

    def one(step, carry):
        for u in range(unroll):
            k = step * unroll + u
            ident = ids_ref[base + k]
            known = jnp.maximum(ident, 0)
            row = lax.div(known, col_blocks)
            col = jnp.where(ident >= 0, lax.rem(known, col_blocks), col_blocks)
            total_ref[col] += jnp.dot(tiles_ref[row], blocks_ref[k], preferred_element_type=F32)
        return carry

    lax.fori_loop(0, count // unroll, one, 0)


def first_kernel(ids_ref, own_ref, mate_ref, blocks_ref, total_ref, tiles_ref, *, col_blocks):
    row_blocks, _, tile = tiles_ref.shape
    tokens = own_ref.shape[0]
    total_ref[...] = jnp.zeros_like(total_ref)
    for i in range(row_blocks):
        tiles_ref[i, :tokens, :] = own_ref[:, i * tile:(i + 1) * tile]
        tiles_ref[i, tokens:, :] = mate_ref[:, i * tile:(i + 1) * tile]
    add_blocks(total_ref, tiles_ref, blocks_ref, ids_ref, 0, col_blocks, 8)


def add_arrivals(where_ref, ids_ref, tiles_ref, blocks, total_ref, places, parts, held, col_blocks):
    for blocks_ref, (offset, shift, start) in zip(blocks, places):
        source = lax.rem(where_ref[0] + (parts - shift), parts)
        base = offset + source * held + start
        add_blocks(total_ref, tiles_ref, blocks_ref, ids_ref, base, col_blocks, 4)


def more_kernel(where_ref, ids_ref, tiles_ref, old_ref, *rest, **plan):
    add_arrivals(where_ref, ids_ref, tiles_ref, rest[:-1], rest[-1], **plan)


def last_kernel(where_ref, ids_ref, tiles_ref, old_ref, *rest, **plan):
    blocks, (total_ref, send_mate, send_own) = rest[:-3], rest[-3:]
    add_arrivals(where_ref, ids_ref, tiles_ref, blocks, total_ref, **plan)
    chips, share, tokens, _ = send_mate.shape
    for chip in range(chips):
        other = (2 * chip + 1 - where_ref[1]) * share
        for q in range(share):
            send_mate[chip, q] = total_ref[other + q, tokens:, :].astype(BF16)
            send_own[chip, q] = total_ref[other + q, :tokens, :].astype(BF16)


def chip_kernel(where_ref, total_ref, core_ref, leaving_ref, *, first):
    chips, share, tokens, _ = core_ref.shape
    for d in range(1, chips):
        to_chip = lax.rem(where_ref[2] + d, chips)
        mine = (2 * to_chip + where_ref[1]) * share
        for q in range(share):
            value = total_ref[mine + q, first:first + tokens, :] + core_ref[to_chip, q].astype(F32)
            leaving_ref[d - 1, q] = value.astype(BF16)


def mate_kernel(where_ref, total_ref, core_ref, *rest):
    pieces, out_ref = rest[:-1], rest[-1]
    _, share, tokens, _ = core_ref.shape
    chip = where_ref[2]
    mine = (2 * chip + where_ref[1]) * share
    for q in range(share):
        value = total_ref[mine + q, tokens:, :] + core_ref[chip, q].astype(F32)
        for piece in pieces:
            value += piece[q].astype(F32)
        out_ref[q] = value.astype(BF16)


def ordered_sum(own, received, place):
    count = len(received) + 1
    if count == 1:
        return own
    if count == 2:
        return own + received[0]
    total = None
    for member in range(count):
        value = own
        for d, other in enumerate(received, 1):
            value = jnp.where(lax.rem(place + (count - d), count) == member, other, value)
        total = value if total is None else total + value
    return total


CONTRACT_LAST = (((1,), (1,)), ((), ()))


def low_rank_kernel(acts_ref, adapter_a_ref, cot_ref, adapter_ref, labels_ref, out_ref):
    rank = adapter_a_ref.shape[0]
    signs = (1 - 2 * labels_ref[...]).astype(F32)
    out_ref[:rank, :] = lax.dot_general(adapter_a_ref[...], acts_ref[...], CONTRACT_LAST, preferred_element_type=F32)
    out_ref[rank:, :] = signs * lax.dot_general(
        adapter_ref[...], cot_ref[...], CONTRACT_LAST, preferred_element_type=F32
    )


def own_grad_kernel(where_ref, cot_ref, labels_ref, both_ref, *rest):
    received, (rounded_ref, pack_ref) = rest[:-2], rest[-2:]
    feats = cot_ref.shape[1]
    rounded = ordered_sum(both_ref[...], [ref[...] for ref in received], where_ref[2]).astype(BF16)
    rounded_ref[...] = rounded
    rank = rounded.shape[0] // 2
    signs = (1 - 2 * labels_ref[...]).astype(F32)
    signed_low = (rounded[:rank].astype(F32) * signs).astype(BF16)
    grad = jnp.dot(signed_low, cot_ref[...], preferred_element_type=F32)
    pack_ref[:, :feats] = (adapter_scale * grad).astype(BF16)
    pack_ref[:, feats:] = rounded[rank:]


def pair_grad_kernel(rounded_ref, acts_ref, mate_acts_ref, pack_ref, mate_pack_ref, out_ref):
    rank, shard_rows = rounded_ref.shape[0] // 2, acts_ref.shape[1]
    feats = pack_ref.shape[1] - rounded_ref.shape[1]
    own = jnp.dot(rounded_ref[rank:, :], acts_ref[...], preferred_element_type=F32)
    mate = jnp.dot(mate_pack_ref[:, feats:], mate_acts_ref[...], preferred_element_type=F32)
    out_ref[:, :shard_rows] = (adapter_scale * (own + mate)).astype(BF16)
    out_ref[:, shard_rows:] = (
        pack_ref[:, :feats].astype(F32) + mate_pack_ref[:, :feats].astype(F32)
    ).astype(BF16)


def grad_sum_kernel(where_ref, own_ref, *rest):
    received, (in_ref, out_ref) = rest[:-2], rest[-2:]
    shard_rows = in_ref.shape[1]
    own, place = own_ref[...].astype(F32), where_ref[3]
    total = ordered_sum(own, [ref[...].astype(F32) for ref in received], place)
    in_ref[...] = total[:, :shard_rows]
    out_ref[...] = total[:, shard_rows:]


def final_kernel(where_ref, rounded_ref, adapter_ref, total_ref, core_ref, *rest):
    pieces, out_ref = rest[:-1], rest[-1]
    _, share, tokens, tile = core_ref.shape
    rank = rounded_ref.shape[0] // 2
    low = rounded_ref[:rank, :].astype(F32).T.astype(BF16)
    chip = where_ref[2]
    mine = (2 * chip + where_ref[1]) * share
    for q in range(share):
        value = total_ref[mine + q, :tokens, :] + core_ref[chip, q].astype(F32)
        for piece in pieces:
            value += piece[q].astype(F32)
        cols = slice(q * tile, (q + 1) * tile)
        extra = jnp.dot(low, adapter_ref[:, cols], preferred_element_type=F32)
        out_ref[:, cols] = (value + adapter_scale * extra).astype(BF16)


def call(kernel, outs, scalars, arrays, flops, aliases=None):
    smem = pl.BlockSpec(memory_space=pltpu.SMEM)
    vmem = pl.BlockSpec(memory_space=pltpu.VMEM)
    return pl.pallas_call(
        kernel,
        out_shape=outs,
        in_specs=[smem] * len(scalars) + [vmem] * len(arrays),
        out_specs=tuple(vmem for _ in outs),
        input_output_aliases=aliases or {},
        cost_estimate=pl.CostEstimate(flops=flops, transcendentals=0, bytes_accessed=1 << 20),
        compiler_params=pltpu.CompilerParams(vmem_limit_bytes=4 * 1024 * 1024),
    )(*scalars, *arrays)


def on_chip(value):
    return pltpu.with_memory_space_constraint(value, pltpu.VMEM)


def after(value, *needed):
    return lax.optimization_barrier((value,) + needed)[0]


def make_body(n_parts, n_row, n_dp):
    chips = n_row // 2
    group = n_dp // 2

    def core_swap(value):
        return lax.ppermute(value, "row", [(i, i ^ 1) for i in range(n_row)])

    def chip_shift(value, d):
        pairs = [(2 * a + c, 2 * ((a + d) % chips) + c) for a in range(chips) for c in range(2)]
        return lax.ppermute(value, "row", pairs)

    def mate_swap(value):
        return lax.ppermute(value, "dp", [(i, i ^ 1) for i in range(n_dp)])

    def group_shift(value, d):
        pairs = [(2 * a + h, 2 * ((a + d) % group) + h) for a in range(group) for h in range(2)]
        return lax.ppermute(value, "dp", pairs)

    def part_shift(value, d):
        return lax.ppermute(value, "parts", [(i, (i + d) % n_parts) for i in range(n_parts)])

    def body(activations, cotangent, forget_labels, kept_blocks, block_ids, adapter_a, output_adapter):
        tokens, shard_rows = activations.shape
        rank = adapter_a.shape[1]
        feats = cotangent.shape[1]
        slots, tile = kept_blocks.shape[1], kept_blocks.shape[-1]
        row_blocks = shard_rows // tile
        col_blocks = D // tile
        share = col_blocks // n_row
        part = lax.axis_index("parts")
        row_index = lax.axis_index("row")
        dp_index = lax.axis_index("dp")
        where = jnp.stack(
            [part, lax.rem(row_index, 2), lax.div(row_index, 2), lax.div(dp_index, 2)]
        ).astype(jnp.int32)
        blocks = kept_blocks[0]
        ids = block_ids[0]
        labels = forget_labels[None, :]

        far_ids = [group_shift(ids, d) for d in range(1, group)]
        all_ids = far_ids[0] if group == 2 else jnp.concatenate(far_ids)
        held = slots // n_parts
        sizes = [held * k // 32 for k in (12, 12, 8)]
        starts = [sum(sizes[:k]) for k in range(len(sizes))]
        own_share = lax.dynamic_slice_in_dim(blocks, part * held, held, axis=0)
        shares = [own_share[start:start + size] for start, size in zip(starts, sizes)]
        direct = []
        for d in range(1, group):
            for leaving, start in zip(shares, starts):
                if start > 0:
                    leaving = after(leaving, all_ids)
                direct.append((group_shift(leaving, d), ((d - 1) * slots, 0, start)))
        mate_activations = mate_swap(activations)

        adapter_early = after(adapter_a, all_ids, *shares)
        (both,) = call(
            low_rank_kernel, (jax.ShapeDtypeStruct((2 * rank, tokens), F32),), (),
            (activations, adapter_early.T, cotangent, output_adapter, labels), 4 * tokens * rank * shard_rows,
        )
        both = both + core_swap(both)
        rounded, pack = call(
            own_grad_kernel,
            (
                jax.ShapeDtypeStruct((2 * rank, tokens), BF16),
                jax.ShapeDtypeStruct((rank, feats + tokens), BF16),
            ),
            (where,), (cotangent, labels, both) + tuple(chip_shift(both, d) for d in range(1, chips)),
            2 * tokens * rank * feats,
        )
        mate_pack = mate_swap(pack)

        both_tokens = 2 * tokens
        per_block = 2 * both_tokens * tile * tile
        total_shape = pltpu.VMEM((col_blocks + 1, both_tokens, tile), F32)
        total, tiles = call(
            functools.partial(first_kernel, col_blocks=col_blocks),
            (total_shape, pltpu.VMEM((row_blocks, both_tokens, tile), BF16)),
            (ids,), (activations, mate_activations, blocks), slots * per_block,
        )
        swapped = []
        for k, (value, (offset, _, start)) in enumerate(direct):
            if k == len(direct) - 2:
                value = after(value, total)
            for e in range(1, n_parts):
                swapped.append((part_shift(value, e), (offset, e, start)))

        (grads,) = call(
            pair_grad_kernel, (jax.ShapeDtypeStruct((rank, shard_rows + feats), BF16),), (),
            (rounded, activations, mate_activations, pack, after(mate_pack, direct[-2][0])),
            4 * tokens * rank * shard_rows,
        )
        grads = after(grads, direct[-1][0])
        far_grads = [group_shift(grads, d) for d in range(1, group)]

        late = swapped[1 - n_parts:]
        early = direct + swapped[:1 - n_parts]

        def plan(items):
            return dict(places=[item[1] for item in items], parts=n_parts, held=held, col_blocks=col_blocks)

        def work(items):
            return sum(item[0].shape[0] for item in items) * per_block

        (total,) = call(
            functools.partial(more_kernel, **plan(early)), (total_shape,), (where, all_ids),
            (on_chip(tiles), on_chip(total)) + tuple(item[0] for item in early), work(early), {3: 0},
        )
        send = pltpu.VMEM((chips, share, tokens, tile), BF16)
        total, send_mate, send_own = call(
            functools.partial(last_kernel, **plan(late)), (total_shape, send, send),
            (after(where, grads), all_ids),
            (on_chip(tiles), on_chip(total)) + tuple(item[0] for item in late), work(late), {3: 0},
        )

        def for_chips(first, core_got, *needed):
            (leaving,) = call(
                functools.partial(chip_kernel, first=first),
                (pltpu.VMEM((chips - 1, share, tokens, tile), BF16),), (where,), (on_chip(total), core_got), 0,
            )
            if needed:
                leaving = after(leaving, *needed)
            return [chip_shift(leaving[d - 1], d) for d in range(1, chips)]

        core_mate = core_swap(send_mate)
        core_own = core_swap(send_own)
        mate_pieces = for_chips(tokens, core_mate)
        (mate_total,) = call(
            mate_kernel, (pltpu.VMEM((share, tokens, tile), BF16),), (where,),
            (on_chip(total), core_mate) + tuple(mate_pieces), 0,
        )
        from_mate = mate_swap(mate_total)
        own_pieces = for_chips(0, core_own, mate_total)
        far_grads = [after(value, mate_total) for value in far_grads]
        in_grad, out_grad = call(
            grad_sum_kernel,
            (jax.ShapeDtypeStruct((rank, shard_rows), F32), jax.ShapeDtypeStruct((rank, feats), F32)),
            (where,), (grads,) + tuple(far_grads), 0,
        )
        (projected,) = call(
            final_kernel, (jax.ShapeDtypeStruct((tokens, feats), BF16),), (where,),
            (rounded, output_adapter, on_chip(total), core_own) + tuple(own_pieces) + (from_mate,),
            2 * tokens * rank * feats,
        )
        return projected, in_grad.T, out_grad

    return body


def solution(mesh):
    placed = (
        P(("parts", "dp"), "row"),
        P(("parts", "dp"), "row"),
        P(("parts", "dp")),
        P("row", "dp", None, None),
        P("row", "dp"),
        P("row", None),
        P(None, "row"),
    )
    return jax.shard_map(
        make_body(mesh.shape["parts"], mesh.shape["row"], mesh.shape["dp"]),
        mesh=mesh,
        in_specs=placed,
        out_specs=(P(("parts", "dp"), "row"), P(("parts", "row"), None), P("parts", "row")),
        check_vma=False,
    )
```

```python
import functools

import jax
import jax.numpy as jnp
from jax import lax
from jax.experimental import pallas as pl
from jax.experimental.pallas import tpu as pltpu
from jax.sharding import PartitionSpec as P

D = 8192

adapter_scale = 2.0

F32 = jnp.float32
BF16 = jnp.bfloat16


def add_blocks(total_ref, tiles_ref, blocks_ref, ids_ref, base, col_blocks, unroll):
    count = blocks_ref.shape[0]

    def one(step, carry):
        for u in range(unroll):
            k = step * unroll + u
            ident = ids_ref[base + k]
            known = jnp.maximum(ident, 0)
            row = lax.div(known, col_blocks)
            col = jnp.where(ident >= 0, lax.rem(known, col_blocks), col_blocks)
            total_ref[col] += jnp.dot(tiles_ref[row], blocks_ref[k], preferred_element_type=F32)
        return carry

    lax.fori_loop(0, count // unroll, one, 0)


def add_arrivals(where_ref, ids_ref, tiles_ref, blocks, total_ref, places, parts, held, col_blocks):
    for blocks_ref, (offset, shift, start) in zip(blocks, places):
        source = lax.rem(where_ref[0] + (parts - shift), parts)
        base = offset + source * held + start
        add_blocks(total_ref, tiles_ref, blocks_ref, ids_ref, base, col_blocks, 2)


def first_kernel(where_ref, own_ids_ref, ids_ref, own_ref, mate_ref, own_blocks_ref, *rest, **plan):
    blocks, (total_ref, tiles_ref) = rest[:-2], rest[-2:]
    row_blocks, _, tile = tiles_ref.shape
    tokens = own_ref.shape[0]
    total_ref[...] = jnp.zeros_like(total_ref)
    for i in range(row_blocks):
        tiles_ref[i, :tokens, :] = own_ref[:, i * tile:(i + 1) * tile]
        tiles_ref[i, tokens:, :] = mate_ref[:, i * tile:(i + 1) * tile]
    add_blocks(total_ref, tiles_ref, own_blocks_ref, own_ids_ref, 0, plan["col_blocks"], 8)
    add_arrivals(where_ref, ids_ref, tiles_ref, blocks, total_ref, **plan)


def more_kernel(where_ref, ids_ref, tiles_ref, old_ref, *rest, **plan):
    add_arrivals(where_ref, ids_ref, tiles_ref, rest[:-1], rest[-1], **plan)


def last_kernel(where_ref, ids_ref, tiles_ref, old_ref, *rest, **plan):
    blocks, (total_ref, send_mate, send_own) = rest[:-3], rest[-3:]
    add_arrivals(where_ref, ids_ref, tiles_ref, blocks, total_ref, **plan)
    chips, share, tokens, _ = send_mate.shape
    for chip in range(chips):
        other = (2 * chip + 1 - where_ref[1]) * share
        for q in range(share):
            send_mate[chip, q] = total_ref[other + q, tokens:, :].astype(BF16)
            send_own[chip, q] = total_ref[other + q, :tokens, :].astype(BF16)


def chip_kernel(where_ref, total_ref, core_ref, leaving_ref, *, first):
    chips, share, tokens, _ = core_ref.shape
    for d in range(1, chips):
        to_chip = lax.rem(where_ref[2] + d, chips)
        mine = (2 * to_chip + where_ref[1]) * share
        for q in range(share):
            value = total_ref[mine + q, first:first + tokens, :] + core_ref[to_chip, q].astype(F32)
            leaving_ref[d - 1, q] = value.astype(BF16)


def mate_kernel(where_ref, total_ref, core_ref, *rest):
    pieces, out_ref = rest[:-1], rest[-1]
    _, share, tokens, _ = core_ref.shape
    chip = where_ref[2]
    mine = (2 * chip + where_ref[1]) * share
    for q in range(share):
        value = total_ref[mine + q, tokens:, :] + core_ref[chip, q].astype(F32)
        for piece in pieces:
            value += piece[q].astype(F32)
        out_ref[q] = value.astype(BF16)


def ordered_sum(own, received, place):
    count = len(received) + 1
    if count == 1:
        return own
    if count == 2:
        return own + received[0]
    total = None
    for member in range(count):
        value = own
        for d, other in enumerate(received, 1):
            value = jnp.where(lax.rem(place + (count - d), count) == member, other, value)
        total = value if total is None else total + value
    return total


CONTRACT_LAST = (((1,), (1,)), ((), ()))


def low_rank_kernel(acts_ref, adapter_a_ref, cot_ref, adapter_ref, labels_ref, out_ref):
    rank = adapter_a_ref.shape[0]
    signs = (1 - 2 * labels_ref[...]).astype(F32)
    out_ref[:rank, :] = lax.dot_general(adapter_a_ref[...], acts_ref[...], CONTRACT_LAST, preferred_element_type=F32)
    out_ref[rank:, :] = signs * lax.dot_general(
        adapter_ref[...], cot_ref[...], CONTRACT_LAST, preferred_element_type=F32
    )


def own_grad_kernel(where_ref, cot_ref, labels_ref, both_ref, *rest):
    received, (rounded_ref, pack_ref) = rest[:-2], rest[-2:]
    feats = cot_ref.shape[1]
    rounded = ordered_sum(both_ref[...], [ref[...] for ref in received], where_ref[2]).astype(BF16)
    rounded_ref[...] = rounded
    rank = rounded.shape[0] // 2
    signs = (1 - 2 * labels_ref[...]).astype(F32)
    signed_low = (rounded[:rank].astype(F32) * signs).astype(BF16)
    grad = jnp.dot(signed_low, cot_ref[...], preferred_element_type=F32)
    pack_ref[:, :feats] = (adapter_scale * grad).astype(BF16)
    pack_ref[:, feats:] = rounded[rank:]


def pair_grad_kernel(where_ref, rounded_ref, acts_ref, mate_acts_ref, pack_ref, mate_pack_ref, half_ref):
    rank, shard_rows = rounded_ref.shape[0] // 2, acts_ref.shape[1]
    feats = pack_ref.shape[1] - rounded_ref.shape[1]
    in_half, out_half = shard_rows // 2, feats // 2
    back, mate_back = rounded_ref[rank:, :], mate_pack_ref[:, feats:]
    for bit in range(2):
        @pl.when(where_ref[3] == bit)
        def _():
            cols = slice(bit * in_half, (bit + 1) * in_half)
            grad = jnp.dot(back, acts_ref[:, cols], preferred_element_type=F32)
            grad += jnp.dot(mate_back, mate_acts_ref[:, cols], preferred_element_type=F32)
            half_ref[:, :in_half] = (adapter_scale * grad).astype(BF16)
            cols = slice(bit * out_half, (bit + 1) * out_half)
            grad = pack_ref[:, cols].astype(F32) + mate_pack_ref[:, cols].astype(F32)
            half_ref[:, in_half:] = grad.astype(BF16)


def grad_sum_kernel(halves_ref, in_ref, out_ref):
    in_half, out_half = in_ref.shape[1] // 2, out_ref.shape[1] // 2
    for bit in range(2):
        total = halves_ref[bit].astype(F32)
        for member in range(2 + bit, halves_ref.shape[0], 2):
            total += halves_ref[member].astype(F32)
        in_ref[:, bit * in_half:(bit + 1) * in_half] = total[:, :in_half]
        out_ref[:, bit * out_half:(bit + 1) * out_half] = total[:, in_half:]


def final_kernel(where_ref, rounded_ref, adapter_ref, total_ref, core_ref, *rest):
    pieces, out_ref = rest[:-1], rest[-1]
    _, share, tokens, tile = core_ref.shape
    rank = rounded_ref.shape[0] // 2
    low = rounded_ref[:rank, :].astype(F32).T.astype(BF16)
    chip = where_ref[2]
    mine = (2 * chip + where_ref[1]) * share
    for q in range(share):
        value = total_ref[mine + q, :tokens, :] + core_ref[chip, q].astype(F32)
        for piece in pieces:
            value += piece[q].astype(F32)
        cols = slice(q * tile, (q + 1) * tile)
        extra = jnp.dot(low, adapter_ref[:, cols], preferred_element_type=F32)
        out_ref[:, cols] = (value + adapter_scale * extra).astype(BF16)


def call(kernel, outs, scalars, arrays, aliases=None):
    smem = pl.BlockSpec(memory_space=pltpu.SMEM)
    vmem = pl.BlockSpec(memory_space=pltpu.VMEM)
    return pl.pallas_call(
        kernel,
        out_shape=outs,
        in_specs=[smem] * len(scalars) + [vmem] * len(arrays),
        out_specs=tuple(vmem for _ in outs),
        input_output_aliases=aliases or {},
        cost_estimate=pl.CostEstimate(flops=0, transcendentals=0, bytes_accessed=0),
        compiler_params=pltpu.CompilerParams(vmem_limit_bytes=4 * 1024 * 1024),
    )(*scalars, *arrays)


def on_chip(value):
    return pltpu.with_memory_space_constraint(value, pltpu.VMEM)


def after(value, *needed):
    return lax.optimization_barrier((value,) + needed)[0]


def make_body(n_parts, n_row, n_dp):
    chips = n_row // 2
    group = n_dp // 2

    def core_swap(value):
        return lax.ppermute(value, "row", [(i, i ^ 1) for i in range(n_row)])

    def chip_shift(value, d):
        pairs = [(2 * a + c, 2 * ((a + d) % chips) + c) for a in range(chips) for c in range(2)]
        return lax.ppermute(value, "row", pairs)

    def mate_swap(value):
        return lax.ppermute(value, "dp", [(i, i ^ 1) for i in range(n_dp)])

    def group_shift(value, d):
        pairs = [(2 * a + h, 2 * ((a + d) % group) + h) for a in range(group) for h in range(2)]
        return lax.ppermute(value, "dp", pairs)

    def part_shift(value, d):
        return lax.ppermute(value, "parts", [(i, (i + d) % n_parts) for i in range(n_parts)])

    def body(activations, cotangent, forget_labels, kept_blocks, block_ids, adapter_a, output_adapter):
        tokens, shard_rows = activations.shape
        rank = adapter_a.shape[1]
        feats = cotangent.shape[1]
        slots, tile = kept_blocks.shape[1], kept_blocks.shape[-1]
        row_blocks = shard_rows // tile
        col_blocks = D // tile
        share = col_blocks // n_row
        part = lax.axis_index("parts")
        row_index = lax.axis_index("row")
        dp_index = lax.axis_index("dp")
        where = jnp.stack(
            [part, lax.rem(row_index, 2), lax.div(row_index, 2), lax.rem(dp_index, 2)]
        ).astype(jnp.int32)
        blocks = kept_blocks[0]
        ids = block_ids[0]
        labels = forget_labels[None, :]

        soon = core_swap(ids)
        far_ids = [group_shift(ids, d) for d in range(1, group)]
        all_ids = far_ids[0] if group == 2 else jnp.concatenate(far_ids)
        held = slots // n_parts
        sizes = [held * k // 32 for k in (14, 10, 8)]
        starts = [sum(sizes[:k]) for k in range(len(sizes))]

        def leaving_chunk(k):
            chunk = lax.dynamic_slice_in_dim(blocks, part * held + starts[k], sizes[k], axis=0)
            return chunk if k == 0 else after(chunk, soon)

        direct = [
            (group_shift(leaving_chunk(k), d), ((d - 1) * slots, 0, starts[k]))
            for d in range(1, group) for k in range(len(starts))
        ]
        mate_activations = mate_swap(after(activations, soon))

        (both,) = call(
            low_rank_kernel, (jax.ShapeDtypeStruct((2 * rank, tokens), F32),), (),
            (activations, after(adapter_a, direct[0][0]).T, cotangent, output_adapter, labels),
        )
        both = both + core_swap(both)
        both_later = after(both, direct[1][0])
        swapped = [
            (part_shift(value, e), (offset, e, start))
            for value, (offset, _, start) in direct for e in range(1, n_parts)
        ]

        def plan(items):
            return dict(places=[item[1] for item in items], parts=n_parts, held=held, col_blocks=col_blocks)

        def values(items):
            return tuple(item[0] for item in items)

        chunks, copies = len(direct), n_parts - 1
        first = []
        more = direct + swapped[:copies * (chunks - 1)]
        last = swapped[copies * (chunks - 1):]
        total_shape = pltpu.VMEM((col_blocks + 1, 2 * tokens, tile), F32)
        total, tiles = call(
            functools.partial(first_kernel, **plan(first)),
            (total_shape, pltpu.VMEM((row_blocks, 2 * tokens, tile), BF16)),
            (where, ids, ids), (activations, mate_activations, blocks) + values(first),
        )

        rounded, pack = call(
            own_grad_kernel,
            (
                jax.ShapeDtypeStruct((2 * rank, tokens), BF16),
                jax.ShapeDtypeStruct((rank, feats + tokens), BF16),
            ),
            (after(where, total),), (cotangent, labels, both) + tuple(chip_shift(both_later, d) for d in range(1, chips)),
        )
        mate_pack = mate_swap(pack)

        (half_grads,) = call(
            pair_grad_kernel, (jax.ShapeDtypeStruct((rank, (shard_rows + feats) // 2), BF16),),
            (where,), (rounded, activations, mate_activations, pack, mate_pack),
        )
        half_grads = after(half_grads, direct[-1][0])
        halves = lax.all_gather(half_grads, "dp")

        (total,) = call(
            functools.partial(more_kernel, **plan(more)), (total_shape,), (where, all_ids),
            (on_chip(tiles), on_chip(total)) + values(more), {3: 0},
        )
        send = pltpu.VMEM((chips, share, tokens, tile), BF16)
        total, send_mate, send_own = call(
            functools.partial(last_kernel, **plan(last)), (total_shape, send, send),
            (after(where, half_grads), all_ids), (on_chip(tiles), on_chip(total)) + values(last), {3: 0},
        )

        def for_chips(first, core_got, where, *needed):
            (leaving,) = call(
                functools.partial(chip_kernel, first=first),
                (pltpu.VMEM((chips - 1, share, tokens, tile), BF16),), (where,), (on_chip(total), core_got),
            )
            if needed:
                leaving = after(leaving, *needed)
            return [chip_shift(leaving[d - 1], d) for d in range(1, chips)]

        core_mate = core_swap(send_mate)
        core_own = core_swap(send_own)
        mate_pieces = for_chips(tokens, core_mate, where)
        (mate_total,) = call(
            mate_kernel, (pltpu.VMEM((share, tokens, tile), BF16),), (where,),
            (on_chip(total), core_mate) + tuple(mate_pieces),
        )
        from_mate = mate_swap(mate_total)
        own_pieces = for_chips(0, core_own, where, mate_total)
        in_grad, out_grad = call(
            grad_sum_kernel,
            (jax.ShapeDtypeStruct((rank, shard_rows), F32), jax.ShapeDtypeStruct((rank, feats), F32)),
            (), (after(halves, mate_total),),
        )
        (projected,) = call(
            final_kernel, (jax.ShapeDtypeStruct((tokens, feats), BF16),), (where,),
            (rounded, output_adapter, on_chip(total), core_own) + tuple(own_pieces) + (from_mate,),
        )
        return projected, in_grad.T, out_grad

    return body


def solution(mesh):
    placed = (
        P(("parts", "dp"), "row"),
        P(("parts", "dp"), "row"),
        P(("parts", "dp")),
        P("row", "dp", None, None),
        P("row", "dp"),
        P("row", None),
        P(None, "row"),
    )
    return jax.shard_map(
        make_body(mesh.shape["parts"], mesh.shape["row"], mesh.shape["dp"]),
        mesh=mesh,
        in_specs=placed,
        out_specs=(P(("parts", "dp"), "row"), P(("parts", "row"), None), P("parts", "row")),
        check_vma=False,
    )
```

```python
import functools

import jax
import jax.numpy as jnp
from jax import lax
from jax.experimental import pallas as pl
from jax.experimental.pallas import tpu as pltpu
from jax.sharding import PartitionSpec as P

D = 8192

adapter_scale = 2.0

F32 = jnp.float32
BF16 = jnp.bfloat16


def add_blocks(total_ref, tiles_ref, blocks_ref, ids_ref, base, col_blocks, unroll):
    count = blocks_ref.shape[0]

    def one(step, carry):
        for u in range(unroll):
            k = step * unroll + u
            ident = ids_ref[base + k]
            known = jnp.maximum(ident, 0)
            row = lax.div(known, col_blocks)
            col = jnp.where(ident >= 0, lax.rem(known, col_blocks), col_blocks)
            total_ref[col] += jnp.dot(tiles_ref[row], blocks_ref[k], preferred_element_type=F32)
        return carry

    lax.fori_loop(0, count // unroll, one, 0)


def add_arrivals(where_ref, ids_ref, tiles_ref, blocks, total_ref, places, parts, held, col_blocks):
    for blocks_ref, (offset, shift, start) in zip(blocks, places):
        source = lax.rem(where_ref[0] + (parts - shift), parts)
        base = offset + source * held + start
        add_blocks(total_ref, tiles_ref, blocks_ref, ids_ref, base, col_blocks, 4)


def first_kernel(where_ref, own_ids_ref, ids_ref, own_ref, mate_ref, own_blocks_ref, *rest, **plan):
    blocks, (total_ref, tiles_ref) = rest[:-2], rest[-2:]
    row_blocks, _, tile = tiles_ref.shape
    tokens = own_ref.shape[0]
    total_ref[...] = jnp.zeros_like(total_ref)
    for i in range(row_blocks):
        tiles_ref[i, :tokens, :] = own_ref[:, i * tile:(i + 1) * tile]
        tiles_ref[i, tokens:, :] = mate_ref[:, i * tile:(i + 1) * tile]
    add_blocks(total_ref, tiles_ref, own_blocks_ref, own_ids_ref, 0, plan["col_blocks"], 8)
    add_arrivals(where_ref, ids_ref, tiles_ref, blocks, total_ref, **plan)


def more_kernel(where_ref, ids_ref, tiles_ref, old_ref, *rest, **plan):
    add_arrivals(where_ref, ids_ref, tiles_ref, rest[:-1], rest[-1], **plan)


def last_kernel(where_ref, ids_ref, tiles_ref, old_ref, *rest, **plan):
    blocks, (total_ref, send_mate, send_own) = rest[:-3], rest[-3:]
    add_arrivals(where_ref, ids_ref, tiles_ref, blocks, total_ref, **plan)
    chips, share, tokens, _ = send_mate.shape
    for chip in range(chips):
        other = (2 * chip + 1 - where_ref[1]) * share
        for q in range(share):
            send_mate[chip, q] = total_ref[other + q, tokens:, :].astype(BF16)
            send_own[chip, q] = total_ref[other + q, :tokens, :].astype(BF16)


def chip_kernel(where_ref, total_ref, core_ref, leaving_ref, *, first):
    chips, share, tokens, _ = core_ref.shape
    for d in range(1, chips):
        to_chip = lax.rem(where_ref[2] + d, chips)
        mine = (2 * to_chip + where_ref[1]) * share
        for q in range(share):
            value = total_ref[mine + q, first:first + tokens, :] + core_ref[to_chip, q].astype(F32)
            leaving_ref[d - 1, q] = value.astype(BF16)


def mate_kernel(where_ref, total_ref, core_ref, *rest):
    pieces, out_ref = rest[:-1], rest[-1]
    _, share, tokens, _ = core_ref.shape
    chip = where_ref[2]
    mine = (2 * chip + where_ref[1]) * share
    for q in range(share):
        value = total_ref[mine + q, tokens:, :] + core_ref[chip, q].astype(F32)
        for piece in pieces:
            value += piece[q].astype(F32)
        out_ref[q] = value.astype(BF16)


def ordered_sum(own, received, place):
    count = len(received) + 1
    if count == 1:
        return own
    if count == 2:
        return own + received[0]
    total = None
    for member in range(count):
        value = own
        for d, other in enumerate(received, 1):
            value = jnp.where(lax.rem(place + (count - d), count) == member, other, value)
        total = value if total is None else total + value
    return total


CONTRACT_LAST = (((1,), (1,)), ((), ()))


def low_rank_kernel(acts_ref, adapter_a_ref, cot_ref, adapter_ref, labels_ref, out_ref):
    rank = adapter_a_ref.shape[0]
    signs = (1 - 2 * labels_ref[...]).astype(F32)
    out_ref[:rank, :] = lax.dot_general(adapter_a_ref[...], acts_ref[...], CONTRACT_LAST, preferred_element_type=F32)
    out_ref[rank:, :] = signs * lax.dot_general(
        adapter_ref[...], cot_ref[...], CONTRACT_LAST, preferred_element_type=F32
    )


def own_grad_kernel(where_ref, cot_ref, labels_ref, both_ref, *rest):
    received, (rounded_ref, pack_ref) = rest[:-2], rest[-2:]
    feats = cot_ref.shape[1]
    rounded = ordered_sum(both_ref[...], [ref[...] for ref in received], where_ref[2]).astype(BF16)
    rounded_ref[...] = rounded
    rank = rounded.shape[0] // 2
    signs = (1 - 2 * labels_ref[...]).astype(F32)
    signed_low = (rounded[:rank].astype(F32) * signs).astype(BF16)
    grad = jnp.dot(signed_low, cot_ref[...], preferred_element_type=F32)
    pack_ref[:, :feats] = (adapter_scale * grad).astype(BF16)
    pack_ref[:, feats:] = rounded[rank:]


def pair_grad_kernel(
    where_ref, rounded_ref, acts_ref, mate_acts_ref, pack_ref, mate_pack_ref, half_ref, other_ref
):
    rank, shard_rows = rounded_ref.shape[0] // 2, acts_ref.shape[1]
    feats = pack_ref.shape[1] - rounded_ref.shape[1]
    in_half, out_half = shard_rows // 2, feats // 2
    back, mate_back = rounded_ref[rank:, :], mate_pack_ref[:, feats:]

    def fill(bit, out_ref):
        cols = slice(bit * in_half, (bit + 1) * in_half)
        grad = jnp.dot(back, acts_ref[:, cols], preferred_element_type=F32)
        grad = grad + jnp.dot(mate_back, mate_acts_ref[:, cols], preferred_element_type=F32)
        out_ref[:, :in_half] = (adapter_scale * grad).astype(BF16)
        cols = slice(bit * out_half, (bit + 1) * out_half)
        grad = pack_ref[:, cols].astype(F32) + mate_pack_ref[:, cols].astype(F32)
        out_ref[:, in_half:] = grad.astype(BF16)

    for bit in range(2):
        @pl.when(where_ref[3] == bit)
        def _():
            fill(bit, half_ref)
            fill(1 - bit, other_ref)


def grad_sum_kernel(where_ref, half_ref, other_ref, *rest):
    received, (in_ref, out_ref) = rest[:-2], rest[-2:]
    in_half, out_half = in_ref.shape[1] // 2, out_ref.shape[1] // 2
    count = len(received) // 2
    place = where_ref[4]

    def add(bit, own_ref, halves):
        total = ordered_sum(own_ref[...].astype(F32), [ref[...].astype(F32) for ref in halves], place)
        in_ref[:, bit * in_half:(bit + 1) * in_half] = total[:, :in_half]
        out_ref[:, bit * out_half:(bit + 1) * out_half] = total[:, in_half:]

    for bit in range(2):
        @pl.when(where_ref[3] == bit)
        def _():
            add(bit, half_ref, received[:count])
            add(1 - bit, other_ref, received[count:])


def final_kernel(where_ref, rounded_ref, adapter_ref, total_ref, core_ref, *rest):
    pieces, out_ref = rest[:-1], rest[-1]
    _, share, tokens, tile = core_ref.shape
    rank = rounded_ref.shape[0] // 2
    low = rounded_ref[:rank, :].astype(F32).T.astype(BF16)
    chip = where_ref[2]
    mine = (2 * chip + where_ref[1]) * share
    for q in range(share):
        value = total_ref[mine + q, :tokens, :] + core_ref[chip, q].astype(F32)
        for piece in pieces:
            value += piece[q].astype(F32)
        cols = slice(q * tile, (q + 1) * tile)
        extra = jnp.dot(low, adapter_ref[:, cols], preferred_element_type=F32)
        out_ref[:, cols] = (value + adapter_scale * extra).astype(BF16)


def call(kernel, outs, scalars, arrays, aliases=None):
    smem = pl.BlockSpec(memory_space=pltpu.SMEM)
    vmem = pl.BlockSpec(memory_space=pltpu.VMEM)
    return pl.pallas_call(
        kernel,
        out_shape=outs,
        in_specs=[smem] * len(scalars) + [vmem] * len(arrays),
        out_specs=tuple(vmem for _ in outs),
        input_output_aliases=aliases or {},
        cost_estimate=pl.CostEstimate(flops=0, transcendentals=0, bytes_accessed=0),
        compiler_params=pltpu.CompilerParams(vmem_limit_bytes=4 * 1024 * 1024),
    )(*scalars, *arrays)


def on_chip(value):
    return pltpu.with_memory_space_constraint(value, pltpu.VMEM)


def after(value, *needed):
    return lax.optimization_barrier((value,) + needed)[0]


def make_body(n_parts, n_row, n_dp):
    chips = n_row // 2
    group = n_dp // 2

    def core_swap(value):
        return lax.ppermute(value, "row", [(i, i ^ 1) for i in range(n_row)])

    def chip_shift(value, d):
        pairs = [(2 * a + c, 2 * ((a + d) % chips) + c) for a in range(chips) for c in range(2)]
        return lax.ppermute(value, "row", pairs)

    def mate_swap(value):
        return lax.ppermute(value, "dp", [(i, i ^ 1) for i in range(n_dp)])

    def group_shift(value, d):
        pairs = [(2 * a + h, 2 * ((a + d) % group) + h) for a in range(group) for h in range(2)]
        return lax.ppermute(value, "dp", pairs)

    def part_shift(value, d):
        return lax.ppermute(value, "parts", [(i, (i + d) % n_parts) for i in range(n_parts)])

    def body(activations, cotangent, forget_labels, kept_blocks, block_ids, adapter_a, output_adapter):
        tokens, shard_rows = activations.shape
        rank = adapter_a.shape[1]
        feats = cotangent.shape[1]
        slots, tile = kept_blocks.shape[1], kept_blocks.shape[-1]
        row_blocks = shard_rows // tile
        col_blocks = D // tile
        share = col_blocks // n_row
        part = lax.axis_index("parts")
        row_index = lax.axis_index("row")
        dp_index = lax.axis_index("dp")
        where = jnp.stack(
            [part, lax.rem(row_index, 2), lax.div(row_index, 2), lax.rem(dp_index, 2), lax.div(dp_index, 2)]
        ).astype(jnp.int32)
        blocks = kept_blocks[0]
        ids = block_ids[0]
        labels = forget_labels[None, :]

        soon = core_swap(ids)
        far_ids = [group_shift(ids, d) for d in range(1, group)]
        all_ids = far_ids[0] if group == 2 else jnp.concatenate(far_ids)
        held = slots // n_parts
        sizes = [held * k // 32 for k in (12, 12, 8)]
        starts = [sum(sizes[:k]) for k in range(len(sizes))]

        def leaving_chunk(k):
            chunk = lax.dynamic_slice_in_dim(blocks, part * held + starts[k], sizes[k], axis=0)
            return chunk if k == 0 else after(chunk, soon)

        direct = [
            (group_shift(leaving_chunk(k), d), ((d - 1) * slots, 0, starts[k]))
            for d in range(1, group) for k in range(len(starts))
        ]
        mate_activations = mate_swap(after(activations, soon))

        (both,) = call(
            low_rank_kernel, (jax.ShapeDtypeStruct((2 * rank, tokens), F32),), (),
            (activations, after(adapter_a, direct[0][0]).T, cotangent, output_adapter, labels),
        )
        both = both + core_swap(both)
        both_later = after(both, direct[1][0])
        swapped = [
            (part_shift(value, e), (offset, e, start))
            for value, (offset, _, start) in direct for e in range(1, n_parts)
        ]

        def plan(items):
            return dict(places=[item[1] for item in items], parts=n_parts, held=held, col_blocks=col_blocks)

        def values(items):
            return tuple(item[0] for item in items)

        chunks, copies = len(direct), n_parts - 1
        first = []
        more = direct + swapped[:copies * (chunks - 1)]
        last = swapped[copies * (chunks - 1):]
        total_shape = pltpu.VMEM((col_blocks + 1, 2 * tokens, tile), F32)
        total, tiles = call(
            functools.partial(first_kernel, **plan(first)),
            (total_shape, pltpu.VMEM((row_blocks, 2 * tokens, tile), BF16)),
            (where, ids, ids), (activations, mate_activations, blocks) + values(first),
        )

        rounded, pack = call(
            own_grad_kernel,
            (
                jax.ShapeDtypeStruct((2 * rank, tokens), BF16),
                jax.ShapeDtypeStruct((rank, feats + tokens), BF16),
            ),
            (after(where, total),), (cotangent, labels, both) + tuple(chip_shift(both_later, d) for d in range(1, chips)),
        )
        mate_pack = mate_swap(pack)

        half_shape = jax.ShapeDtypeStruct((rank, (shard_rows + feats) // 2), BF16)
        half_grads, other_grads = call(
            pair_grad_kernel, (half_shape, half_shape), (where,), (rounded, activations, mate_activations, pack, mate_pack),
        )
        half_grads = after(half_grads, direct[-1][0])
        far_grads = [group_shift(half_grads, d) for d in range(1, group)]

        (total,) = call(
            functools.partial(more_kernel, **plan(more)), (total_shape,), (where, all_ids),
            (on_chip(tiles), on_chip(total)) + values(more), {3: 0},
        )
        send = pltpu.VMEM((chips, share, tokens, tile), BF16)
        total, send_mate, send_own = call(
            functools.partial(last_kernel, **plan(last)), (total_shape, send, send),
            (after(where, half_grads), all_ids), (on_chip(tiles), on_chip(total)) + values(last), {3: 0},
        )

        def for_chips(first, core_got, where, *needed):
            (leaving,) = call(
                functools.partial(chip_kernel, first=first),
                (pltpu.VMEM((chips - 1, share, tokens, tile), BF16),), (where,), (on_chip(total), core_got),
            )
            if needed:
                leaving = after(leaving, *needed)
            return [chip_shift(leaving[d - 1], d) for d in range(1, chips)]

        core_mate = core_swap(send_mate)
        core_own = core_swap(send_own)
        mate_pieces = for_chips(tokens, core_mate, where)
        (mate_total,) = call(
            mate_kernel, (pltpu.VMEM((share, tokens, tile), BF16),), (where,),
            (on_chip(total), core_mate) + tuple(mate_pieces),
        )
        from_mate = mate_swap(mate_total)
        own_pieces = for_chips(0, core_own, where, mate_total)
        from_mate_grads = [mate_swap(value) for value in far_grads]
        in_grad, out_grad = call(
            grad_sum_kernel,
            (jax.ShapeDtypeStruct((rank, shard_rows), F32), jax.ShapeDtypeStruct((rank, feats), F32)),
            (where,), (half_grads, other_grads) + tuple(far_grads) + tuple(after(value, mate_total) for value in from_mate_grads),
        )
        (projected,) = call(
            final_kernel, (jax.ShapeDtypeStruct((tokens, feats), BF16),), (where,),
            (rounded, output_adapter, on_chip(total), core_own) + tuple(own_pieces) + (from_mate,),
        )
        return projected, in_grad.T, out_grad

    return body


def solution(mesh):
    placed = (
        P(("parts", "dp"), "row"),
        P(("parts", "dp"), "row"),
        P(("parts", "dp")),
        P("row", "dp", None, None),
        P("row", "dp"),
        P("row", None),
        P(None, "row"),
    )
    return jax.shard_map(
        make_body(mesh.shape["parts"], mesh.shape["row"], mesh.shape["dp"]),
        mesh=mesh,
        in_specs=placed,
        out_specs=(P(("parts", "dp"), "row"), P(("parts", "row"), None), P("parts", "row")),
        check_vma=False,
    )
```

```python
import functools

import jax
import jax.numpy as jnp
from jax import lax
from jax.experimental import pallas as pl
from jax.experimental.pallas import tpu as pltpu
from jax.sharding import PartitionSpec as P

D = 8192

adapter_scale = 2.0

F32 = jnp.float32
BF16 = jnp.bfloat16


def add_blocks(total_ref, tiles_ref, blocks_ref, ids_ref, base, col_blocks):
    count = blocks_ref.shape[0]
    unroll = max(u for u in range(1, 9) if count % u == 0)

    def one(step, carry):
        for u in range(unroll):
            k = step * unroll + u
            ident = ids_ref[base + k]
            known = jnp.maximum(ident, 0)
            row = lax.div(known, col_blocks)
            col = jnp.where(ident >= 0, lax.rem(known, col_blocks), col_blocks)
            total_ref[col] += jnp.dot(tiles_ref[row], blocks_ref[k], preferred_element_type=F32)
        return carry

    lax.fori_loop(0, count // unroll, one, 0)


def add_arrivals(where_ref, ids_ref, tiles_ref, blocks, total_ref, places, parts, held, col_blocks):
    for blocks_ref, (offset, shift, start) in zip(blocks, places):
        source = lax.rem(where_ref[0] + (parts - shift), parts)
        base = offset + source * held + start
        add_blocks(total_ref, tiles_ref, blocks_ref, ids_ref, base, col_blocks)


def first_kernel(where_ref, own_ids_ref, ids_ref, own_ref, mate_ref, own_blocks_ref, *rest, **plan):
    blocks, (total_ref, tiles_ref) = rest[:-2], rest[-2:]
    row_blocks, _, tile = tiles_ref.shape
    tokens = own_ref.shape[0]
    total_ref[...] = jnp.zeros_like(total_ref)
    for i in range(row_blocks):
        tiles_ref[i, :tokens, :] = own_ref[:, i * tile:(i + 1) * tile]
        tiles_ref[i, tokens:, :] = mate_ref[:, i * tile:(i + 1) * tile]
    add_blocks(total_ref, tiles_ref, own_blocks_ref, own_ids_ref, 0, plan["col_blocks"])
    add_arrivals(where_ref, ids_ref, tiles_ref, blocks, total_ref, **plan)


def more_kernel(where_ref, ids_ref, tiles_ref, old_ref, *rest, **plan):
    add_arrivals(where_ref, ids_ref, tiles_ref, rest[:-1], rest[-1], **plan)


def last_kernel(where_ref, ids_ref, tiles_ref, old_ref, *rest, **plan):
    blocks, (total_ref, send_mate, send_own) = rest[:-3], rest[-3:]
    add_arrivals(where_ref, ids_ref, tiles_ref, blocks, total_ref, **plan)
    chips, share, tokens, _ = send_mate.shape
    for chip in range(chips):
        other = (2 * chip + 1 - where_ref[1]) * share
        for q in range(share):
            send_mate[chip, q] = total_ref[other + q, tokens:, :].astype(BF16)
            send_own[chip, q] = total_ref[other + q, :tokens, :].astype(BF16)


def chip_kernel(where_ref, total_ref, core_ref, leaving_ref, *, first, blocks):
    chips, share, tokens, _ = core_ref.shape
    for d in range(1, chips):
        to_chip = lax.rem(where_ref[2] + d, chips)
        mine = (2 * to_chip + where_ref[1]) * share
        for k, q in enumerate(blocks):
            value = total_ref[mine + q, first:first + tokens, :] + core_ref[to_chip, q].astype(F32)
            leaving_ref[d - 1, k] = value.astype(BF16)


def mate_kernel(where_ref, total_ref, core_ref, *rest, blocks):
    pieces, out_ref = rest[:-1], rest[-1]
    _, share, tokens, _ = core_ref.shape
    chip = where_ref[2]
    mine = (2 * chip + where_ref[1]) * share
    for k, q in enumerate(blocks):
        value = total_ref[mine + q, tokens:, :] + core_ref[chip, q].astype(F32)
        for piece in pieces:
            value += piece[k].astype(F32)
        out_ref[k] = value.astype(BF16)


def ordered_sum(own, received, place):
    count = len(received) + 1
    if count == 1:
        return own
    if count == 2:
        return own + received[0]
    total = None
    for member in range(count):
        value = own
        for d, other in enumerate(received, 1):
            value = jnp.where(lax.rem(place + (count - d), count) == member, other, value)
        total = value if total is None else total + value
    return total


CONTRACT_LAST = (((1,), (1,)), ((), ()))


def low_rank_kernel(acts_ref, adapter_a_ref, cot_ref, adapter_ref, labels_ref, out_ref):
    rank = adapter_a_ref.shape[0]
    signs = (1 - 2 * labels_ref[...]).astype(F32)
    out_ref[:rank, :] = lax.dot_general(adapter_a_ref[...], acts_ref[...], CONTRACT_LAST, preferred_element_type=F32)
    out_ref[rank:, :] = signs * lax.dot_general(
        adapter_ref[...], cot_ref[...], CONTRACT_LAST, preferred_element_type=F32
    )


def own_grad_kernel(where_ref, cot_ref, labels_ref, both_ref, *rest):
    received, (rounded_ref, pack_ref) = rest[:-2], rest[-2:]
    feats = cot_ref.shape[1]
    rounded = ordered_sum(both_ref[...], [ref[...] for ref in received], where_ref[2]).astype(BF16)
    rounded_ref[...] = rounded
    rank = rounded.shape[0] // 2
    signs = (1 - 2 * labels_ref[...]).astype(F32)
    signed_low = (rounded[:rank].astype(F32) * signs).astype(BF16)
    grad = jnp.dot(signed_low, cot_ref[...], preferred_element_type=F32)
    pack_ref[:, :feats] = (adapter_scale * grad).astype(BF16)
    pack_ref[:, feats:] = rounded[rank:]


def pair_grad_kernel(
    where_ref, rounded_ref, acts_ref, mate_acts_ref, pack_ref, mate_pack_ref, half_ref, other_ref
):
    rank, shard_rows = rounded_ref.shape[0] // 2, acts_ref.shape[1]
    feats = pack_ref.shape[1] - rounded_ref.shape[1]
    in_half, out_half = shard_rows // 2, feats // 2
    back, mate_back = rounded_ref[rank:, :], mate_pack_ref[:, feats:]

    def fill(bit, out_ref):
        cols = slice(bit * in_half, (bit + 1) * in_half)
        grad = jnp.dot(back, acts_ref[:, cols], preferred_element_type=F32)
        grad = grad + jnp.dot(mate_back, mate_acts_ref[:, cols], preferred_element_type=F32)
        out_ref[:, :in_half] = (adapter_scale * grad).astype(BF16)
        cols = slice(bit * out_half, (bit + 1) * out_half)
        grad = pack_ref[:, cols].astype(F32) + mate_pack_ref[:, cols].astype(F32)
        out_ref[:, in_half:] = grad.astype(BF16)

    for bit in range(2):
        @pl.when(where_ref[3] == bit)
        def _():
            fill(bit, half_ref)
            fill(1 - bit, other_ref)


def grad_sum_kernel(where_ref, half_ref, other_ref, *rest):
    received, (in_ref, out_ref) = rest[:-2], rest[-2:]
    in_half, out_half = in_ref.shape[1] // 2, out_ref.shape[1] // 2
    count = len(received) // 2
    place = where_ref[4]

    def add(bit, own_ref, halves):
        total = ordered_sum(own_ref[...].astype(F32), [ref[...].astype(F32) for ref in halves], place)
        in_ref[:, bit * in_half:(bit + 1) * in_half] = total[:, :in_half]
        out_ref[:, bit * out_half:(bit + 1) * out_half] = total[:, in_half:]

    for bit in range(2):
        @pl.when(where_ref[3] == bit)
        def _():
            add(bit, half_ref, received[:count])
            add(1 - bit, other_ref, received[count:])


def near_kernel(where_ref, rounded_ref, adapter_ref, total_ref, core_ref, *rest):
    from_mate, near_ref = rest[:-1], rest[-1]
    _, share, tokens, tile = core_ref.shape
    rank = rounded_ref.shape[0] // 2
    low = rounded_ref[:rank, :].astype(F32).T.astype(BF16)
    chip = where_ref[2]
    mine = (2 * chip + where_ref[1]) * share
    size = from_mate[0].shape[0]
    for q in range(share):
        value = total_ref[mine + q, :tokens, :] + core_ref[chip, q].astype(F32)
        value += from_mate[q // size][q % size].astype(F32)
        extra = jnp.dot(low, adapter_ref[:, q * tile:(q + 1) * tile], preferred_element_type=F32)
        near_ref[q] = value + adapter_scale * extra


def final_kernel(near_ref, *rest):
    pieces, out_ref = rest[:-1], rest[-1]
    share, _, tile = near_ref.shape
    for q in range(share):
        value = near_ref[q]
        for piece in pieces:
            value += piece[q].astype(F32)
        out_ref[:, q * tile:(q + 1) * tile] = value.astype(BF16)


def call(kernel, outs, scalars, arrays, aliases=None):
    smem = pl.BlockSpec(memory_space=pltpu.SMEM)
    vmem = pl.BlockSpec(memory_space=pltpu.VMEM)
    return pl.pallas_call(
        kernel,
        out_shape=outs,
        in_specs=[smem] * len(scalars) + [vmem] * len(arrays),
        out_specs=tuple(vmem for _ in outs),
        input_output_aliases=aliases or {},
        cost_estimate=pl.CostEstimate(flops=0, transcendentals=0, bytes_accessed=0),
        compiler_params=pltpu.CompilerParams(vmem_limit_bytes=4 * 1024 * 1024),
    )(*scalars, *arrays)


def on_chip(value):
    return pltpu.with_memory_space_constraint(value, pltpu.VMEM)


def after(value, *needed):
    return lax.optimization_barrier((value,) + needed)[0]


def make_body(n_parts, n_row, n_dp):
    chips = n_row // 2
    group = n_dp // 2

    def core_swap(value):
        return lax.ppermute(value, "row", [(i, i ^ 1) for i in range(n_row)])

    def chip_shift(value, d):
        pairs = [(2 * a + c, 2 * ((a + d) % chips) + c) for a in range(chips) for c in range(2)]
        return lax.ppermute(value, "row", pairs)

    def mate_swap(value):
        return lax.ppermute(value, "dp", [(i, i ^ 1) for i in range(n_dp)])

    def group_shift(value, d):
        pairs = [(2 * a + h, 2 * ((a + d) % group) + h) for a in range(group) for h in range(2)]
        return lax.ppermute(value, "dp", pairs)

    def part_shift(value, d):
        return lax.ppermute(value, "parts", [(i, (i + d) % n_parts) for i in range(n_parts)])

    def body(activations, cotangent, forget_labels, kept_blocks, block_ids, adapter_a, output_adapter):
        tokens, shard_rows = activations.shape
        rank = adapter_a.shape[1]
        feats = cotangent.shape[1]
        slots, tile = kept_blocks.shape[1], kept_blocks.shape[-1]
        row_blocks = shard_rows // tile
        col_blocks = D // tile
        share = col_blocks // n_row
        part = lax.axis_index("parts")
        row_index = lax.axis_index("row")
        dp_index = lax.axis_index("dp")
        where = jnp.stack(
            [part, lax.rem(row_index, 2), lax.div(row_index, 2), lax.rem(dp_index, 2), lax.div(dp_index, 2)]
        ).astype(jnp.int32)
        blocks = kept_blocks[0]
        ids = block_ids[0]
        labels = forget_labels[None, :]

        far_ids = [group_shift(ids, d) for d in range(1, group)]
        all_ids = far_ids[0] if group == 2 else jnp.concatenate(far_ids)
        held = slots // n_parts
        sizes = [held * k // 32 for k in (16, 10, 6)]
        starts = [sum(sizes[:k]) for k in range(len(sizes))]

        def leaving_chunk(k):
            return lax.dynamic_slice_in_dim(blocks, part * held + starts[k], sizes[k], axis=0)

        first_chunk = leaving_chunk(0)
        soon = core_swap(after(ids, first_chunk))
        leaving_chunks = [first_chunk] + [after(leaving_chunk(k), soon) for k in range(1, len(starts))]
        direct = [
            (group_shift(leaving_chunks[k], d), ((d - 1) * slots, 0, starts[k]))
            for d in range(1, group) for k in range(len(starts))
        ]
        mate_activations = mate_swap(activations)

        (both,) = call(
            low_rank_kernel, (jax.ShapeDtypeStruct((2 * rank, tokens), F32),), (),
            (activations, after(adapter_a, direct[0][0]).T, cotangent, output_adapter, labels),
        )
        both = both + core_swap(both)
        both_later = after(both, direct[1][0])
        swapped = [
            (part_shift(value, e), (offset, e, start))
            for value, (offset, _, start) in direct for e in range(1, n_parts)
        ]

        def plan(items):
            return dict(places=[item[1] for item in items], parts=n_parts, held=held, col_blocks=col_blocks)

        def values(items):
            return tuple(item[0] for item in items)

        chunks, copies = len(direct), n_parts - 1
        first = []
        more = direct + swapped[:copies * (chunks - 1)]
        last = swapped[copies * (chunks - 1):]
        total_shape = pltpu.VMEM((col_blocks + 1, 2 * tokens, tile), F32)
        total, tiles = call(
            functools.partial(first_kernel, **plan(first)),
            (total_shape, pltpu.VMEM((row_blocks, 2 * tokens, tile), BF16)),
            (where, ids, ids), (activations, mate_activations, blocks) + values(first),
        )

        rounded, pack = call(
            own_grad_kernel,
            (
                jax.ShapeDtypeStruct((2 * rank, tokens), BF16),
                jax.ShapeDtypeStruct((rank, feats + tokens), BF16),
            ),
            (after(where, total),), (cotangent, labels, both) + tuple(chip_shift(both_later, d) for d in range(1, chips)),
        )
        mate_pack = mate_swap(pack)

        half_shape = jax.ShapeDtypeStruct((rank, (shard_rows + feats) // 2), BF16)
        half_grads, other_grads = call(
            pair_grad_kernel, (half_shape, half_shape), (where,), (rounded, activations, mate_activations, pack, mate_pack),
        )
        far_grads = [group_shift(half_grads, d) for d in range(1, group)]

        (total,) = call(
            functools.partial(more_kernel, **plan(more)), (total_shape,), (where, all_ids),
            (on_chip(tiles), on_chip(total)) + values(more), {3: 0},
        )
        send = pltpu.VMEM((chips, share, tokens, tile), BF16)
        total, send_mate, send_own = call(
            functools.partial(last_kernel, **plan(last)), (total_shape, send, send),
            (after(where, half_grads), all_ids), (on_chip(tiles), on_chip(total)) + values(last), {3: 0},
        )

        def for_chips(first, core_got, where, blocks):
            (leaving,) = call(
                functools.partial(chip_kernel, first=first, blocks=blocks),
                (pltpu.VMEM((chips - 1, len(blocks), tokens, tile), BF16),),
                (where,), (on_chip(total), core_got),
            )
            return [chip_shift(leaving[d - 1], d) for d in range(1, chips)]

        core_mate = core_swap(send_mate)
        core_own = core_swap(send_own)
        halves = [tuple(range(share // 2)), tuple(range(share // 2, share))]
        mate_pieces = [for_chips(tokens, core_mate, where, part_blocks) for part_blocks in halves]
        mate_totals = []
        for part_blocks, got in zip(halves, mate_pieces):
            mate_totals += call(
                functools.partial(mate_kernel, blocks=part_blocks),
                (pltpu.VMEM((len(part_blocks), tokens, tile), BF16),), (where,),
                (on_chip(total), core_mate) + tuple(got),
            )
        from_mate = [mate_swap(value) for value in mate_totals]
        own_pieces = for_chips(0, core_own, after(where, mate_totals[0]), tuple(range(share)))
        from_mate_grads = [mate_swap(after(value, *from_mate)) for value in far_grads]
        in_grad, out_grad = call(
            grad_sum_kernel,
            (jax.ShapeDtypeStruct((rank, shard_rows), F32), jax.ShapeDtypeStruct((rank, feats), F32)),
            (where,), (half_grads, other_grads) + tuple(far_grads) + tuple(from_mate_grads),
        )
        (near,) = call(
            near_kernel, (pltpu.VMEM((share, tokens, tile), F32),), (where,),
            (rounded, output_adapter, on_chip(total), core_own) + tuple(from_mate),
        )
        (projected,) = call(
            final_kernel, (jax.ShapeDtypeStruct((tokens, feats), BF16),), (), (on_chip(near),) + tuple(own_pieces),
        )
        return projected, in_grad.T, out_grad

    return body


def solution(mesh):
    placed = (
        P(("parts", "dp"), "row"),
        P(("parts", "dp"), "row"),
        P(("parts", "dp")),
        P("row", "dp", None, None),
        P("row", "dp"),
        P("row", None),
        P(None, "row"),
    )
    return jax.shard_map(
        make_body(mesh.shape["parts"], mesh.shape["row"], mesh.shape["dp"]),
        mesh=mesh,
        in_specs=placed,
        out_specs=(P(("parts", "dp"), "row"), P(("parts", "row"), None), P("parts", "row")),
        check_vma=False,
    )
```

```python
import functools

import jax
import jax.numpy as jnp
from jax import lax
from jax.experimental import pallas as pl
from jax.experimental.pallas import tpu as pltpu
from jax.sharding import PartitionSpec as P

D = 8192

adapter_scale = 2.0

F32 = jnp.float32
BF16 = jnp.bfloat16


def add_blocks(total_ref, tiles_ref, blocks_ref, ids_ref, base, col_blocks):
    count = blocks_ref.shape[0]
    unroll = max(u for u in range(1, 9) if count % u == 0)

    def one(step, carry):
        for u in range(unroll):
            k = step * unroll + u
            ident = ids_ref[base + k]
            known = jnp.maximum(ident, 0)
            row = lax.div(known, col_blocks)
            col = jnp.where(ident >= 0, lax.rem(known, col_blocks), col_blocks)
            total_ref[col] += jnp.dot(tiles_ref[row], blocks_ref[k], preferred_element_type=F32)
        return carry

    lax.fori_loop(0, count // unroll, one, 0)


def add_arrivals(where_ref, ids_ref, tiles_ref, blocks, total_ref, places, parts, held, col_blocks):
    for blocks_ref, (offset, shift, start) in zip(blocks, places):
        source = lax.rem(where_ref[0] + (parts - shift), parts)
        base = offset + source * held + start
        add_blocks(total_ref, tiles_ref, blocks_ref, ids_ref, base, col_blocks)


def first_kernel(where_ref, own_ids_ref, ids_ref, own_ref, mate_ref, own_blocks_ref, *rest, **plan):
    blocks, (total_ref, tiles_ref) = rest[:-2], rest[-2:]
    row_blocks, _, tile = tiles_ref.shape
    tokens = own_ref.shape[0]
    total_ref[...] = jnp.zeros_like(total_ref)
    for i in range(row_blocks):
        tiles_ref[i, :tokens, :] = own_ref[:, i * tile:(i + 1) * tile]
        tiles_ref[i, tokens:, :] = mate_ref[:, i * tile:(i + 1) * tile]
    add_blocks(total_ref, tiles_ref, own_blocks_ref, own_ids_ref, 0, plan["col_blocks"])
    add_arrivals(where_ref, ids_ref, tiles_ref, blocks, total_ref, **plan)


def more_kernel(where_ref, ids_ref, tiles_ref, old_ref, *rest, **plan):
    add_arrivals(where_ref, ids_ref, tiles_ref, rest[:-1], rest[-1], **plan)


def last_kernel(where_ref, ids_ref, tiles_ref, old_ref, *rest, block_count, **plan):
    blocks, total_ref, sends = rest[:block_count], rest[block_count], rest[block_count + 1:]
    add_arrivals(where_ref, ids_ref, tiles_ref, blocks, total_ref, **plan)
    far_mate, near_mate, far_own, near_own = sends[:4], sends[4:5], sends[5:7], sends[7:]
    tokens, share = near_own[0].shape[1], near_own[0].shape[0]
    chips = far_own[0].shape[0] + 1

    def copy(pieces, token, d):
        to_chip = lax.rem(where_ref[2] + d, chips)
        block = (2 * to_chip + 1 - where_ref[1]) * share
        for piece in pieces:
            target = piece.at[d - 1] if d > 0 else piece
            for k in range(target.shape[0]):
                target[k] = total_ref[block + k, token:token + tokens, :].astype(BF16)
            block = block + target.shape[0]

    for d in range(1, chips):
        copy(far_mate, tokens, d)
    copy(near_mate, tokens, 0)
    for d in range(1, chips):
        copy(far_own, 0, d)
    copy(near_own, 0, 0)


def chip_kernel(where_ref, total_ref, *rest, token, block):
    pieces, leaving_ref = rest[:-1], rest[-1]
    others, _, tokens, _ = leaving_ref.shape
    chips = others + 1
    for d in range(1, chips):
        to_chip = lax.rem(where_ref[2] + d, chips)
        first = (2 * to_chip + where_ref[1]) * where_ref[5] + block
        done = 0
        for piece in pieces:
            for k in range(piece.shape[1]):
                value = total_ref[first + done, token:token + tokens, :] + piece[d - 1, k].astype(F32)
                leaving_ref[d - 1, done] = value.astype(BF16)
                done += 1


def mate_kernel(where_ref, total_ref, core_ref, *rest, block):
    pieces, out_ref = rest[:-1], rest[-1]
    size, tokens, _ = out_ref.shape
    first = (2 * where_ref[2] + where_ref[1]) * where_ref[5] + block
    for k in range(size):
        value = total_ref[first + k, tokens:, :] + core_ref[block + k].astype(F32)
        for piece in pieces:
            value += piece[k].astype(F32)
        out_ref[k] = value.astype(BF16)


def ordered_sum(own, received, place):
    count = len(received) + 1
    if count == 1:
        return own
    if count == 2:
        return own + received[0]
    total = None
    for member in range(count):
        value = own
        for d, other in enumerate(received, 1):
            value = jnp.where(lax.rem(place + (count - d), count) == member, other, value)
        total = value if total is None else total + value
    return total


CONTRACT_LAST = (((1,), (1,)), ((), ()))


def low_rank_kernel(acts_ref, adapter_a_ref, cot_ref, adapter_ref, labels_ref, out_ref):
    rank = adapter_a_ref.shape[0]
    signs = (1 - 2 * labels_ref[...]).astype(F32)
    out_ref[:rank, :] = lax.dot_general(adapter_a_ref[...], acts_ref[...], CONTRACT_LAST, preferred_element_type=F32)
    out_ref[rank:, :] = signs * lax.dot_general(
        adapter_ref[...], cot_ref[...], CONTRACT_LAST, preferred_element_type=F32
    )


def own_grad_kernel(where_ref, cot_ref, labels_ref, both_ref, *rest):
    received, (rounded_ref, pack_ref) = rest[:-2], rest[-2:]
    feats = cot_ref.shape[1]
    rounded = ordered_sum(both_ref[...], [ref[...] for ref in received], where_ref[2]).astype(BF16)
    rounded_ref[...] = rounded
    rank = rounded.shape[0] // 2
    signs = (1 - 2 * labels_ref[...]).astype(F32)
    signed_low = (rounded[:rank].astype(F32) * signs).astype(BF16)
    grad = jnp.dot(signed_low, cot_ref[...], preferred_element_type=F32)
    pack_ref[:, :feats] = (adapter_scale * grad).astype(BF16)
    pack_ref[:, feats:] = rounded[rank:]


def pair_grad_kernel(
    where_ref, rounded_ref, acts_ref, mate_acts_ref, pack_ref, mate_pack_ref, half_ref, other_ref
):
    rank, shard_rows = rounded_ref.shape[0] // 2, acts_ref.shape[1]
    feats = pack_ref.shape[1] - rounded_ref.shape[1]
    in_half, out_half = shard_rows // 2, feats // 2
    back, mate_back = rounded_ref[rank:, :], mate_pack_ref[:, feats:]

    def fill(bit, out_ref):
        cols = slice(bit * in_half, (bit + 1) * in_half)
        grad = jnp.dot(back, acts_ref[:, cols], preferred_element_type=F32)
        grad = grad + jnp.dot(mate_back, mate_acts_ref[:, cols], preferred_element_type=F32)
        out_ref[:, :in_half] = (adapter_scale * grad).astype(BF16)
        cols = slice(bit * out_half, (bit + 1) * out_half)
        grad = pack_ref[:, cols].astype(F32) + mate_pack_ref[:, cols].astype(F32)
        out_ref[:, in_half:] = grad.astype(BF16)

    for bit in range(2):
        @pl.when(where_ref[3] == bit)
        def _():
            fill(bit, half_ref)
            fill(1 - bit, other_ref)


def grad_sum_kernel(where_ref, half_ref, other_ref, *rest):
    received, (in_ref, out_ref) = rest[:-2], rest[-2:]
    in_half, out_half = in_ref.shape[1] // 2, out_ref.shape[1] // 2
    count = len(received) // 2
    place = where_ref[4]

    def add(bit, own_ref, halves):
        total = ordered_sum(own_ref[...].astype(F32), [ref[...].astype(F32) for ref in halves], place)
        in_ref[:, bit * in_half:(bit + 1) * in_half] = total[:, :in_half]
        out_ref[:, bit * out_half:(bit + 1) * out_half] = total[:, in_half:]

    for bit in range(2):
        @pl.when(where_ref[3] == bit)
        def _():
            add(bit, half_ref, received[:count])
            add(1 - bit, other_ref, received[count:])


def near_kernel(where_ref, rounded_ref, adapter_ref, total_ref, core_ref, *rest):
    from_mate, near_ref = rest[:-1], rest[-1]
    share, tokens, tile = core_ref.shape
    rank = rounded_ref.shape[0] // 2
    low = rounded_ref[:rank, :].astype(F32).T.astype(BF16)
    mine = (2 * where_ref[2] + where_ref[1]) * share
    size = from_mate[0].shape[0]
    for q in range(share):
        piece = from_mate[0][q] if q < size else from_mate[1][q - size]
        value = total_ref[mine + q, :tokens, :] + core_ref[q].astype(F32)
        value += piece.astype(F32)
        extra = jnp.dot(low, adapter_ref[:, q * tile:(q + 1) * tile], preferred_element_type=F32)
        near_ref[q] = value + adapter_scale * extra


def final_kernel(near_ref, *rest):
    pieces, out_ref = rest[:-1], rest[-1]
    share, _, tile = near_ref.shape
    for q in range(share):
        value = near_ref[q]
        for piece in pieces:
            value += piece[q].astype(F32)
        out_ref[:, q * tile:(q + 1) * tile] = value.astype(BF16)


def call(kernel, outs, scalars, arrays, aliases=None):
    smem = pl.BlockSpec(memory_space=pltpu.SMEM)
    vmem = pl.BlockSpec(memory_space=pltpu.VMEM)
    return pl.pallas_call(
        kernel,
        out_shape=outs,
        in_specs=[smem] * len(scalars) + [vmem] * len(arrays),
        out_specs=tuple(vmem for _ in outs),
        input_output_aliases=aliases or {},
        cost_estimate=pl.CostEstimate(flops=0, transcendentals=0, bytes_accessed=0),
        compiler_params=pltpu.CompilerParams(vmem_limit_bytes=4 * 1024 * 1024),
    )(*scalars, *arrays)


def on_chip(value):
    return pltpu.with_memory_space_constraint(value, pltpu.VMEM)


def after(value, *needed):
    return lax.optimization_barrier((value,) + needed)[0]


def make_body(n_parts, n_row, n_dp):
    chips = n_row // 2
    group = n_dp // 2

    def core_swap(value):
        return lax.ppermute(value, "row", [(i, i ^ 1) for i in range(n_row)])

    def chip_shift(value, d):
        pairs = [(2 * a + c, 2 * ((a + d) % chips) + c) for a in range(chips) for c in range(2)]
        return lax.ppermute(value, "row", pairs)

    def mate_swap(value):
        return lax.ppermute(value, "dp", [(i, i ^ 1) for i in range(n_dp)])

    def group_shift(value, d):
        pairs = [(2 * a + h, 2 * ((a + d) % group) + h) for a in range(group) for h in range(2)]
        return lax.ppermute(value, "dp", pairs)

    def part_shift(value, d):
        return lax.ppermute(value, "parts", [(i, (i + d) % n_parts) for i in range(n_parts)])

    def body(activations, cotangent, forget_labels, kept_blocks, block_ids, adapter_a, output_adapter):
        tokens, shard_rows = activations.shape
        rank = adapter_a.shape[1]
        feats = cotangent.shape[1]
        slots, tile = kept_blocks.shape[1], kept_blocks.shape[-1]
        row_blocks = shard_rows // tile
        col_blocks = D // tile
        share = col_blocks // n_row
        part = lax.axis_index("parts")
        row_index = lax.axis_index("row")
        dp_index = lax.axis_index("dp")
        where = jnp.stack([
            part, lax.rem(row_index, 2), lax.div(row_index, 2),
            lax.rem(dp_index, 2), lax.div(dp_index, 2), jnp.int32(share),
        ]).astype(jnp.int32)
        blocks = kept_blocks[0]
        ids = block_ids[0]
        labels = forget_labels[None, :]

        far_ids = [group_shift(ids, d) for d in range(1, group)]
        all_ids = far_ids[0] if group == 2 else jnp.concatenate(far_ids)
        held = slots // n_parts
        sizes = [held * k // 32 for k in (16, 10, 6)]
        starts = [sum(sizes[:k]) for k in range(len(sizes))]
        leaving_chunks = [
            after(lax.dynamic_slice_in_dim(blocks, part * held + start, size, axis=0), all_ids)
            for start, size in zip(starts, sizes)
        ]
        direct = [
            (group_shift(leaving_chunks[k], d), ((d - 1) * slots, 0, starts[k]))
            for d in range(1, group) for k in range(len(starts))
        ]
        mate_activations = mate_swap(after(activations, all_ids))

        soon = core_swap(after(ids + 1, all_ids, leaving_chunks[0]))
        (both,) = call(
            low_rank_kernel, (jax.ShapeDtypeStruct((2 * rank, tokens), F32),), (),
            (activations, after(adapter_a, soon).T, cotangent, after(output_adapter, soon), labels),
        )
        both = both + core_swap(both)
        rounded, pack = call(
            own_grad_kernel,
            (
                jax.ShapeDtypeStruct((2 * rank, tokens), BF16),
                jax.ShapeDtypeStruct((rank, feats + tokens), BF16),
            ),
            (where,), (cotangent, labels, both) + tuple(chip_shift(both, d) for d in range(1, chips)),
        )
        mate_pack = mate_swap(pack)

        def chunk(items, k):
            return [item for item in items if item[1][2] == starts[k]]

        def plan(items):
            return dict(places=[item[1] for item in items], parts=n_parts, held=held, col_blocks=col_blocks)

        def values(items):
            return tuple(item[0] for item in items)

        total_shape = pltpu.VMEM((col_blocks + 1, 2 * tokens, tile), F32)
        total, tiles = call(
            functools.partial(first_kernel, **plan([])),
            (total_shape, pltpu.VMEM((row_blocks, 2 * tokens, tile), BF16)),
            (after(where, rounded, leaving_chunks[-1]), ids, all_ids), (activations, mate_activations, blocks),
        )
        half_shape = jax.ShapeDtypeStruct((rank, (shard_rows + feats) // 2), BF16)
        half_grads, other_grads = call(
            pair_grad_kernel, (half_shape, half_shape), (where,), (rounded, activations, mate_activations, pack, mate_pack),
        )
        far_grads = [group_shift(half_grads, d) for d in range(1, group)]

        swapped = [
            (part_shift(after(value, total) if start == 0 else after(value, half_grads) if start == starts[1] else value, e), (offset, e, start))
            for value, (offset, _, start) in direct for e in range(1, n_parts)
        ]
        more = direct + chunk(swapped, 0) + chunk(swapped, 1)
        last = chunk(swapped, 2)

        (total,) = call(
            functools.partial(more_kernel, **plan(more)), (total_shape,), (where, all_ids),
            (on_chip(tiles), on_chip(total)) + values(more), {3: 0},
        )
        small = share // 4
        half = share // 2

        def far_piece(size):
            return pltpu.VMEM((chips - 1, size, tokens, tile), BF16)

        def near_piece(size):
            return pltpu.VMEM((size, tokens, tile), BF16)

        total, *sends = call(
            functools.partial(last_kernel, block_count=len(last), **plan(last)),
            (total_shape,) + (far_piece(small),) * 4 + (near_piece(share),)
            + (far_piece(half),) * 2 + (near_piece(share),),
            (after(where, half_grads), all_ids), (on_chip(tiles), on_chip(total)) + values(last), {3: 0},
        )

        cores = [core_swap(value) for value in sends[:5]]

        def for_chips(pieces, token, block, *needed):
            size = sum(piece.shape[1] for piece in pieces)
            (leaving,) = call(
                functools.partial(chip_kernel, token=token, block=block), (far_piece(size),),
                (after(where, *needed) if needed else where,), (on_chip(total),) + tuple(pieces),
            )
            return leaving, [chip_shift(leaving[d - 1], d) for d in range(1, chips)]

        leaving_first, pieces_first = for_chips(cores[:1], tokens, 0)
        leaving_second, pieces_second = for_chips(cores[1:4], tokens, small, leaving_first)
        cores += [core_swap(after(value, leaving_second)) for value in sends[5:]]
        leaving_own, own_pieces = for_chips(cores[5:7], 0, 0)
        far_grads = [after(value, *pieces_first) for value in far_grads]
        mate_grads = [mate_swap(value) for value in far_grads]

        def for_mate(pieces, size, block, *needed):
            (value,) = call(
                functools.partial(mate_kernel, block=block), (near_piece(size),),
                (after(where, *needed) if needed else where,), (on_chip(total), cores[4]) + tuple(pieces),
            )
            return mate_swap(value)

        from_mate_first = for_mate(pieces_first, small, 0)
        from_mate = [
            from_mate_first, for_mate(pieces_second, share - small, small, from_mate_first, *mate_grads),
        ]
        in_grad, out_grad = call(
            grad_sum_kernel,
            (jax.ShapeDtypeStruct((rank, shard_rows), F32), jax.ShapeDtypeStruct((rank, feats), F32)),
            (where,), (half_grads, other_grads) + tuple(far_grads) + tuple(mate_grads),
        )
        (near,) = call(
            near_kernel, (pltpu.VMEM((share, tokens, tile), F32),), (where,),
            (rounded, output_adapter, on_chip(total), cores[7]) + tuple(from_mate),
        )
        (projected,) = call(
            final_kernel, (jax.ShapeDtypeStruct((tokens, feats), BF16),), (), (on_chip(near),) + tuple(own_pieces),
        )
        return projected, in_grad.T, out_grad

    return body


def solution(mesh):
    placed = (
        P(("parts", "dp"), "row"),
        P(("parts", "dp"), "row"),
        P(("parts", "dp")),
        P("row", "dp", None, None),
        P("row", "dp"),
        P("row", None),
        P(None, "row"),
    )
    return jax.shard_map(
        make_body(mesh.shape["parts"], mesh.shape["row"], mesh.shape["dp"]),
        mesh=mesh,
        in_specs=placed,
        out_specs=(P(("parts", "dp"), "row"), P(("parts", "row"), None), P("parts", "row")),
        check_vma=False,
    )
```

```python
import functools

import jax
import jax.numpy as jnp
from jax import lax
from jax.experimental import pallas as pl
from jax.experimental.pallas import tpu as pltpu
from jax.sharding import PartitionSpec as P

D = 8192

adapter_scale = 2.0

F32 = jnp.float32
BF16 = jnp.bfloat16


def add_blocks(total_ref, tiles_ref, blocks_ref, count, ident_at, col_blocks):
    unroll = max(u for u in range(1, 9) if count % u == 0)

    def one(step, carry):
        for u in range(unroll):
            k = step * unroll + u
            ident = ident_at(k)
            known = jnp.maximum(ident, 0)
            row = lax.div(known, col_blocks)
            col = jnp.where(ident >= 0, lax.rem(known, col_blocks), col_blocks)
            total_ref[col] += jnp.dot(tiles_ref[row], blocks_ref[k], preferred_element_type=F32)
        return carry

    lax.fori_loop(0, count // unroll, one, 0)


def add_arrivals(where_ref, ids_ref, tiles_ref, blocks, total_ref, places, parts, held, col_blocks):
    for blocks_ref, (source, shift, start, size) in zip(blocks, places):
        base = lax.rem(where_ref[0] + (parts - shift), parts) * held + start
        add_blocks(
            total_ref, tiles_ref, blocks_ref, size, lambda k: ids_ref[source, base + k], col_blocks
        )


def ids_kernel(*refs, col_blocks):
    coded, ids_ref = refs[:-1], refs[-1]
    for source, ref in enumerate(coded):
        code = ref[ref.shape[0] - 1].astype(F32)
        ids_ref[source:source + 1, :] = (code[0:1, :] * col_blocks + code[1:2, :]).astype(jnp.int32)


def first_kernel(where_ref, ids_ref, own_ref, mate_ref, own_blocks_ref, total_ref, tiles_ref, *, col_blocks):
    row_blocks, _, tile = tiles_ref.shape
    tokens = own_ref.shape[0]
    total_ref[...] = jnp.zeros_like(total_ref)
    for i in range(row_blocks):
        tiles_ref[i, :tokens, :] = own_ref[:, i * tile:(i + 1) * tile]
        tiles_ref[i, tokens:, :] = mate_ref[:, i * tile:(i + 1) * tile]
    add_blocks(
        total_ref, tiles_ref, own_blocks_ref, own_blocks_ref.shape[0], lambda k: ids_ref[k], col_blocks
    )


def more_kernel(where_ref, ids_ref, tiles_ref, old_ref, *rest, **plan):
    add_arrivals(where_ref, ids_ref, tiles_ref, rest[:-1], rest[-1], **plan)


def last_kernel(where_ref, ids_ref, tiles_ref, old_ref, *rest, block_count, **plan):
    blocks, total_ref, sends = rest[:block_count], rest[block_count], rest[block_count + 1:]
    add_arrivals(where_ref, ids_ref, tiles_ref, blocks, total_ref, **plan)
    far_mate, near_mate, far_own, near_own = sends[:4], sends[4:5], sends[5:7], sends[7:]
    tokens, share = near_own[0].shape[1], near_own[0].shape[0]
    chips = far_own[0].shape[0] + 1

    def copy(pieces, token, d):
        to_chip = lax.rem(where_ref[2] + d, chips)
        block = (2 * to_chip + 1 - where_ref[1]) * share
        for piece in pieces:
            target = piece.at[d - 1] if d > 0 else piece
            for k in range(target.shape[0]):
                target[k] = total_ref[block + k, token:token + tokens, :].astype(BF16)
            block = block + target.shape[0]

    for d in range(1, chips):
        copy(far_mate, tokens, d)
    copy(near_mate, tokens, 0)
    for d in range(1, chips):
        copy(far_own, 0, d)
    copy(near_own, 0, 0)


def chip_kernel(where_ref, total_ref, *rest, token, block):
    pieces, leaving_ref = rest[:-1], rest[-1]
    others, _, tokens, _ = leaving_ref.shape
    chips = others + 1
    for d in range(1, chips):
        to_chip = lax.rem(where_ref[2] + d, chips)
        first = (2 * to_chip + where_ref[1]) * where_ref[5] + block
        done = 0
        for piece in pieces:
            for k in range(piece.shape[1]):
                value = total_ref[first + done, token:token + tokens, :] + piece[d - 1, k].astype(F32)
                leaving_ref[d - 1, done] = value.astype(BF16)
                done += 1


def mate_kernel(where_ref, total_ref, core_ref, *rest, block):
    pieces, out_ref = rest[:-1], rest[-1]
    size, tokens, _ = out_ref.shape
    first = (2 * where_ref[2] + where_ref[1]) * where_ref[5] + block
    for k in range(size):
        value = total_ref[first + k, tokens:, :] + core_ref[block + k].astype(F32)
        for piece in pieces:
            value += piece[k].astype(F32)
        out_ref[k] = value.astype(BF16)


def ordered_sum(own, received, place):
    count = len(received) + 1
    if count == 1:
        return own
    if count == 2:
        return own + received[0]
    total = None
    for member in range(count):
        value = own
        for d, other in enumerate(received, 1):
            value = jnp.where(lax.rem(place + (count - d), count) == member, other, value)
        total = value if total is None else total + value
    return total


CONTRACT_LAST = (((1,), (1,)), ((), ()))


def low_rank_kernel(acts_ref, adapter_a_ref, cot_ref, adapter_ref, labels_ref, out_ref):
    rank = adapter_a_ref.shape[0]
    signs = (1 - 2 * labels_ref[...]).astype(F32)
    out_ref[:rank, :] = lax.dot_general(adapter_a_ref[...], acts_ref[...], CONTRACT_LAST, preferred_element_type=F32)
    out_ref[rank:, :] = signs * lax.dot_general(
        adapter_ref[...], cot_ref[...], CONTRACT_LAST, preferred_element_type=F32
    )


def own_grad_kernel(where_ref, cot_ref, labels_ref, both_ref, *rest):
    received, (rounded_ref, pack_ref) = rest[:-2], rest[-2:]
    feats = cot_ref.shape[1]
    rounded = ordered_sum(both_ref[...], [ref[...] for ref in received], where_ref[2]).astype(BF16)
    rounded_ref[...] = rounded
    rank = rounded.shape[0] // 2
    signs = (1 - 2 * labels_ref[...]).astype(F32)
    signed_low = (rounded[:rank].astype(F32) * signs).astype(BF16)
    grad = jnp.dot(signed_low, cot_ref[...], preferred_element_type=F32)
    pack_ref[:, :feats] = (adapter_scale * grad).astype(BF16)
    pack_ref[:, feats:] = rounded[rank:]


def pair_grad_kernel(
    where_ref, rounded_ref, acts_ref, mate_acts_ref, pack_ref, mate_pack_ref, half_ref, other_ref
):
    rank, shard_rows = rounded_ref.shape[0] // 2, acts_ref.shape[1]
    feats = pack_ref.shape[1] - rounded_ref.shape[1]
    in_half, out_half = shard_rows // 2, feats // 2
    back, mate_back = rounded_ref[rank:, :], mate_pack_ref[:, feats:]

    def fill(bit, out_ref):
        cols = slice(bit * in_half, (bit + 1) * in_half)
        grad = jnp.dot(back, acts_ref[:, cols], preferred_element_type=F32)
        grad = grad + jnp.dot(mate_back, mate_acts_ref[:, cols], preferred_element_type=F32)
        out_ref[:, :in_half] = (adapter_scale * grad).astype(BF16)
        cols = slice(bit * out_half, (bit + 1) * out_half)
        grad = pack_ref[:, cols].astype(F32) + mate_pack_ref[:, cols].astype(F32)
        out_ref[:, in_half:] = grad.astype(BF16)

    for bit in range(2):
        @pl.when(where_ref[3] == bit)
        def _():
            fill(bit, half_ref)
            fill(1 - bit, other_ref)


def grad_sum_kernel(where_ref, half_ref, other_ref, *rest):
    received, (in_ref, out_ref) = rest[:-2], rest[-2:]
    in_half, out_half = in_ref.shape[1] // 2, out_ref.shape[1] // 2
    count = len(received) // 2
    place = where_ref[4]

    def add(bit, own_ref, halves):
        total = ordered_sum(own_ref[...].astype(F32), [ref[...].astype(F32) for ref in halves], place)
        in_ref[:, bit * in_half:(bit + 1) * in_half] = total[:, :in_half]
        out_ref[:, bit * out_half:(bit + 1) * out_half] = total[:, in_half:]

    for bit in range(2):
        @pl.when(where_ref[3] == bit)
        def _():
            add(bit, half_ref, received[:count])
            add(1 - bit, other_ref, received[count:])


def near_kernel(where_ref, rounded_ref, adapter_ref, total_ref, core_ref, *rest):
    from_mate, near_ref = rest[:-1], rest[-1]
    share, tokens, tile = core_ref.shape
    rank = rounded_ref.shape[0] // 2
    low = rounded_ref[:rank, :].astype(F32).T.astype(BF16)
    mine = (2 * where_ref[2] + where_ref[1]) * share
    size = from_mate[0].shape[0]
    for q in range(share):
        piece = from_mate[0][q] if q < size else from_mate[1][q - size]
        value = total_ref[mine + q, :tokens, :] + core_ref[q].astype(F32)
        value += piece.astype(F32)
        extra = jnp.dot(low, adapter_ref[:, q * tile:(q + 1) * tile], preferred_element_type=F32)
        near_ref[q] = value + adapter_scale * extra


def final_kernel(near_ref, *rest):
    pieces, out_ref = rest[:-1], rest[-1]
    share, _, tile = near_ref.shape
    for q in range(share):
        value = near_ref[q]
        for piece in pieces:
            value += piece[q].astype(F32)
        out_ref[:, q * tile:(q + 1) * tile] = value.astype(BF16)


def call(kernel, outs, scalars, arrays, aliases=None):
    smem = pl.BlockSpec(memory_space=pltpu.SMEM)
    vmem = pl.BlockSpec(memory_space=pltpu.VMEM)
    return pl.pallas_call(
        kernel,
        out_shape=outs,
        in_specs=[smem] * len(scalars) + [vmem] * len(arrays),
        out_specs=tuple(vmem for _ in outs),
        input_output_aliases=aliases or {},
        cost_estimate=pl.CostEstimate(flops=0, transcendentals=0, bytes_accessed=0),
        compiler_params=pltpu.CompilerParams(vmem_limit_bytes=4 * 1024 * 1024),
    )(*scalars, *arrays)


def on_chip(value):
    return pltpu.with_memory_space_constraint(value, pltpu.VMEM)


def after(value, *needed):
    return lax.optimization_barrier((value,) + needed)[0]


def make_body(n_parts, n_row, n_dp):
    chips = n_row // 2
    group = n_dp // 2

    def core_swap(value):
        return lax.ppermute(value, "row", [(i, i ^ 1) for i in range(n_row)])

    def chip_shift(value, d):
        pairs = [(2 * a + c, 2 * ((a + d) % chips) + c) for a in range(chips) for c in range(2)]
        return lax.ppermute(value, "row", pairs)

    def mate_swap(value):
        return lax.ppermute(value, "dp", [(i, i ^ 1) for i in range(n_dp)])

    def group_shift(value, d):
        pairs = [(2 * a + h, 2 * ((a + d) % group) + h) for a in range(group) for h in range(2)]
        return lax.ppermute(value, "dp", pairs)

    def part_shift(value, d):
        return lax.ppermute(value, "parts", [(i, (i + d) % n_parts) for i in range(n_parts)])

    def body(activations, cotangent, forget_labels, kept_blocks, block_ids, adapter_a, output_adapter):
        tokens, shard_rows = activations.shape
        rank = adapter_a.shape[1]
        feats = cotangent.shape[1]
        slots, tile = kept_blocks.shape[1], kept_blocks.shape[-1]
        row_blocks = shard_rows // tile
        col_blocks = D // tile
        share = col_blocks // n_row
        part = lax.axis_index("parts")
        row_index = lax.axis_index("row")
        dp_index = lax.axis_index("dp")
        where = jnp.stack([
            part, lax.rem(row_index, 2), lax.div(row_index, 2),
            lax.rem(dp_index, 2), lax.div(dp_index, 2), jnp.int32(share),
        ]).astype(jnp.int32)
        blocks = kept_blocks[0]
        ids = block_ids[0]
        labels = forget_labels[None, :]

        held = slots // n_parts
        sizes = [held * k // 32 for k in (14, 12, 6)]
        starts = [sum(sizes[:k]) for k in range(len(sizes))]
        leaving_chunks = [
            lax.dynamic_slice_in_dim(blocks, part * held + start, size, axis=0)
            for start, size in zip(starts, sizes)
        ]
        known = jnp.maximum(ids, 0)
        code = jnp.stack([
            jnp.where(ids >= 0, lax.div(known, col_blocks), -1),
            jnp.where(ids >= 0, lax.rem(known, col_blocks), 0),
        ]).astype(BF16)
        code = jnp.pad(code, ((0, tile - 2), (0, tile - slots)))[None]
        soon = core_swap(after(ids + 1, leaving_chunks[0]))
        leaving_chunks[1] = jnp.concatenate([leaving_chunks[1], code], axis=0)
        leaving_chunks[1:] = [after(chunk, soon) for chunk in leaving_chunks[1:]]
        direct = [
            (group_shift(leaving_chunks[k], d), (d - 1, 0, starts[k], sizes[k]))
            for d in range(1, group) for k in range(len(starts))
        ]
        mate_activations = mate_swap(activations)

        (both,) = call(
            low_rank_kernel, (jax.ShapeDtypeStruct((2 * rank, tokens), F32),), (),
            (activations, after(adapter_a, soon).T, cotangent, after(output_adapter, soon), labels),
        )
        both = both + core_swap(both)
        rounded, pack = call(
            own_grad_kernel,
            (
                jax.ShapeDtypeStruct((2 * rank, tokens), BF16),
                jax.ShapeDtypeStruct((rank, feats + tokens), BF16),
            ),
            (where,), (cotangent, labels, both) + tuple(chip_shift(both, d) for d in range(1, chips)),
        )
        mate_pack = mate_swap(pack)

        def chunk(items, k):
            return [item for item in items if item[1][2] == starts[k]]

        def plan(items):
            return dict(places=[item[1] for item in items], parts=n_parts, held=held, col_blocks=col_blocks)

        def values(items):
            return tuple(item[0] for item in items)

        total_shape = pltpu.VMEM((col_blocks + 1, 2 * tokens, tile), F32)
        total, tiles = call(
            functools.partial(first_kernel, col_blocks=col_blocks),
            (total_shape, pltpu.VMEM((row_blocks, 2 * tokens, tile), BF16)),
            (after(where, rounded, leaving_chunks[-1]), ids), (activations, mate_activations, blocks),
        )
        half_shape = jax.ShapeDtypeStruct((rank, (shard_rows + feats) // 2), BF16)
        half_grads, other_grads = call(
            pair_grad_kernel, (half_shape, half_shape), (where,), (rounded, activations, mate_activations, pack, mate_pack),
        )
        far_grads = [group_shift(half_grads, d) for d in range(1, group)]

        (all_ids,) = call(
            functools.partial(ids_kernel, col_blocks=col_blocks),
            (jax.ShapeDtypeStruct((group - 1, tile), jnp.int32),), (),
            tuple(value for value, place in direct if place[2] == starts[1]),
        )
        gates = {starts[0]: rounded, starts[1]: total, starts[2]: half_grads}
        swapped = [
            (part_shift(after(value, gates[start])[:size], e), (source, e, start, size))
            for value, (source, _, start, size) in direct for e in range(1, n_parts)
        ]
        more = direct + chunk(swapped, 0) + chunk(swapped, 1)
        last = chunk(swapped, 2)

        (total,) = call(
            functools.partial(more_kernel, **plan(more)), (total_shape,), (where, all_ids),
            (on_chip(tiles), on_chip(total)) + values(more), {3: 0},
        )
        small = share // 4
        half = share // 2

        def far_piece(size):
            return pltpu.VMEM((chips - 1, size, tokens, tile), BF16)

        def near_piece(size):
            return pltpu.VMEM((size, tokens, tile), BF16)

        total, *sends = call(
            functools.partial(last_kernel, block_count=len(last), **plan(last)),
            (total_shape,) + (far_piece(small),) * 4 + (near_piece(share),)
            + (far_piece(half),) * 2 + (near_piece(share),),
            (after(where, half_grads), all_ids), (on_chip(tiles), on_chip(total)) + values(last), {3: 0},
        )

        cores = [core_swap(value) for value in sends[:5]]

        def for_chips(pieces, token, block, *needed):
            size = sum(piece.shape[1] for piece in pieces)
            (leaving,) = call(
                functools.partial(chip_kernel, token=token, block=block), (far_piece(size),),
                (after(where, *needed) if needed else where,), (on_chip(total),) + tuple(pieces),
            )
            return leaving, [chip_shift(leaving[d - 1], d) for d in range(1, chips)]

        leaving_first, pieces_first = for_chips(cores[:1], tokens, 0)
        leaving_second, pieces_second = for_chips(cores[1:4], tokens, small, leaving_first)
        cores += [core_swap(after(value, leaving_second)) for value in sends[5:]]
        leaving_own, own_pieces = for_chips(cores[5:7], 0, 0)
        far_grads = [after(value, *pieces_first) for value in far_grads]
        mate_grads = [mate_swap(value) for value in far_grads]

        def for_mate(pieces, size, block, *needed):
            (value,) = call(
                functools.partial(mate_kernel, block=block), (near_piece(size),),
                (after(where, *needed) if needed else where,), (on_chip(total), cores[4]) + tuple(pieces),
            )
            return mate_swap(value)

        from_mate_first = for_mate(pieces_first, small, 0)
        from_mate = [
            from_mate_first, for_mate(pieces_second, share - small, small, from_mate_first, *mate_grads),
        ]
        in_grad, out_grad = call(
            grad_sum_kernel,
            (jax.ShapeDtypeStruct((rank, shard_rows), F32), jax.ShapeDtypeStruct((rank, feats), F32)),
            (where,), (half_grads, other_grads) + tuple(far_grads) + tuple(mate_grads),
        )
        (near,) = call(
            near_kernel, (pltpu.VMEM((share, tokens, tile), F32),), (where,),
            (rounded, output_adapter, on_chip(total), cores[7]) + tuple(from_mate),
        )
        (projected,) = call(
            final_kernel, (jax.ShapeDtypeStruct((tokens, feats), BF16),), (), (on_chip(near),) + tuple(own_pieces),
        )
        return projected, in_grad.T, out_grad

    return body


def solution(mesh):
    placed = (
        P(("parts", "dp"), "row"),
        P(("parts", "dp"), "row"),
        P(("parts", "dp")),
        P("row", "dp", None, None),
        P("row", "dp"),
        P("row", None),
        P(None, "row"),
    )
    return jax.shard_map(
        make_body(mesh.shape["parts"], mesh.shape["row"], mesh.shape["dp"]),
        mesh=mesh,
        in_specs=placed,
        out_specs=(P(("parts", "dp"), "row"), P(("parts", "row"), None), P("parts", "row")),
        check_vma=False,
    )
```

```python
import functools

import jax
import jax.numpy as jnp
from jax import lax
from jax.experimental import pallas as pl
from jax.experimental.pallas import tpu as pltpu
from jax.sharding import PartitionSpec as P

D = 8192

adapter_scale = 2.0

F32 = jnp.float32
BF16 = jnp.bfloat16


def add_blocks(total_ref, tiles_ref, blocks_ref, count, ident_at, col_blocks):
    unroll = max(u for u in range(1, 9) if count % u == 0)

    def one(step, carry):
        for u in range(unroll):
            k = step * unroll + u
            ident = ident_at(k)
            known = jnp.maximum(ident, 0)
            row = lax.div(known, col_blocks)
            col = jnp.where(ident >= 0, lax.rem(known, col_blocks), col_blocks)
            total_ref[col] += jnp.dot(tiles_ref[row], blocks_ref[k], preferred_element_type=F32)
        return carry

    lax.fori_loop(0, count // unroll, one, 0)


def add_arrivals(where_ref, ids_ref, tiles_ref, blocks, total_ref, places, parts, held, col_blocks):
    for blocks_ref, (source, shift, start, size) in zip(blocks, places):
        base = lax.rem(where_ref[0] + (parts - shift), parts) * held + start
        add_blocks(
            total_ref, tiles_ref, blocks_ref, size, lambda k: ids_ref[source, base + k], col_blocks
        )


def ids_kernel(*refs, col_blocks):
    coded, ids_ref = refs[:-1], refs[-1]
    for source, ref in enumerate(coded):
        code = ref[ref.shape[0] - 1].astype(F32)
        ids_ref[source:source + 1, :] = (code[0:1, :] * col_blocks + code[1:2, :]).astype(jnp.int32)


def first_kernel(where_ref, ids_ref, own_ref, mate_ref, own_blocks_ref, total_ref, tiles_ref, *, col_blocks):
    row_blocks, _, tile = tiles_ref.shape
    tokens = own_ref.shape[0]
    total_ref[...] = jnp.zeros_like(total_ref)
    for i in range(row_blocks):
        tiles_ref[i, :tokens, :] = own_ref[:, i * tile:(i + 1) * tile]
        tiles_ref[i, tokens:, :] = mate_ref[:, i * tile:(i + 1) * tile]
    add_blocks(
        total_ref, tiles_ref, own_blocks_ref, own_blocks_ref.shape[0], lambda k: ids_ref[k], col_blocks
    )


def more_kernel(where_ref, ids_ref, tiles_ref, old_ref, *rest, **plan):
    add_arrivals(where_ref, ids_ref, tiles_ref, rest[:-1], rest[-1], **plan)


def last_kernel(where_ref, ids_ref, tiles_ref, old_ref, *rest, block_count, **plan):
    blocks, total_ref, sends = rest[:block_count], rest[block_count], rest[block_count + 1:]
    add_arrivals(where_ref, ids_ref, tiles_ref, blocks, total_ref, **plan)
    far_mate, near_mate, far_own, near_own = sends[:4], sends[4:5], sends[5:7], sends[7:]
    tokens, share = near_own[0].shape[1], near_own[0].shape[0]
    chips = far_own[0].shape[0] + 1

    def copy(pieces, token, d):
        to_chip = lax.rem(where_ref[2] + d, chips)
        block = (2 * to_chip + 1 - where_ref[1]) * share
        for piece in pieces:
            target = piece.at[d - 1] if d > 0 else piece
            for k in range(target.shape[0]):
                target[k] = total_ref[block + k, token:token + tokens, :].astype(BF16)
            block = block + target.shape[0]

    for d in range(1, chips):
        copy(far_mate, tokens, d)
    copy(near_mate, tokens, 0)
    for d in range(1, chips):
        copy(far_own, 0, d)
    copy(near_own, 0, 0)


def chip_kernel(where_ref, total_ref, *rest, token, block):
    pieces, leaving_ref = rest[:-1], rest[-1]
    others, _, tokens, _ = leaving_ref.shape
    chips = others + 1
    for d in range(1, chips):
        to_chip = lax.rem(where_ref[2] + d, chips)
        first = (2 * to_chip + where_ref[1]) * where_ref[5] + block
        done = 0
        for piece in pieces:
            for k in range(piece.shape[1]):
                value = total_ref[first + done, token:token + tokens, :] + piece[d - 1, k].astype(F32)
                leaving_ref[d - 1, done] = value.astype(BF16)
                done += 1


def mate_kernel(where_ref, total_ref, core_ref, *rest, block):
    pieces, out_ref = rest[:-1], rest[-1]
    size, tokens, _ = out_ref.shape
    first = (2 * where_ref[2] + where_ref[1]) * where_ref[5] + block
    for k in range(size):
        value = total_ref[first + k, tokens:, :] + core_ref[block + k].astype(F32)
        for piece in pieces:
            value += piece[k].astype(F32)
        out_ref[k] = value.astype(BF16)


def ordered_sum(own, received, place):
    count = len(received) + 1
    if count == 1:
        return own
    if count == 2:
        return own + received[0]
    total = None
    for member in range(count):
        value = own
        for d, other in enumerate(received, 1):
            value = jnp.where(lax.rem(place + (count - d), count) == member, other, value)
        total = value if total is None else total + value
    return total


CONTRACT_LAST = (((1,), (1,)), ((), ()))


def low_rank_kernel(acts_ref, adapter_a_ref, cot_ref, adapter_ref, labels_ref, out_ref):
    rank = adapter_a_ref.shape[0]
    signs = (1 - 2 * labels_ref[...]).astype(F32)
    out_ref[:rank, :] = lax.dot_general(adapter_a_ref[...], acts_ref[...], CONTRACT_LAST, preferred_element_type=F32)
    out_ref[rank:, :] = signs * lax.dot_general(
        adapter_ref[...], cot_ref[...], CONTRACT_LAST, preferred_element_type=F32
    )


def own_grad_kernel(where_ref, cot_ref, labels_ref, both_ref, *rest):
    received, (rounded_ref, pack_ref) = rest[:-2], rest[-2:]
    feats = cot_ref.shape[1]
    rounded = ordered_sum(both_ref[...], [ref[...] for ref in received], where_ref[2]).astype(BF16)
    rounded_ref[...] = rounded
    rank = rounded.shape[0] // 2
    signs = (1 - 2 * labels_ref[...]).astype(F32)
    signed_low = (rounded[:rank].astype(F32) * signs).astype(BF16)
    grad = jnp.dot(signed_low, cot_ref[...], preferred_element_type=F32)
    pack_ref[:, :feats] = (adapter_scale * grad).astype(BF16)
    pack_ref[:, feats:] = rounded[rank:]


def pair_grad_kernel(
    where_ref, rounded_ref, acts_ref, mate_acts_ref, pack_ref, mate_pack_ref, half_ref, other_ref
):
    rank, shard_rows = rounded_ref.shape[0] // 2, acts_ref.shape[1]
    feats = pack_ref.shape[1] - rounded_ref.shape[1]
    in_half, out_half = shard_rows // 2, feats // 2
    back, mate_back = rounded_ref[rank:, :], mate_pack_ref[:, feats:]

    def fill(bit, out_ref):
        cols = slice(bit * in_half, (bit + 1) * in_half)
        grad = jnp.dot(back, acts_ref[:, cols], preferred_element_type=F32)
        grad = grad + jnp.dot(mate_back, mate_acts_ref[:, cols], preferred_element_type=F32)
        out_ref[:, :in_half] = (adapter_scale * grad).astype(BF16)
        cols = slice(bit * out_half, (bit + 1) * out_half)
        grad = pack_ref[:, cols].astype(F32) + mate_pack_ref[:, cols].astype(F32)
        out_ref[:, in_half:] = grad.astype(BF16)

    for bit in range(2):
        @pl.when(where_ref[3] == bit)
        def _():
            fill(bit, half_ref)
            fill(1 - bit, other_ref)


def grad_sum_kernel(where_ref, half_ref, other_ref, *rest):
    received, (in_ref, out_ref) = rest[:-2], rest[-2:]
    in_half, out_half = in_ref.shape[1] // 2, out_ref.shape[1] // 2
    count = len(received) // 2
    place = where_ref[4]

    def add(bit, own_ref, halves):
        total = ordered_sum(own_ref[...].astype(F32), [ref[...].astype(F32) for ref in halves], place)
        in_ref[:, bit * in_half:(bit + 1) * in_half] = total[:, :in_half]
        out_ref[:, bit * out_half:(bit + 1) * out_half] = total[:, in_half:]

    for bit in range(2):
        @pl.when(where_ref[3] == bit)
        def _():
            add(bit, half_ref, received[:count])
            add(1 - bit, other_ref, received[count:])


def near_kernel(where_ref, rounded_ref, adapter_ref, total_ref, core_ref, *rest):
    from_mate, near_ref = rest[:-1], rest[-1]
    share, tokens, tile = core_ref.shape
    rank = rounded_ref.shape[0] // 2
    low = rounded_ref[:rank, :].astype(F32).T.astype(BF16)
    mine = (2 * where_ref[2] + where_ref[1]) * share
    size = from_mate[0].shape[0]
    for q in range(share):
        piece = from_mate[0][q] if q < size else from_mate[1][q - size]
        value = total_ref[mine + q, :tokens, :] + core_ref[q].astype(F32)
        value += piece.astype(F32)
        extra = jnp.dot(low, adapter_ref[:, q * tile:(q + 1) * tile], preferred_element_type=F32)
        near_ref[q] = value + adapter_scale * extra


def final_kernel(near_ref, *rest):
    pieces, out_ref = rest[:-1], rest[-1]
    share, _, tile = near_ref.shape
    for q in range(share):
        value = near_ref[q]
        for piece in pieces:
            value += piece[q].astype(F32)
        out_ref[:, q * tile:(q + 1) * tile] = value.astype(BF16)


def call(kernel, outs, scalars, arrays, aliases=None):
    smem = pl.BlockSpec(memory_space=pltpu.SMEM)
    vmem = pl.BlockSpec(memory_space=pltpu.VMEM)
    return pl.pallas_call(
        kernel,
        out_shape=outs,
        in_specs=[smem] * len(scalars) + [vmem] * len(arrays),
        out_specs=tuple(vmem for _ in outs),
        input_output_aliases=aliases or {},
        cost_estimate=pl.CostEstimate(flops=0, transcendentals=0, bytes_accessed=0),
        compiler_params=pltpu.CompilerParams(vmem_limit_bytes=4 * 1024 * 1024),
    )(*scalars, *arrays)


def on_chip(value):
    return pltpu.with_memory_space_constraint(value, pltpu.VMEM)


def after(value, *needed):
    return lax.optimization_barrier((value,) + needed)[0]


def make_body(n_parts, n_row, n_dp):
    chips = n_row // 2
    group = n_dp // 2

    def core_swap(value):
        return lax.ppermute(value, "row", [(i, i ^ 1) for i in range(n_row)])

    def chip_shift(value, d):
        pairs = [(2 * a + c, 2 * ((a + d) % chips) + c) for a in range(chips) for c in range(2)]
        return lax.ppermute(value, "row", pairs)

    def mate_swap(value):
        return lax.ppermute(value, "dp", [(i, i ^ 1) for i in range(n_dp)])

    def group_shift(value, d):
        pairs = [(2 * a + h, 2 * ((a + d) % group) + h) for a in range(group) for h in range(2)]
        return lax.ppermute(value, "dp", pairs)

    def part_shift(value, d):
        return lax.ppermute(value, "parts", [(i, (i + d) % n_parts) for i in range(n_parts)])

    def body(activations, cotangent, forget_labels, kept_blocks, block_ids, adapter_a, output_adapter):
        tokens, shard_rows = activations.shape
        rank = adapter_a.shape[1]
        feats = cotangent.shape[1]
        slots, tile = kept_blocks.shape[1], kept_blocks.shape[-1]
        row_blocks = shard_rows // tile
        col_blocks = D // tile
        share = col_blocks // n_row
        part = lax.axis_index("parts")
        row_index = lax.axis_index("row")
        dp_index = lax.axis_index("dp")
        where = jnp.stack([
            part, lax.rem(row_index, 2), lax.div(row_index, 2),
            lax.rem(dp_index, 2), lax.div(dp_index, 2), jnp.int32(share),
        ]).astype(jnp.int32)
        blocks = kept_blocks[0]
        ids = block_ids[0]
        labels = forget_labels[None, :]

        held = slots // n_parts
        sizes = [held * k // 32 for k in (16, 10, 6)]
        starts = [sum(sizes[:k]) for k in range(len(sizes))]
        leaving_chunks = [
            lax.dynamic_slice_in_dim(blocks, part * held + start, size, axis=0)
            for start, size in zip(starts, sizes)
        ]
        known = jnp.maximum(ids, 0)
        code = jnp.stack([
            jnp.where(ids >= 0, lax.div(known, col_blocks), -1),
            jnp.where(ids >= 0, lax.rem(known, col_blocks), 0),
        ]).astype(BF16)
        code = jnp.pad(code, ((0, tile - 2), (0, tile - slots)))[None]
        soon = core_swap(after(ids + 1, leaving_chunks[0]))
        leaving_chunks[1] = jnp.concatenate([leaving_chunks[1], code], axis=0)
        leaving_chunks[1:] = [after(chunk, soon) for chunk in leaving_chunks[1:]]
        direct = [
            (group_shift(leaving_chunks[k], d), (d - 1, 0, starts[k], sizes[k]))
            for d in range(1, group) for k in range(len(starts))
        ]
        mate_activations = mate_swap(activations)

        (both,) = call(
            low_rank_kernel, (jax.ShapeDtypeStruct((2 * rank, tokens), F32),), (),
            (activations, after(adapter_a, soon).T, cotangent, after(output_adapter, soon), labels),
        )
        both = both + core_swap(both)
        rounded, pack = call(
            own_grad_kernel,
            (
                jax.ShapeDtypeStruct((2 * rank, tokens), BF16),
                jax.ShapeDtypeStruct((rank, feats + tokens), BF16),
            ),
            (where,), (cotangent, labels, both) + tuple(chip_shift(both, d) for d in range(1, chips)),
        )
        mate_pack = mate_swap(pack)

        def chunk(items, k):
            return [item for item in items if item[1][2] == starts[k]]

        def plan(items):
            return dict(places=[item[1] for item in items], parts=n_parts, held=held, col_blocks=col_blocks)

        def values(items):
            return tuple(item[0] for item in items)

        total_shape = pltpu.VMEM((col_blocks + 1, 2 * tokens, tile), F32)
        total, tiles = call(
            functools.partial(first_kernel, col_blocks=col_blocks),
            (total_shape, pltpu.VMEM((row_blocks, 2 * tokens, tile), BF16)),
            (after(where, rounded, leaving_chunks[-1]), ids), (activations, mate_activations, blocks),
        )
        half_shape = jax.ShapeDtypeStruct((rank, (shard_rows + feats) // 2), BF16)
        half_grads, other_grads = call(
            pair_grad_kernel, (half_shape, half_shape), (after(where, total),), (rounded, activations, mate_activations, pack, mate_pack),
        )
        far_grads = [group_shift(half_grads, d) for d in range(1, group)]

        (all_ids,) = call(
            functools.partial(ids_kernel, col_blocks=col_blocks),
            (jax.ShapeDtypeStruct((group - 1, tile), jnp.int32),), (),
            tuple(value for value, place in direct if place[2] == starts[1]),
        )
        gates = {starts[0]: (rounded,), starts[1]: (mate_activations,), starts[2]: (half_grads, total)}
        swapped = [
            (part_shift((after(value, *gates[start]) if gates[start] else value)[:size], e), (source, e, start, size))
            for value, (source, _, start, size) in direct for e in range(1, n_parts)
        ]
        more = direct + chunk(swapped, 0) + chunk(swapped, 1)
        last = chunk(swapped, 2)

        (total,) = call(
            functools.partial(more_kernel, **plan(more)), (total_shape,), (where, all_ids),
            (on_chip(tiles), on_chip(total)) + values(more), {3: 0},
        )
        small = share // 4
        half = share // 2

        def far_piece(size):
            return pltpu.VMEM((chips - 1, size, tokens, tile), BF16)

        def near_piece(size):
            return pltpu.VMEM((size, tokens, tile), BF16)

        total, *sends = call(
            functools.partial(last_kernel, block_count=len(last), **plan(last)),
            (total_shape,) + (far_piece(small),) * 4 + (near_piece(share),)
            + (far_piece(half),) * 2 + (near_piece(share),),
            (after(where, half_grads), all_ids), (on_chip(tiles), on_chip(total)) + values(last), {3: 0},
        )

        cores = [core_swap(value) for value in sends[:5]]

        def for_chips(pieces, token, block, *needed):
            size = sum(piece.shape[1] for piece in pieces)
            (leaving,) = call(
                functools.partial(chip_kernel, token=token, block=block), (far_piece(size),),
                (after(where, *needed) if needed else where,), (on_chip(total),) + tuple(pieces),
            )
            return leaving, [chip_shift(leaving[d - 1], d) for d in range(1, chips)]

        leaving_first, pieces_first = for_chips(cores[:1], tokens, 0)
        leaving_second, pieces_second = for_chips(cores[1:4], tokens, small, leaving_first)
        cores += [core_swap(after(value, leaving_second)) for value in sends[5:]]
        leaving_own, own_pieces = for_chips(cores[5:7], 0, 0)
        far_grads = [after(value, *pieces_first) for value in far_grads]
        mate_grads = [mate_swap(value) for value in far_grads]

        def for_mate(pieces, size, block, *needed):
            (value,) = call(
                functools.partial(mate_kernel, block=block), (near_piece(size),),
                (after(where, *needed) if needed else where,), (on_chip(total), cores[4]) + tuple(pieces),
            )
            return mate_swap(value)

        from_mate_first = for_mate(pieces_first, small, 0)
        from_mate = [
            from_mate_first, for_mate(pieces_second, share - small, small, from_mate_first, *mate_grads),
        ]
        in_grad, out_grad = call(
            grad_sum_kernel,
            (jax.ShapeDtypeStruct((rank, shard_rows), F32), jax.ShapeDtypeStruct((rank, feats), F32)),
            (where,), (half_grads, other_grads) + tuple(far_grads) + tuple(mate_grads),
        )
        (near,) = call(
            near_kernel, (pltpu.VMEM((share, tokens, tile), F32),), (where,),
            (rounded, output_adapter, on_chip(total), cores[7]) + tuple(from_mate),
        )
        (projected,) = call(
            final_kernel, (jax.ShapeDtypeStruct((tokens, feats), BF16),), (), (on_chip(near),) + tuple(own_pieces),
        )
        return projected, in_grad.T, out_grad

    return body


def solution(mesh):
    placed = (
        P(("parts", "dp"), "row"),
        P(("parts", "dp"), "row"),
        P(("parts", "dp")),
        P("row", "dp", None, None),
        P("row", "dp"),
        P("row", None),
        P(None, "row"),
    )
    return jax.shard_map(
        make_body(mesh.shape["parts"], mesh.shape["row"], mesh.shape["dp"]),
        mesh=mesh,
        in_specs=placed,
        out_specs=(P(("parts", "dp"), "row"), P(("parts", "row"), None), P("parts", "row")),
        check_vma=False,
    )
```

```python
import functools

import jax
import jax.numpy as jnp
from jax import lax
from jax.experimental import pallas as pl
from jax.experimental.pallas import tpu as pltpu
from jax.sharding import PartitionSpec as P

D = 8192

adapter_scale = 2.0

F32 = jnp.float32
BF16 = jnp.bfloat16


def add_blocks(total_ref, tiles_ref, blocks_ref, count, ident_at, col_blocks):
    unroll = max(u for u in range(1, 9) if count % u == 0)

    def one(step, carry):
        for u in range(unroll):
            k = step * unroll + u
            ident = ident_at(k)
            known = jnp.maximum(ident, 0)
            row = lax.div(known, col_blocks)
            col = jnp.where(ident >= 0, lax.rem(known, col_blocks), col_blocks)
            total_ref[col] += jnp.dot(tiles_ref[row], blocks_ref[k], preferred_element_type=F32)
        return carry

    lax.fori_loop(0, count // unroll, one, 0)


def add_arrivals(where_ref, ids_ref, tiles_ref, blocks, total_ref, places, parts, held, col_blocks):
    for blocks_ref, (source, shift, start, size) in zip(blocks, places):
        base = lax.rem(where_ref[0] + (parts - shift), parts) * held + start
        add_blocks(
            total_ref, tiles_ref, blocks_ref, size, lambda k: ids_ref[source, base + k], col_blocks
        )


def ids_kernel(*refs, col_blocks):
    coded, ids_ref = refs[:-1], refs[-1]
    for source, ref in enumerate(coded):
        code = ref[ref.shape[0] - 1].astype(F32)
        ids_ref[source:source + 1, :] = (code[0:1, :] * col_blocks + code[1:2, :]).astype(jnp.int32)


def first_kernel(where_ref, ids_ref, own_ref, mate_ref, own_blocks_ref, total_ref, tiles_ref, *, col_blocks):
    row_blocks, _, tile = tiles_ref.shape
    tokens = own_ref.shape[0]
    total_ref[...] = jnp.zeros_like(total_ref)
    for i in range(row_blocks):
        tiles_ref[i, :tokens, :] = own_ref[:, i * tile:(i + 1) * tile]
        tiles_ref[i, tokens:, :] = mate_ref[:, i * tile:(i + 1) * tile]
    add_blocks(
        total_ref, tiles_ref, own_blocks_ref, own_blocks_ref.shape[0], lambda k: ids_ref[k], col_blocks
    )


def more_kernel(where_ref, ids_ref, tiles_ref, old_ref, *rest, **plan):
    add_arrivals(where_ref, ids_ref, tiles_ref, rest[:-1], rest[-1], **plan)


def last_kernel(where_ref, ids_ref, tiles_ref, old_ref, *rest, block_count, **plan):
    blocks, total_ref, sends = rest[:block_count], rest[block_count], rest[block_count + 1:]
    add_arrivals(where_ref, ids_ref, tiles_ref, blocks, total_ref, **plan)
    far_mate, near_mate, far_own, near_own = sends[:4], sends[4:5], sends[5:7], sends[7:]
    tokens, share = near_own[0].shape[1], near_own[0].shape[0]
    chips = far_own[0].shape[0] + 1

    def copy(pieces, token, d):
        to_chip = lax.rem(where_ref[2] + d, chips)
        block = (2 * to_chip + 1 - where_ref[1]) * share
        for piece in pieces:
            target = piece.at[d - 1] if d > 0 else piece
            for k in range(target.shape[0]):
                target[k] = total_ref[block + k, token:token + tokens, :].astype(BF16)
            block = block + target.shape[0]

    for d in range(1, chips):
        copy(far_mate, tokens, d)
    copy(near_mate, tokens, 0)
    for d in range(1, chips):
        copy(far_own, 0, d)
    copy(near_own, 0, 0)


def chip_kernel(where_ref, total_ref, *rest, token, block):
    pieces, leaving_ref = rest[:-1], rest[-1]
    others, _, tokens, _ = leaving_ref.shape
    chips = others + 1
    for d in range(1, chips):
        to_chip = lax.rem(where_ref[2] + d, chips)
        first = (2 * to_chip + where_ref[1]) * where_ref[5] + block
        done = 0
        for piece in pieces:
            for k in range(piece.shape[1]):
                value = total_ref[first + done, token:token + tokens, :] + piece[d - 1, k].astype(F32)
                leaving_ref[d - 1, done] = value.astype(BF16)
                done += 1


def mate_kernel(where_ref, total_ref, core_ref, *rest, block):
    pieces, out_ref = rest[:-1], rest[-1]
    size, tokens, _ = out_ref.shape
    first = (2 * where_ref[2] + where_ref[1]) * where_ref[5] + block
    for k in range(size):
        value = total_ref[first + k, tokens:, :] + core_ref[block + k].astype(F32)
        for piece in pieces:
            value += piece[k].astype(F32)
        out_ref[k] = value.astype(BF16)


def ordered_sum(own, received, place):
    count = len(received) + 1
    if count == 1:
        return own
    if count == 2:
        return own + received[0]
    total = None
    for member in range(count):
        value = own
        for d, other in enumerate(received, 1):
            value = jnp.where(lax.rem(place + (count - d), count) == member, other, value)
        total = value if total is None else total + value
    return total


CONTRACT_LAST = (((1,), (1,)), ((), ()))


def low_rank_kernel(acts_ref, adapter_a_ref, cot_ref, adapter_ref, labels_ref, out_ref):
    rank = adapter_a_ref.shape[0]
    signs = (1 - 2 * labels_ref[...]).astype(F32)
    out_ref[:rank, :] = lax.dot_general(adapter_a_ref[...], acts_ref[...], CONTRACT_LAST, preferred_element_type=F32)
    out_ref[rank:, :] = signs * lax.dot_general(
        adapter_ref[...], cot_ref[...], CONTRACT_LAST, preferred_element_type=F32
    )


def own_grad_kernel(where_ref, cot_ref, labels_ref, both_ref, *rest):
    received, (rounded_ref, pack_ref) = rest[:-2], rest[-2:]
    feats = cot_ref.shape[1]
    rounded = ordered_sum(both_ref[...], [ref[...] for ref in received], where_ref[2]).astype(BF16)
    rounded_ref[...] = rounded
    rank = rounded.shape[0] // 2
    signs = (1 - 2 * labels_ref[...]).astype(F32)
    signed_low = (rounded[:rank].astype(F32) * signs).astype(BF16)
    grad = jnp.dot(signed_low, cot_ref[...], preferred_element_type=F32)
    pack_ref[:, :feats] = (adapter_scale * grad).astype(BF16)
    pack_ref[:, feats:] = rounded[rank:]


def pair_grad_kernel(
    where_ref, rounded_ref, acts_ref, mate_acts_ref, pack_ref, mate_pack_ref, half_ref, other_ref
):
    rank, shard_rows = rounded_ref.shape[0] // 2, acts_ref.shape[1]
    feats = pack_ref.shape[1] - rounded_ref.shape[1]
    in_half, out_half = shard_rows // 2, feats // 2
    back, mate_back = rounded_ref[rank:, :], mate_pack_ref[:, feats:]

    def fill(bit, out_ref):
        cols = slice(bit * in_half, (bit + 1) * in_half)
        grad = jnp.dot(back, acts_ref[:, cols], preferred_element_type=F32)
        grad = grad + jnp.dot(mate_back, mate_acts_ref[:, cols], preferred_element_type=F32)
        out_ref[:, :in_half] = (adapter_scale * grad).astype(BF16)
        cols = slice(bit * out_half, (bit + 1) * out_half)
        grad = pack_ref[:, cols].astype(F32) + mate_pack_ref[:, cols].astype(F32)
        out_ref[:, in_half:] = grad.astype(BF16)

    for bit in range(2):
        @pl.when(where_ref[3] == bit)
        def _():
            fill(bit, half_ref)
            fill(1 - bit, other_ref)


def grad_sum_kernel(where_ref, half_ref, other_ref, *rest):
    received, (in_ref, out_ref) = rest[:-2], rest[-2:]
    in_half, out_half = in_ref.shape[1] // 2, out_ref.shape[1] // 2
    count = len(received) // 2
    place = where_ref[4]

    def add(bit, own_ref, halves):
        total = ordered_sum(own_ref[...].astype(F32), [ref[...].astype(F32) for ref in halves], place)
        in_ref[:, bit * in_half:(bit + 1) * in_half] = total[:, :in_half]
        out_ref[:, bit * out_half:(bit + 1) * out_half] = total[:, in_half:]

    for bit in range(2):
        @pl.when(where_ref[3] == bit)
        def _():
            add(bit, half_ref, received[:count])
            add(1 - bit, other_ref, received[count:])


def near_kernel(where_ref, rounded_ref, adapter_ref, total_ref, core_ref, *rest):
    from_mate, near_ref = rest[:-1], rest[-1]
    share, tokens, tile = core_ref.shape
    rank = rounded_ref.shape[0] // 2
    low = rounded_ref[:rank, :].astype(F32).T.astype(BF16)
    mine = (2 * where_ref[2] + where_ref[1]) * share
    size = from_mate[0].shape[0]
    for q in range(share):
        piece = from_mate[0][q] if q < size else from_mate[1][q - size]
        value = total_ref[mine + q, :tokens, :] + core_ref[q].astype(F32)
        value += piece.astype(F32)
        extra = jnp.dot(low, adapter_ref[:, q * tile:(q + 1) * tile], preferred_element_type=F32)
        near_ref[q] = value + adapter_scale * extra


def final_kernel(near_ref, *rest):
    pieces, out_ref = rest[:-1], rest[-1]
    share, _, tile = near_ref.shape
    for q in range(share):
        value = near_ref[q]
        for piece in pieces:
            value += piece[q].astype(F32)
        out_ref[:, q * tile:(q + 1) * tile] = value.astype(BF16)


def call(kernel, outs, scalars, arrays, aliases=None):
    smem = pl.BlockSpec(memory_space=pltpu.SMEM)
    vmem = pl.BlockSpec(memory_space=pltpu.VMEM)
    return pl.pallas_call(
        kernel,
        out_shape=outs,
        in_specs=[smem] * len(scalars) + [vmem] * len(arrays),
        out_specs=tuple(vmem for _ in outs),
        input_output_aliases=aliases or {},
        cost_estimate=pl.CostEstimate(flops=0, transcendentals=0, bytes_accessed=0),
        compiler_params=pltpu.CompilerParams(vmem_limit_bytes=4 * 1024 * 1024),
    )(*scalars, *arrays)


def on_chip(value):
    return pltpu.with_memory_space_constraint(value, pltpu.VMEM)


def after(value, *needed):
    return lax.optimization_barrier((value,) + needed)[0]


def make_body(n_parts, n_row, n_dp):
    chips = n_row // 2
    group = n_dp // 2

    def core_swap(value):
        return lax.ppermute(value, "row", [(i, i ^ 1) for i in range(n_row)])

    def chip_shift(value, d):
        pairs = [(2 * a + c, 2 * ((a + d) % chips) + c) for a in range(chips) for c in range(2)]
        return lax.ppermute(value, "row", pairs)

    def mate_swap(value):
        return lax.ppermute(value, "dp", [(i, i ^ 1) for i in range(n_dp)])

    def group_shift(value, d):
        pairs = [(2 * a + h, 2 * ((a + d) % group) + h) for a in range(group) for h in range(2)]
        return lax.ppermute(value, "dp", pairs)

    def part_shift(value, d):
        return lax.ppermute(value, "parts", [(i, (i + d) % n_parts) for i in range(n_parts)])

    def body(activations, cotangent, forget_labels, kept_blocks, block_ids, adapter_a, output_adapter):
        tokens, shard_rows = activations.shape
        rank = adapter_a.shape[1]
        feats = cotangent.shape[1]
        slots, tile = kept_blocks.shape[1], kept_blocks.shape[-1]
        row_blocks = shard_rows // tile
        col_blocks = D // tile
        share = col_blocks // n_row
        part = lax.axis_index("parts")
        row_index = lax.axis_index("row")
        dp_index = lax.axis_index("dp")
        where = jnp.stack([
            part, lax.rem(row_index, 2), lax.div(row_index, 2),
            lax.rem(dp_index, 2), lax.div(dp_index, 2), jnp.int32(share),
        ]).astype(jnp.int32)
        blocks = kept_blocks[0]
        ids = block_ids[0]
        labels = forget_labels[None, :]

        held = slots // n_parts
        sizes = [held * k // 32 for k in (16, 10, 6)]
        starts = [sum(sizes[:k]) for k in range(len(sizes))]
        leaving_chunks = [
            lax.dynamic_slice_in_dim(blocks, part * held + start, size, axis=0)
            for start, size in zip(starts, sizes)
        ]
        known = jnp.maximum(ids, 0)
        code = jnp.stack([
            jnp.where(ids >= 0, lax.div(known, col_blocks), -1),
            jnp.where(ids >= 0, lax.rem(known, col_blocks), 0),
        ]).astype(BF16)
        code = jnp.pad(code, ((0, tile - 2), (0, tile - slots)))[None]
        soon = core_swap(after(ids, leaving_chunks[0]))
        leaving_chunks[1] = jnp.concatenate([leaving_chunks[1], code], axis=0)
        leaving_chunks[1:] = [after(chunk, soon) for chunk in leaving_chunks[1:]]
        direct = [
            (group_shift(leaving_chunks[k], d), (d - 1, 0, starts[k], sizes[k]))
            for d in range(1, group) for k in range(len(starts))
        ]
        mate_activations = mate_swap(activations)

        (both,) = call(
            low_rank_kernel, (jax.ShapeDtypeStruct((2 * rank, tokens), F32),), (),
            (activations, after(adapter_a, soon).T, cotangent, after(output_adapter, soon), labels),
        )
        both = both + core_swap(both)
        rounded, pack = call(
            own_grad_kernel,
            (
                jax.ShapeDtypeStruct((2 * rank, tokens), BF16),
                jax.ShapeDtypeStruct((rank, feats + tokens), BF16),
            ),
            (where,), (cotangent, labels, both) + tuple(chip_shift(both, d) for d in range(1, chips)),
        )
        mate_pack = mate_swap(pack)

        def chunk(items, k):
            return [item for item in items if item[1][2] == starts[k]]

        def plan(items):
            return dict(places=[item[1] for item in items], parts=n_parts, held=held, col_blocks=col_blocks)

        def values(items):
            return tuple(item[0] for item in items)

        total_shape = pltpu.VMEM((col_blocks + 1, 2 * tokens, tile), F32)
        total, tiles = call(
            functools.partial(first_kernel, col_blocks=col_blocks),
            (total_shape, pltpu.VMEM((row_blocks, 2 * tokens, tile), BF16)),
            (after(where, rounded, leaving_chunks[-1]), ids), (activations, mate_activations, blocks),
        )
        half_shape = jax.ShapeDtypeStruct((rank, (shard_rows + feats) // 2), BF16)
        half_grads, other_grads = call(
            pair_grad_kernel, (half_shape, half_shape), (where,), (rounded, activations, mate_activations, pack, mate_pack),
        )
        far_grads = [group_shift(half_grads, d) for d in range(1, group)]

        (all_ids,) = call(
            functools.partial(ids_kernel, col_blocks=col_blocks),
            (jax.ShapeDtypeStruct((group - 1, tile), jnp.int32),), (),
            tuple(value for value, place in direct if place[2] == starts[1]),
        )
        gates = {starts[0]: (rounded, mate_activations), starts[1]: (total,), starts[2]: (half_grads,)}
        swapped = [
            (part_shift(after(value, *gates[start])[:size], e), (source, e, start, size))
            for value, (source, _, start, size) in direct for e in range(1, n_parts)
        ]
        more = direct + chunk(swapped, 0) + chunk(swapped, 1)
        last = chunk(swapped, 2)

        (total,) = call(
            functools.partial(more_kernel, **plan(more)), (total_shape,), (where, all_ids),
            (on_chip(tiles), on_chip(total)) + values(more), {3: 0},
        )
        small = share // 4
        half = share // 2

        def far_piece(size):
            return pltpu.VMEM((chips - 1, size, tokens, tile), BF16)

        def near_piece(size):
            return pltpu.VMEM((size, tokens, tile), BF16)

        total, *sends = call(
            functools.partial(last_kernel, block_count=len(last), **plan(last)),
            (total_shape,) + (far_piece(small),) * 4 + (near_piece(share),)
            + (far_piece(half),) * 2 + (near_piece(share),),
            (after(where, half_grads), all_ids), (on_chip(tiles), on_chip(total)) + values(last), {3: 0},
        )

        cores = [core_swap(value) for value in sends[:5]]

        def for_chips(pieces, token, block, *needed):
            size = sum(piece.shape[1] for piece in pieces)
            (leaving,) = call(
                functools.partial(chip_kernel, token=token, block=block), (far_piece(size),),
                (after(where, *needed) if needed else where,), (on_chip(total),) + tuple(pieces),
            )
            return leaving, [chip_shift(leaving[d - 1], d) for d in range(1, chips)]

        leaving_first, pieces_first = for_chips(cores[:1], tokens, 0)
        leaving_second, pieces_second = for_chips(cores[1:4], tokens, small, leaving_first)
        cores += [core_swap(after(value, leaving_second)) for value in sends[5:]]
        leaving_own, own_pieces = for_chips(cores[5:7], 0, 0)
        far_grads = [after(value, *pieces_first) for value in far_grads]
        mate_grads = [mate_swap(value) for value in far_grads]

        def for_mate(pieces, size, block, *needed):
            (value,) = call(
                functools.partial(mate_kernel, block=block), (near_piece(size),),
                (after(where, *needed) if needed else where,), (on_chip(total), cores[4]) + tuple(pieces),
            )
            return mate_swap(value)

        from_mate_first = for_mate(pieces_first, small, 0)
        from_mate = [
            from_mate_first, for_mate(pieces_second, share - small, small, from_mate_first, *mate_grads),
        ]
        in_grad, out_grad = call(
            grad_sum_kernel,
            (jax.ShapeDtypeStruct((rank, shard_rows), F32), jax.ShapeDtypeStruct((rank, feats), F32)),
            (where,), (half_grads, other_grads) + tuple(far_grads) + tuple(mate_grads),
        )
        (near,) = call(
            near_kernel, (pltpu.VMEM((share, tokens, tile), F32),), (where,),
            (rounded, output_adapter, on_chip(total), cores[7]) + tuple(from_mate),
        )
        (projected,) = call(
            final_kernel, (jax.ShapeDtypeStruct((tokens, feats), BF16),), (), (on_chip(near),) + tuple(own_pieces),
        )
        return projected, in_grad.T, out_grad

    return body


def solution(mesh):
    placed = (
        P(("parts", "dp"), "row"),
        P(("parts", "dp"), "row"),
        P(("parts", "dp")),
        P("row", "dp", None, None),
        P("row", "dp"),
        P("row", None),
        P(None, "row"),
    )
    return jax.shard_map(
        make_body(mesh.shape["parts"], mesh.shape["row"], mesh.shape["dp"]),
        mesh=mesh,
        in_specs=placed,
        out_specs=(P(("parts", "dp"), "row"), P(("parts", "row"), None), P("parts", "row")),
        check_vma=False,
    )
```

```python
import functools

import jax
import jax.numpy as jnp
from jax import lax
from jax.experimental import pallas as pl
from jax.experimental.pallas import tpu as pltpu
from jax.sharding import PartitionSpec as P

D = 8192

adapter_scale = 2.0

F32 = jnp.float32
BF16 = jnp.bfloat16


def add_blocks(total_ref, tiles_ref, blocks_ref, count, ident_at, col_blocks):
    unroll = max(u for u in range(1, 9) if count % u == 0)

    def one(step, carry):
        for u in range(unroll):
            k = step * unroll + u
            ident = ident_at(k)
            known = jnp.maximum(ident, 0)
            row = lax.div(known, col_blocks)
            col = jnp.where(ident >= 0, lax.rem(known, col_blocks), col_blocks)
            total_ref[col] += jnp.dot(tiles_ref[row], blocks_ref[k], preferred_element_type=F32)
        return carry

    lax.fori_loop(0, count // unroll, one, 0)


def add_arrivals(where_ref, ids_ref, tiles_ref, blocks, total_ref, places, parts, held, col_blocks):
    for blocks_ref, (source, shift, start, size) in zip(blocks, places):
        base = lax.rem(where_ref[0] + (parts - shift), parts) * held + start
        add_blocks(
            total_ref, tiles_ref, blocks_ref, size, lambda k: ids_ref[source, base + k], col_blocks
        )


def ids_kernel(*refs, col_blocks):
    coded, ids_ref = refs[:-1], refs[-1]
    for source, ref in enumerate(coded):
        code = ref[ref.shape[0] - 1].astype(F32)
        ids_ref[source:source + 1, :] = (code[0:1, :] * col_blocks + code[1:2, :]).astype(jnp.int32)


def first_kernel(where_ref, ids_ref, own_ref, mate_ref, own_blocks_ref, total_ref, tiles_ref, *, col_blocks):
    row_blocks, _, tile = tiles_ref.shape
    tokens = own_ref.shape[0]
    total_ref[...] = jnp.zeros_like(total_ref)
    for i in range(row_blocks):
        tiles_ref[i, :tokens, :] = own_ref[:, i * tile:(i + 1) * tile]
        tiles_ref[i, tokens:, :] = mate_ref[:, i * tile:(i + 1) * tile]
    add_blocks(
        total_ref, tiles_ref, own_blocks_ref, own_blocks_ref.shape[0], lambda k: ids_ref[k], col_blocks
    )


def more_kernel(where_ref, ids_ref, tiles_ref, old_ref, *rest, **plan):
    add_arrivals(where_ref, ids_ref, tiles_ref, rest[:-1], rest[-1], **plan)


def last_kernel(where_ref, ids_ref, tiles_ref, old_ref, *rest, block_count, **plan):
    blocks, total_ref, sends = rest[:block_count], rest[block_count], rest[block_count + 1:]
    add_arrivals(where_ref, ids_ref, tiles_ref, blocks, total_ref, **plan)
    far_mate, near_mate, far_own, near_own = sends[:4], sends[4:5], sends[5:7], sends[7:]
    tokens, share = near_own[0].shape[1], near_own[0].shape[0]
    chips = far_own[0].shape[0] + 1

    def copy(pieces, token, d):
        to_chip = lax.rem(where_ref[2] + d, chips)
        block = (2 * to_chip + 1 - where_ref[1]) * share
        for piece in pieces:
            target = piece.at[d - 1] if d > 0 else piece
            for k in range(target.shape[0]):
                target[k] = total_ref[block + k, token:token + tokens, :].astype(BF16)
            block = block + target.shape[0]

    for d in range(1, chips):
        copy(far_mate, tokens, d)
    copy(near_mate, tokens, 0)
    for d in range(1, chips):
        copy(far_own, 0, d)
    copy(near_own, 0, 0)


def chip_kernel(where_ref, total_ref, *rest, token, block):
    pieces, leaving_ref = rest[:-1], rest[-1]
    others, _, tokens, _ = leaving_ref.shape
    chips = others + 1
    for d in range(1, chips):
        to_chip = lax.rem(where_ref[2] + d, chips)
        first = (2 * to_chip + where_ref[1]) * where_ref[5] + block
        done = 0
        for piece in pieces:
            for k in range(piece.shape[1]):
                value = total_ref[first + done, token:token + tokens, :] + piece[d - 1, k].astype(F32)
                leaving_ref[d - 1, done] = value.astype(BF16)
                done += 1


def mate_kernel(where_ref, total_ref, core_ref, *rest, block):
    pieces, out_ref = rest[:-1], rest[-1]
    size, tokens, _ = out_ref.shape
    first = (2 * where_ref[2] + where_ref[1]) * where_ref[5] + block
    for k in range(size):
        value = total_ref[first + k, tokens:, :] + core_ref[block + k].astype(F32)
        for piece in pieces:
            value += piece[k].astype(F32)
        out_ref[k] = value.astype(BF16)


def ordered_sum(own, received, place):
    count = len(received) + 1
    if count == 1:
        return own
    if count == 2:
        return own + received[0]
    total = None
    for member in range(count):
        value = own
        for d, other in enumerate(received, 1):
            value = jnp.where(lax.rem(place + (count - d), count) == member, other, value)
        total = value if total is None else total + value
    return total


CONTRACT_LAST = (((1,), (1,)), ((), ()))


def low_rank_kernel(acts_ref, adapter_a_ref, cot_ref, adapter_ref, labels_ref, out_ref):
    rank = adapter_a_ref.shape[0]
    signs = (1 - 2 * labels_ref[...]).astype(F32)
    out_ref[:rank, :] = lax.dot_general(adapter_a_ref[...], acts_ref[...], CONTRACT_LAST, preferred_element_type=F32)
    out_ref[rank:, :] = signs * lax.dot_general(
        adapter_ref[...], cot_ref[...], CONTRACT_LAST, preferred_element_type=F32
    )


def own_grad_kernel(where_ref, cot_ref, labels_ref, both_ref, *rest):
    received, (rounded_ref, pack_ref) = rest[:-2], rest[-2:]
    feats = cot_ref.shape[1]
    rounded = ordered_sum(both_ref[...], [ref[...] for ref in received], where_ref[2]).astype(BF16)
    rounded_ref[...] = rounded
    rank = rounded.shape[0] // 2
    signs = (1 - 2 * labels_ref[...]).astype(F32)
    signed_low = (rounded[:rank].astype(F32) * signs).astype(BF16)
    grad = jnp.dot(signed_low, cot_ref[...], preferred_element_type=F32)
    pack_ref[:, :feats] = (adapter_scale * grad).astype(BF16)
    pack_ref[:, feats:] = rounded[rank:]


def pair_grad_kernel(
    where_ref, rounded_ref, acts_ref, mate_acts_ref, pack_ref, mate_pack_ref, half_ref, other_ref
):
    rank, shard_rows = rounded_ref.shape[0] // 2, acts_ref.shape[1]
    feats = pack_ref.shape[1] - rounded_ref.shape[1]
    in_half, out_half = shard_rows // 2, feats // 2
    back, mate_back = rounded_ref[rank:, :], mate_pack_ref[:, feats:]

    def fill(bit, out_ref):
        cols = slice(bit * in_half, (bit + 1) * in_half)
        grad = jnp.dot(back, acts_ref[:, cols], preferred_element_type=F32)
        grad = grad + jnp.dot(mate_back, mate_acts_ref[:, cols], preferred_element_type=F32)
        out_ref[:, :in_half] = (adapter_scale * grad).astype(BF16)
        cols = slice(bit * out_half, (bit + 1) * out_half)
        grad = pack_ref[:, cols].astype(F32) + mate_pack_ref[:, cols].astype(F32)
        out_ref[:, in_half:] = grad.astype(BF16)

    for bit in range(2):
        @pl.when(where_ref[3] == bit)
        def _():
            fill(bit, half_ref)
            fill(1 - bit, other_ref)


def grad_sum_kernel(where_ref, half_ref, other_ref, *rest):
    received, (in_ref, out_ref) = rest[:-2], rest[-2:]
    in_half, out_half = in_ref.shape[1] // 2, out_ref.shape[1] // 2
    count = len(received) // 2
    place = where_ref[4]

    def add(bit, own_ref, halves):
        total = ordered_sum(own_ref[...].astype(F32), [ref[...].astype(F32) for ref in halves], place)
        in_ref[:, bit * in_half:(bit + 1) * in_half] = total[:, :in_half]
        out_ref[:, bit * out_half:(bit + 1) * out_half] = total[:, in_half:]

    for bit in range(2):
        @pl.when(where_ref[3] == bit)
        def _():
            add(bit, half_ref, received[:count])
            add(1 - bit, other_ref, received[count:])


def near_kernel(where_ref, rounded_ref, adapter_ref, total_ref, core_ref, *rest):
    from_mate, near_ref = rest[:-1], rest[-1]
    share, tokens, tile = core_ref.shape
    rank = rounded_ref.shape[0] // 2
    low = rounded_ref[:rank, :].astype(F32).T.astype(BF16)
    mine = (2 * where_ref[2] + where_ref[1]) * share
    size = from_mate[0].shape[0]
    for q in range(share):
        piece = from_mate[0][q] if q < size else from_mate[1][q - size]
        value = total_ref[mine + q, :tokens, :] + core_ref[q].astype(F32)
        value += piece.astype(F32)
        extra = jnp.dot(low, adapter_ref[:, q * tile:(q + 1) * tile], preferred_element_type=F32)
        near_ref[q] = value + adapter_scale * extra


def final_kernel(near_ref, *rest):
    pieces, out_ref = rest[:-1], rest[-1]
    share, _, tile = near_ref.shape
    for q in range(share):
        value = near_ref[q]
        for piece in pieces:
            value += piece[q].astype(F32)
        out_ref[:, q * tile:(q + 1) * tile] = value.astype(BF16)


def call(kernel, outs, scalars, arrays, aliases=None):
    smem = pl.BlockSpec(memory_space=pltpu.SMEM)
    vmem = pl.BlockSpec(memory_space=pltpu.VMEM)
    return pl.pallas_call(
        kernel,
        out_shape=outs,
        in_specs=[smem] * len(scalars) + [vmem] * len(arrays),
        out_specs=tuple(vmem for _ in outs),
        input_output_aliases=aliases or {},
        cost_estimate=pl.CostEstimate(flops=0, transcendentals=0, bytes_accessed=0),
        compiler_params=pltpu.CompilerParams(vmem_limit_bytes=4 * 1024 * 1024),
    )(*scalars, *arrays)


def on_chip(value):
    return pltpu.with_memory_space_constraint(value, pltpu.VMEM)


def after(value, *needed):
    return lax.optimization_barrier((value,) + needed)[0]


def make_body(n_parts, n_row, n_dp):
    chips = n_row // 2
    group = n_dp // 2

    def core_swap(value):
        return lax.ppermute(value, "row", [(i, i ^ 1) for i in range(n_row)])

    def chip_shift(value, d):
        pairs = [(2 * a + c, 2 * ((a + d) % chips) + c) for a in range(chips) for c in range(2)]
        return lax.ppermute(value, "row", pairs)

    def mate_swap(value):
        return lax.ppermute(value, "dp", [(i, i ^ 1) for i in range(n_dp)])

    def group_shift(value, d):
        pairs = [(2 * a + h, 2 * ((a + d) % group) + h) for a in range(group) for h in range(2)]
        return lax.ppermute(value, "dp", pairs)

    def part_shift(value, d):
        return lax.ppermute(value, "parts", [(i, (i + d) % n_parts) for i in range(n_parts)])

    def body(activations, cotangent, forget_labels, kept_blocks, block_ids, adapter_a, output_adapter):
        tokens, shard_rows = activations.shape
        rank = adapter_a.shape[1]
        feats = cotangent.shape[1]
        slots, tile = kept_blocks.shape[1], kept_blocks.shape[-1]
        row_blocks = shard_rows // tile
        col_blocks = D // tile
        share = col_blocks // n_row
        part = lax.axis_index("parts")
        row_index = lax.axis_index("row")
        dp_index = lax.axis_index("dp")
        where = jnp.stack([
            part, lax.rem(row_index, 2), lax.div(row_index, 2),
            lax.rem(dp_index, 2), lax.div(dp_index, 2), jnp.int32(share),
        ]).astype(jnp.int32)
        blocks = kept_blocks[0]
        ids = block_ids[0]
        labels = forget_labels[None, :]

        held = slots // n_parts
        sizes = [held * k // 32 for k in (16, 10, 6)]
        starts = [sum(sizes[:k]) for k in range(len(sizes))]
        leaving_chunks = [
            lax.dynamic_slice_in_dim(blocks, part * held + start, size, axis=0)
            for start, size in zip(starts, sizes)
        ]
        known = jnp.maximum(ids, 0)
        code = jnp.stack([
            jnp.where(ids >= 0, lax.div(known, col_blocks), -1),
            jnp.where(ids >= 0, lax.rem(known, col_blocks), 0),
        ]).astype(BF16)
        code = jnp.pad(code, ((0, tile - 2), (0, tile - slots)))[None]
        soon = core_swap(ids)
        leaving_chunks[1] = jnp.concatenate([leaving_chunks[1], code], axis=0)
        leaving_chunks = [after(chunk, soon) for chunk in leaving_chunks]
        direct = [
            (group_shift(leaving_chunks[k], d), (d - 1, 0, starts[k], sizes[k]))
            for d in range(1, group) for k in range(len(starts))
        ]
        mate_activations = mate_swap(activations)

        (both,) = call(
            low_rank_kernel, (jax.ShapeDtypeStruct((2 * rank, tokens), F32),), (),
            (activations, after(adapter_a, soon).T, cotangent, after(output_adapter, soon), labels),
        )
        both = both + core_swap(both)
        rounded, pack = call(
            own_grad_kernel,
            (
                jax.ShapeDtypeStruct((2 * rank, tokens), BF16),
                jax.ShapeDtypeStruct((rank, feats + tokens), BF16),
            ),
            (where,), (cotangent, labels, both) + tuple(chip_shift(both, d) for d in range(1, chips)),
        )
        mate_pack = mate_swap(pack)

        def chunk(items, k):
            return [item for item in items if item[1][2] == starts[k]]

        def plan(items):
            return dict(places=[item[1] for item in items], parts=n_parts, held=held, col_blocks=col_blocks)

        def values(items):
            return tuple(item[0] for item in items)

        total_shape = pltpu.VMEM((col_blocks + 1, 2 * tokens, tile), F32)
        total, tiles = call(
            functools.partial(first_kernel, col_blocks=col_blocks),
            (total_shape, pltpu.VMEM((row_blocks, 2 * tokens, tile), BF16)),
            (after(where, rounded, leaving_chunks[-1]), ids), (activations, mate_activations, blocks),
        )
        half_shape = jax.ShapeDtypeStruct((rank, (shard_rows + feats) // 2), BF16)
        half_grads, other_grads = call(
            pair_grad_kernel, (half_shape, half_shape), (where,), (rounded, activations, mate_activations, pack, mate_pack),
        )
        far_grads = [group_shift(half_grads, d) for d in range(1, group)]

        (all_ids,) = call(
            functools.partial(ids_kernel, col_blocks=col_blocks),
            (jax.ShapeDtypeStruct((group - 1, tile), jnp.int32),), (),
            tuple(value for value, place in direct if place[2] == starts[1]),
        )
        gates = {starts[0]: (rounded,), starts[1]: (total,), starts[2]: (half_grads,)}
        swapped = [
            (part_shift(after(value, *gates[start])[:size], e), (source, e, start, size))
            for value, (source, _, start, size) in direct for e in range(1, n_parts)
        ]
        more = direct + chunk(swapped, 0) + chunk(swapped, 1)
        last = chunk(swapped, 2)

        (total,) = call(
            functools.partial(more_kernel, **plan(more)), (total_shape,), (where, all_ids),
            (on_chip(tiles), on_chip(total)) + values(more), {3: 0},
        )
        small = share // 4
        half = share // 2

        def far_piece(size):
            return pltpu.VMEM((chips - 1, size, tokens, tile), BF16)

        def near_piece(size):
            return pltpu.VMEM((size, tokens, tile), BF16)

        total, *sends = call(
            functools.partial(last_kernel, block_count=len(last), **plan(last)),
            (total_shape,) + (far_piece(small),) * 4 + (near_piece(share),)
            + (far_piece(half),) * 2 + (near_piece(share),),
            (after(where, half_grads), all_ids), (on_chip(tiles), on_chip(total)) + values(last), {3: 0},
        )

        cores = [core_swap(value) for value in sends[:5]]

        def for_chips(pieces, token, block, *needed):
            size = sum(piece.shape[1] for piece in pieces)
            (leaving,) = call(
                functools.partial(chip_kernel, token=token, block=block), (far_piece(size),),
                (after(where, *needed) if needed else where,), (on_chip(total),) + tuple(pieces),
            )
            return leaving, [chip_shift(leaving[d - 1], d) for d in range(1, chips)]

        leaving_first, pieces_first = for_chips(cores[:1], tokens, 0)
        leaving_second, pieces_second = for_chips(cores[1:4], tokens, small, leaving_first)
        cores += [core_swap(after(value, leaving_second)) for value in sends[5:]]
        leaving_own, own_pieces = for_chips(cores[5:7], 0, 0)
        far_grads = [after(value, *pieces_first) for value in far_grads]
        mate_grads = [mate_swap(value) for value in far_grads]

        def for_mate(pieces, size, block, *needed):
            (value,) = call(
                functools.partial(mate_kernel, block=block), (near_piece(size),),
                (after(where, *needed) if needed else where,), (on_chip(total), cores[4]) + tuple(pieces),
            )
            return mate_swap(value)

        from_mate_first = for_mate(pieces_first, small, 0)
        from_mate = [
            from_mate_first, for_mate(pieces_second, share - small, small, from_mate_first, *mate_grads),
        ]
        in_grad, out_grad = call(
            grad_sum_kernel,
            (jax.ShapeDtypeStruct((rank, shard_rows), F32), jax.ShapeDtypeStruct((rank, feats), F32)),
            (where,), (half_grads, other_grads) + tuple(far_grads) + tuple(mate_grads),
        )
        (near,) = call(
            near_kernel, (pltpu.VMEM((share, tokens, tile), F32),), (where,),
            (rounded, output_adapter, on_chip(total), cores[7]) + tuple(from_mate),
        )
        (projected,) = call(
            final_kernel, (jax.ShapeDtypeStruct((tokens, feats), BF16),), (), (on_chip(near),) + tuple(own_pieces),
        )
        return projected, in_grad.T, out_grad

    return body


def solution(mesh):
    placed = (
        P(("parts", "dp"), "row"),
        P(("parts", "dp"), "row"),
        P(("parts", "dp")),
        P("row", "dp", None, None),
        P("row", "dp"),
        P("row", None),
        P(None, "row"),
    )
    return jax.shard_map(
        make_body(mesh.shape["parts"], mesh.shape["row"], mesh.shape["dp"]),
        mesh=mesh,
        in_specs=placed,
        out_specs=(P(("parts", "dp"), "row"), P(("parts", "row"), None), P("parts", "row")),
        check_vma=False,
    )
```

```python
import functools

import jax
import jax.numpy as jnp
from jax import lax
from jax.experimental import pallas as pl
from jax.experimental.pallas import tpu as pltpu
from jax.sharding import PartitionSpec as P

D = 8192

adapter_scale = 2.0

F32 = jnp.float32
BF16 = jnp.bfloat16


def add_blocks(total_ref, tiles_ref, blocks_ref, count, ident_at, col_blocks):
    unroll = max(u for u in range(1, 9) if count % u == 0)

    def one(step, carry):
        for u in range(unroll):
            k = step * unroll + u
            ident = ident_at(k)
            known = jnp.maximum(ident, 0)
            row = lax.div(known, col_blocks)
            col = jnp.where(ident >= 0, lax.rem(known, col_blocks), col_blocks)
            total_ref[col] += jnp.dot(tiles_ref[row], blocks_ref[k], preferred_element_type=F32)
        return carry

    lax.fori_loop(0, count // unroll, one, 0)


def add_arrivals(where_ref, ids_ref, tiles_ref, blocks, total_ref, places, parts, held, col_blocks):
    for blocks_ref, (source, shift, start, size) in zip(blocks, places):
        base = lax.rem(where_ref[0] + (parts - shift), parts) * held + start
        add_blocks(
            total_ref, tiles_ref, blocks_ref, size, lambda k: ids_ref[source, base + k], col_blocks
        )


def ids_kernel(*refs, col_blocks):
    coded, ids_ref = refs[:-1], refs[-1]
    for source, ref in enumerate(coded):
        code = ref[ref.shape[0] - 1].astype(F32)
        ids_ref[source:source + 1, :] = (code[0:1, :] * col_blocks + code[1:2, :]).astype(jnp.int32)


def first_kernel(where_ref, ids_ref, own_ref, mate_ref, own_blocks_ref, total_ref, tiles_ref, *, col_blocks):
    row_blocks, _, tile = tiles_ref.shape
    tokens = own_ref.shape[0]
    total_ref[...] = jnp.zeros_like(total_ref)
    for i in range(row_blocks):
        tiles_ref[i, :tokens, :] = own_ref[:, i * tile:(i + 1) * tile]
        tiles_ref[i, tokens:, :] = mate_ref[:, i * tile:(i + 1) * tile]
    add_blocks(
        total_ref, tiles_ref, own_blocks_ref, own_blocks_ref.shape[0], lambda k: ids_ref[k], col_blocks
    )


def more_kernel(where_ref, ids_ref, tiles_ref, old_ref, *rest, **plan):
    add_arrivals(where_ref, ids_ref, tiles_ref, rest[:-1], rest[-1], **plan)


def last_kernel(where_ref, ids_ref, tiles_ref, old_ref, *rest, block_count, **plan):
    blocks, total_ref, sends = rest[:block_count], rest[block_count], rest[block_count + 1:]
    add_arrivals(where_ref, ids_ref, tiles_ref, blocks, total_ref, **plan)
    far_mate, near_mate, far_own, near_own = sends[:4], sends[4:6], sends[6:8], sends[8:]
    tokens, share = near_own[0].shape[1], near_own[0].shape[0]
    chips = far_own[0].shape[0] + 1

    def copy(pieces, token, d):
        to_chip = lax.rem(where_ref[2] + d, chips)
        block = (2 * to_chip + 1 - where_ref[1]) * share
        for piece in pieces:
            target = piece.at[d - 1] if d > 0 else piece
            for k in range(target.shape[0]):
                target[k] = total_ref[block + k, token:token + tokens, :].astype(BF16)
            block = block + target.shape[0]

    for d in range(1, chips):
        copy(far_mate, tokens, d)
    copy(near_mate, tokens, 0)
    for d in range(1, chips):
        copy(far_own, 0, d)
    copy(near_own, 0, 0)


def chip_kernel(where_ref, total_ref, *rest, token, block):
    pieces, leaving_ref = rest[:-1], rest[-1]
    others, _, tokens, _ = leaving_ref.shape
    chips = others + 1
    for d in range(1, chips):
        to_chip = lax.rem(where_ref[2] + d, chips)
        first = (2 * to_chip + where_ref[1]) * where_ref[5] + block
        done = 0
        for piece in pieces:
            for k in range(piece.shape[1]):
                value = total_ref[first + done, token:token + tokens, :] + piece[d - 1, k].astype(F32)
                leaving_ref[d - 1, done] = value.astype(BF16)
                done += 1


def mate_kernel(where_ref, total_ref, core_ref, *rest, block):
    pieces, out_ref = rest[:-1], rest[-1]
    size, tokens, _ = out_ref.shape
    first = (2 * where_ref[2] + where_ref[1]) * where_ref[5] + block
    for k in range(size):
        value = total_ref[first + k, tokens:, :] + core_ref[k].astype(F32)
        for piece in pieces:
            value += piece[k].astype(F32)
        out_ref[k] = value.astype(BF16)


def ordered_sum(own, received, place):
    count = len(received) + 1
    if count == 1:
        return own
    if count == 2:
        return own + received[0]
    total = None
    for member in range(count):
        value = own
        for d, other in enumerate(received, 1):
            value = jnp.where(lax.rem(place + (count - d), count) == member, other, value)
        total = value if total is None else total + value
    return total


CONTRACT_LAST = (((1,), (1,)), ((), ()))


def low_rank_kernel(acts_ref, adapter_a_ref, cot_ref, adapter_ref, labels_ref, out_ref):
    rank = adapter_a_ref.shape[0]
    signs = (1 - 2 * labels_ref[...]).astype(F32)
    out_ref[:rank, :] = lax.dot_general(adapter_a_ref[...], acts_ref[...], CONTRACT_LAST, preferred_element_type=F32)
    out_ref[rank:, :] = signs * lax.dot_general(
        adapter_ref[...], cot_ref[...], CONTRACT_LAST, preferred_element_type=F32
    )


def own_grad_kernel(where_ref, cot_ref, labels_ref, both_ref, *rest):
    received, (rounded_ref, pack_ref) = rest[:-2], rest[-2:]
    feats = cot_ref.shape[1]
    rounded = ordered_sum(both_ref[...], [ref[...] for ref in received], where_ref[2]).astype(BF16)
    rounded_ref[...] = rounded
    rank = rounded.shape[0] // 2
    signs = (1 - 2 * labels_ref[...]).astype(F32)
    signed_low = (rounded[:rank].astype(F32) * signs).astype(BF16)
    grad = jnp.dot(signed_low, cot_ref[...], preferred_element_type=F32)
    pack_ref[:, :feats] = (adapter_scale * grad).astype(BF16)
    pack_ref[:, feats:] = rounded[rank:]


def pair_grad_kernel(
    where_ref, rounded_ref, acts_ref, mate_acts_ref, pack_ref, mate_pack_ref, half_ref, other_ref
):
    rank, shard_rows = rounded_ref.shape[0] // 2, acts_ref.shape[1]
    feats = pack_ref.shape[1] - rounded_ref.shape[1]
    in_half, out_half = shard_rows // 2, feats // 2
    back, mate_back = rounded_ref[rank:, :], mate_pack_ref[:, feats:]

    def fill(bit, out_ref):
        cols = slice(bit * in_half, (bit + 1) * in_half)
        grad = jnp.dot(back, acts_ref[:, cols], preferred_element_type=F32)
        grad = grad + jnp.dot(mate_back, mate_acts_ref[:, cols], preferred_element_type=F32)
        out_ref[:, :in_half] = (adapter_scale * grad).astype(BF16)
        cols = slice(bit * out_half, (bit + 1) * out_half)
        grad = pack_ref[:, cols].astype(F32) + mate_pack_ref[:, cols].astype(F32)
        out_ref[:, in_half:] = grad.astype(BF16)

    for bit in range(2):
        @pl.when(where_ref[3] == bit)
        def _():
            fill(bit, half_ref)
            fill(1 - bit, other_ref)


def grad_sum_kernel(where_ref, half_ref, other_ref, *rest):
    received, (in_ref, out_ref) = rest[:-2], rest[-2:]
    in_half, out_half = in_ref.shape[1] // 2, out_ref.shape[1] // 2
    count = len(received) // 2
    place = where_ref[4]

    def add(bit, own_ref, halves):
        total = ordered_sum(own_ref[...].astype(F32), [ref[...].astype(F32) for ref in halves], place)
        in_ref[:, bit * in_half:(bit + 1) * in_half] = total[:, :in_half]
        out_ref[:, bit * out_half:(bit + 1) * out_half] = total[:, in_half:]

    for bit in range(2):
        @pl.when(where_ref[3] == bit)
        def _():
            add(bit, half_ref, received[:count])
            add(1 - bit, other_ref, received[count:])


def near_kernel(where_ref, rounded_ref, adapter_ref, total_ref, core_ref, *rest):
    from_mate, near_ref = rest[:-1], rest[-1]
    share, tokens, tile = core_ref.shape
    rank = rounded_ref.shape[0] // 2
    low = rounded_ref[:rank, :].astype(F32).T.astype(BF16)
    mine = (2 * where_ref[2] + where_ref[1]) * share
    size = from_mate[0].shape[0]
    for q in range(share):
        piece = from_mate[0][q] if q < size else from_mate[1][q - size]
        value = total_ref[mine + q, :tokens, :] + core_ref[q].astype(F32)
        value += piece.astype(F32)
        extra = jnp.dot(low, adapter_ref[:, q * tile:(q + 1) * tile], preferred_element_type=F32)
        near_ref[q] = value + adapter_scale * extra


def final_kernel(near_ref, *rest):
    pieces, out_ref = rest[:-1], rest[-1]
    share, _, tile = near_ref.shape
    for q in range(share):
        value = near_ref[q]
        for piece in pieces:
            value += piece[q].astype(F32)
        out_ref[:, q * tile:(q + 1) * tile] = value.astype(BF16)


def call(kernel, outs, scalars, arrays, aliases=None):
    smem = pl.BlockSpec(memory_space=pltpu.SMEM)
    vmem = pl.BlockSpec(memory_space=pltpu.VMEM)
    return pl.pallas_call(
        kernel,
        out_shape=outs,
        in_specs=[smem] * len(scalars) + [vmem] * len(arrays),
        out_specs=tuple(vmem for _ in outs),
        input_output_aliases=aliases or {},
        cost_estimate=pl.CostEstimate(flops=0, transcendentals=0, bytes_accessed=0),
        compiler_params=pltpu.CompilerParams(vmem_limit_bytes=4 * 1024 * 1024),
    )(*scalars, *arrays)


def on_chip(value):
    return pltpu.with_memory_space_constraint(value, pltpu.VMEM)


def after(value, *needed):
    return lax.optimization_barrier((value,) + needed)[0]


def make_body(n_parts, n_row, n_dp):
    chips = n_row // 2
    group = n_dp // 2

    def core_swap(value):
        return lax.ppermute(value, "row", [(i, i ^ 1) for i in range(n_row)])

    def chip_shift(value, d):
        pairs = [(2 * a + c, 2 * ((a + d) % chips) + c) for a in range(chips) for c in range(2)]
        return lax.ppermute(value, "row", pairs)

    def mate_swap(value):
        return lax.ppermute(value, "dp", [(i, i ^ 1) for i in range(n_dp)])

    def group_shift(value, d):
        pairs = [(2 * a + h, 2 * ((a + d) % group) + h) for a in range(group) for h in range(2)]
        return lax.ppermute(value, "dp", pairs)

    def part_shift(value, d):
        return lax.ppermute(value, "parts", [(i, (i + d) % n_parts) for i in range(n_parts)])

    def body(activations, cotangent, forget_labels, kept_blocks, block_ids, adapter_a, output_adapter):
        tokens, shard_rows = activations.shape
        rank = adapter_a.shape[1]
        feats = cotangent.shape[1]
        slots, tile = kept_blocks.shape[1], kept_blocks.shape[-1]
        row_blocks = shard_rows // tile
        col_blocks = D // tile
        share = col_blocks // n_row
        part = lax.axis_index("parts")
        row_index = lax.axis_index("row")
        dp_index = lax.axis_index("dp")
        where = jnp.stack([
            part, lax.rem(row_index, 2), lax.div(row_index, 2),
            lax.rem(dp_index, 2), lax.div(dp_index, 2), jnp.int32(share),
        ]).astype(jnp.int32)
        blocks = kept_blocks[0]
        ids = block_ids[0]
        labels = forget_labels[None, :]

        held = slots // n_parts
        sizes = [held * k // 32 for k in (16, 10, 6)]
        starts = [sum(sizes[:k]) for k in range(len(sizes))]
        leaving_chunks = [
            lax.dynamic_slice_in_dim(blocks, part * held + start, size, axis=0)
            for start, size in zip(starts, sizes)
        ]
        known = jnp.maximum(ids, 0)
        code = jnp.stack([
            jnp.where(ids >= 0, lax.div(known, col_blocks), -1),
            jnp.where(ids >= 0, lax.rem(known, col_blocks), 0),
        ]).astype(BF16)
        code = jnp.pad(code, ((0, tile - 2), (0, tile - slots)))[None]
        soon = core_swap(ids)
        leaving_chunks[1] = jnp.concatenate([leaving_chunks[1], code], axis=0)
        leaving_chunks = [after(chunk, soon) for chunk in leaving_chunks]
        direct = [
            (group_shift(leaving_chunks[k], d), (d - 1, 0, starts[k], sizes[k]))
            for d in range(1, group) for k in range(len(starts))
        ]
        mate_activations = mate_swap(activations)

        (both,) = call(
            low_rank_kernel, (jax.ShapeDtypeStruct((2 * rank, tokens), F32),), (),
            (activations, after(adapter_a, soon).T, cotangent, after(output_adapter, soon), labels),
        )
        both = both + core_swap(both)
        rounded, pack = call(
            own_grad_kernel,
            (
                jax.ShapeDtypeStruct((2 * rank, tokens), BF16),
                jax.ShapeDtypeStruct((rank, feats + tokens), BF16),
            ),
            (where,), (cotangent, labels, both) + tuple(chip_shift(both, d) for d in range(1, chips)),
        )
        mate_pack = mate_swap(pack)

        def chunk(items, k):
            return [item for item in items if item[1][2] == starts[k]]

        def plan(items):
            return dict(places=[item[1] for item in items], parts=n_parts, held=held, col_blocks=col_blocks)

        def values(items):
            return tuple(item[0] for item in items)

        total_shape = pltpu.VMEM((col_blocks + 1, 2 * tokens, tile), F32)
        total, tiles = call(
            functools.partial(first_kernel, col_blocks=col_blocks),
            (total_shape, pltpu.VMEM((row_blocks, 2 * tokens, tile), BF16)),
            (after(where, rounded, leaving_chunks[-1]), ids), (activations, mate_activations, blocks),
        )
        half_shape = jax.ShapeDtypeStruct((rank, (shard_rows + feats) // 2), BF16)
        half_grads, other_grads = call(
            pair_grad_kernel, (half_shape, half_shape), (where,), (rounded, activations, mate_activations, pack, mate_pack),
        )
        far_grads = [group_shift(half_grads, d) for d in range(1, group)]

        (all_ids,) = call(
            functools.partial(ids_kernel, col_blocks=col_blocks),
            (jax.ShapeDtypeStruct((group - 1, tile), jnp.int32),), (),
            tuple(value for value, place in direct if place[2] == starts[1]),
        )
        gates = {starts[0]: (rounded,), starts[1]: (total,), starts[2]: (half_grads,)}
        swapped = [
            (part_shift(after(value, *gates[start])[:size], e), (source, e, start, size))
            for value, (source, _, start, size) in direct for e in range(1, n_parts)
        ]
        more = direct + chunk(swapped, 0) + chunk(swapped, 1)
        last = chunk(swapped, 2)

        (total,) = call(
            functools.partial(more_kernel, **plan(more)), (total_shape,), (where, all_ids),
            (on_chip(tiles), on_chip(total)) + values(more), {3: 0},
        )
        small = max(1, 2 * share // 16)
        rest = share - small
        thirds = (rest - 2 * (rest // 3), rest // 3, rest // 3)
        half = share // 2

        def far_piece(size):
            return pltpu.VMEM((chips - 1, size, tokens, tile), BF16)

        def near_piece(size):
            return pltpu.VMEM((size, tokens, tile), BF16)

        total, *sends = call(
            functools.partial(last_kernel, block_count=len(last), **plan(last)),
            (total_shape, far_piece(small)) + tuple(far_piece(size) for size in thirds)
            + (near_piece(small), near_piece(rest))
            + (far_piece(half),) * 2 + (near_piece(share),),
            (after(where, half_grads), all_ids), (on_chip(tiles), on_chip(total)) + values(last), {3: 0},
        )

        cores = [core_swap(value) for value in sends[:6]]

        def for_chips(pieces, token, block, *needed):
            size = sum(piece.shape[1] for piece in pieces)
            (leaving,) = call(
                functools.partial(chip_kernel, token=token, block=block), (far_piece(size),),
                (after(where, *needed) if needed else where,), (on_chip(total),) + tuple(pieces),
            )
            return leaving, [chip_shift(leaving[d - 1], d) for d in range(1, chips)]

        leaving_first, pieces_first = for_chips(cores[:1], tokens, 0)
        leaving_second, pieces_second = for_chips(cores[1:4], tokens, small, leaving_first)
        cores += [core_swap(after(value, leaving_second)) for value in sends[6:]]
        leaving_own, own_pieces = for_chips(cores[6:8], 0, 0)
        def for_mate(core_got, pieces, block, *needed):
            (value,) = call(
                functools.partial(mate_kernel, block=block), (near_piece(core_got.shape[0]),),
                (after(where, *needed) if needed else where,), (on_chip(total), core_got) + tuple(pieces),
            )
            return mate_swap(value)

        from_mate_first = for_mate(cores[4], pieces_first, 0)
        far_grads = [after(value, from_mate_first) for value in far_grads]
        mate_grads = [mate_swap(value) for value in far_grads]
        from_mate = [
            from_mate_first, for_mate(cores[5], pieces_second, small, *mate_grads),
        ]
        in_grad, out_grad = call(
            grad_sum_kernel,
            (jax.ShapeDtypeStruct((rank, shard_rows), F32), jax.ShapeDtypeStruct((rank, feats), F32)),
            (where,), (half_grads, other_grads) + tuple(far_grads) + tuple(mate_grads),
        )
        (near,) = call(
            near_kernel, (pltpu.VMEM((share, tokens, tile), F32),), (where,),
            (rounded, output_adapter, on_chip(total), cores[8]) + tuple(from_mate),
        )
        (projected,) = call(
            final_kernel, (jax.ShapeDtypeStruct((tokens, feats), BF16),), (), (on_chip(near),) + tuple(own_pieces),
        )
        return projected, in_grad.T, out_grad

    return body


def solution(mesh):
    placed = (
        P(("parts", "dp"), "row"),
        P(("parts", "dp"), "row"),
        P(("parts", "dp")),
        P("row", "dp", None, None),
        P("row", "dp"),
        P("row", None),
        P(None, "row"),
    )
    return jax.shard_map(
        make_body(mesh.shape["parts"], mesh.shape["row"], mesh.shape["dp"]),
        mesh=mesh,
        in_specs=placed,
        out_specs=(P(("parts", "dp"), "row"), P(("parts", "row"), None), P("parts", "row")),
        check_vma=False,
    )
```

```python
import functools

import jax
import jax.numpy as jnp
from jax import lax
from jax.experimental import pallas as pl
from jax.experimental.pallas import tpu as pltpu
from jax.sharding import PartitionSpec as P

D = 8192

adapter_scale = 2.0

F32 = jnp.float32
BF16 = jnp.bfloat16


def add_blocks(total_ref, tiles_ref, blocks_ref, count, ident_at, col_blocks):
    unroll = max(u for u in range(1, 9) if count % u == 0)

    def one(step, carry):
        for u in range(unroll):
            k = step * unroll + u
            ident = ident_at(k)
            known = jnp.maximum(ident, 0)
            row = lax.div(known, col_blocks)
            col = jnp.where(ident >= 0, lax.rem(known, col_blocks), col_blocks)
            total_ref[col] += jnp.dot(tiles_ref[row], blocks_ref[k], preferred_element_type=F32)
        return carry

    lax.fori_loop(0, count // unroll, one, 0)


def add_arrivals(where_ref, ids_ref, tiles_ref, blocks, total_ref, places, parts, held, col_blocks):
    for blocks_ref, (source, shift, start, size) in zip(blocks, places):
        base = lax.rem(where_ref[0] + (parts - shift), parts) * held + start
        add_blocks(
            total_ref, tiles_ref, blocks_ref, size, lambda k: ids_ref[source, base + k], col_blocks
        )


def ids_kernel(*refs, col_blocks):
    coded, ids_ref = refs[:-1], refs[-1]
    for source, ref in enumerate(coded):
        code = ref[ref.shape[0] - 1].astype(F32)
        ids_ref[source:source + 1, :] = (code[0:1, :] * col_blocks + code[1:2, :]).astype(jnp.int32)


def first_kernel(where_ref, ids_ref, own_ref, mate_ref, own_blocks_ref, total_ref, tiles_ref, *, col_blocks):
    row_blocks, _, tile = tiles_ref.shape
    tokens = own_ref.shape[0]
    total_ref[...] = jnp.zeros_like(total_ref)
    for i in range(row_blocks):
        tiles_ref[i, :tokens, :] = own_ref[:, i * tile:(i + 1) * tile]
        tiles_ref[i, tokens:, :] = mate_ref[:, i * tile:(i + 1) * tile]
    add_blocks(
        total_ref, tiles_ref, own_blocks_ref, own_blocks_ref.shape[0], lambda k: ids_ref[k], col_blocks
    )


def more_kernel(where_ref, ids_ref, tiles_ref, old_ref, *rest, **plan):
    add_arrivals(where_ref, ids_ref, tiles_ref, rest[:-1], rest[-1], **plan)


def last_kernel(where_ref, ids_ref, tiles_ref, old_ref, *rest, block_count, **plan):
    blocks, total_ref, sends = rest[:block_count], rest[block_count], rest[block_count + 1:]
    add_arrivals(where_ref, ids_ref, tiles_ref, blocks, total_ref, **plan)
    far_mate, near_mate, far_own, near_own = sends[:4], sends[4:5], sends[5:7], sends[7:]
    tokens, share = near_own[0].shape[1], near_own[0].shape[0]
    chips = far_own[0].shape[0] + 1

    def copy(pieces, token, d):
        to_chip = lax.rem(where_ref[2] + d, chips)
        block = (2 * to_chip + 1 - where_ref[1]) * share
        for piece in pieces:
            target = piece.at[d - 1] if d > 0 else piece
            for k in range(target.shape[0]):
                target[k] = total_ref[block + k, token:token + tokens, :].astype(BF16)
            block = block + target.shape[0]

    for d in range(1, chips):
        copy(far_mate, tokens, d)
    copy(near_mate, tokens, 0)
    for d in range(1, chips):
        copy(far_own, 0, d)
    copy(near_own, 0, 0)


def chip_kernel(where_ref, total_ref, *rest, token, block):
    pieces, leaving_ref = rest[:-1], rest[-1]
    others, _, tokens, _ = leaving_ref.shape
    chips = others + 1
    for d in range(1, chips):
        to_chip = lax.rem(where_ref[2] + d, chips)
        first = (2 * to_chip + where_ref[1]) * where_ref[5] + block
        done = 0
        for piece in pieces:
            for k in range(piece.shape[1]):
                value = total_ref[first + done, token:token + tokens, :] + piece[d - 1, k].astype(F32)
                leaving_ref[d - 1, done] = value.astype(BF16)
                done += 1


def mate_kernel(where_ref, total_ref, core_ref, *rest, block):
    pieces, out_ref = rest[:-1], rest[-1]
    size, tokens, _ = out_ref.shape
    first = (2 * where_ref[2] + where_ref[1]) * where_ref[5] + block
    for k in range(size):
        value = total_ref[first + k, tokens:, :] + core_ref[block + k].astype(F32)
        for piece in pieces:
            value += piece[k].astype(F32)
        out_ref[k] = value.astype(BF16)


def ordered_sum(own, received, place):
    count = len(received) + 1
    if count == 1:
        return own
    if count == 2:
        return own + received[0]
    total = None
    for member in range(count):
        value = own
        for d, other in enumerate(received, 1):
            value = jnp.where(lax.rem(place + (count - d), count) == member, other, value)
        total = value if total is None else total + value
    return total


CONTRACT_LAST = (((1,), (1,)), ((), ()))


def low_rank_kernel(acts_ref, adapter_a_ref, cot_ref, adapter_ref, labels_ref, out_ref):
    rank = adapter_a_ref.shape[0]
    signs = (1 - 2 * labels_ref[...]).astype(F32)
    out_ref[:rank, :] = lax.dot_general(adapter_a_ref[...], acts_ref[...], CONTRACT_LAST, preferred_element_type=F32)
    out_ref[rank:, :] = signs * lax.dot_general(
        adapter_ref[...], cot_ref[...], CONTRACT_LAST, preferred_element_type=F32
    )


def own_grad_kernel(where_ref, cot_ref, labels_ref, both_ref, *rest):
    received, (rounded_ref, kept_ref, pack_ref) = rest[:-3], rest[-3:]
    half = kept_ref.shape[1]
    rounded = ordered_sum(both_ref[...], [ref[...] for ref in received], where_ref[2]).astype(BF16)
    rounded_ref[...] = rounded
    rank = rounded.shape[0] // 2
    signs = (1 - 2 * labels_ref[...]).astype(F32)
    signed_low = (rounded[:rank].astype(F32) * signs).astype(BF16)

    def grad(bit):
        cols = cot_ref[:, bit * half:(bit + 1) * half]
        return adapter_scale * jnp.dot(signed_low, cols, preferred_element_type=F32)

    for bit in range(2):
        @pl.when(where_ref[3] == bit)
        def _():
            kept_ref[...] = grad(bit)
            pack_ref[:, :half] = grad(1 - bit).astype(BF16)
    pack_ref[:, half:] = rounded[rank:]


def pair_grad_kernel(
    where_ref, rounded_ref, acts_ref, mate_acts_ref, kept_ref, mate_pack_ref, half_ref, other_ref
):
    rank, in_half, out_half = rounded_ref.shape[0] // 2, other_ref.shape[1], kept_ref.shape[1]
    back, mate_back = rounded_ref[rank:, :], mate_pack_ref[:, out_half:]

    def grad(bit):
        cols = slice(bit * in_half, (bit + 1) * in_half)
        own = jnp.dot(back, acts_ref[:, cols], preferred_element_type=F32)
        mate = jnp.dot(mate_back, mate_acts_ref[:, cols], preferred_element_type=F32)
        return (adapter_scale * (own + mate)).astype(BF16)

    for bit in range(2):
        @pl.when(where_ref[3] == bit)
        def _():
            half_ref[:, :in_half] = grad(bit)
            other_ref[...] = grad(1 - bit)
    half_ref[:, in_half:] = (kept_ref[...] + mate_pack_ref[:, :out_half].astype(F32)).astype(BF16)


def forward_kernel(where_ref, half_ref, *rest, in_half):
    count = len(rest) // 2
    received, outs = rest[:count], rest[count:]
    for ref, out_ref in zip(received, outs):
        out_ref[:, :in_half] = ref[:, :in_half]
    total = ordered_sum(
        half_ref[:, in_half:].astype(F32), [ref[:, in_half:].astype(F32) for ref in received], where_ref[4]
    )
    outs[0][:, in_half:] = total.astype(BF16)


def grad_sum_kernel(where_ref, half_ref, other_ref, *rest):
    received, (in_ref, out_ref) = rest[:-2], rest[-2:]
    in_half, out_half = in_ref.shape[1] // 2, out_ref.shape[1] // 2
    count = len(received) // 3
    far, sent, passed = received[:count], received[count:2 * count], received[2 * count:]

    def total(own, halves):
        return ordered_sum(own.astype(F32), [ref[:, :in_half].astype(F32) for ref in halves], where_ref[4])

    for bit in range(2):
        @pl.when(where_ref[3] == bit)
        def _():
            mine, others = slice(bit * in_half, (bit + 1) * in_half), slice((1 - bit) * in_half, (2 - bit) * in_half)
            in_ref[:, mine] = total(half_ref[:, :in_half], far)
            in_ref[:, others] = total(other_ref[...], passed)
            out_ref[:, bit * out_half:(bit + 1) * out_half] = sent[0][:, in_half:].astype(F32)
            out_ref[:, (1 - bit) * out_half:(2 - bit) * out_half] = passed[0][:, in_half:].astype(F32)


def near_kernel(where_ref, rounded_ref, adapter_ref, total_ref, core_ref, *rest):
    from_mate, near_ref = rest[:-1], rest[-1]
    share, tokens, tile = core_ref.shape
    rank = rounded_ref.shape[0] // 2
    low = rounded_ref[:rank, :].astype(F32).T.astype(BF16)
    mine = (2 * where_ref[2] + where_ref[1]) * share
    size = from_mate[0].shape[0]
    for q in range(share):
        piece = from_mate[0][q] if q < size else from_mate[1][q - size]
        value = total_ref[mine + q, :tokens, :] + core_ref[q].astype(F32)
        value += piece.astype(F32)
        extra = jnp.dot(low, adapter_ref[:, q * tile:(q + 1) * tile], preferred_element_type=F32)
        near_ref[q] = value + adapter_scale * extra


def final_kernel(near_ref, *rest):
    pieces, out_ref = rest[:-1], rest[-1]
    share, _, tile = near_ref.shape
    for q in range(share):
        value = near_ref[q]
        for piece in pieces:
            value += piece[q].astype(F32)
        out_ref[:, q * tile:(q + 1) * tile] = value.astype(BF16)


def call(kernel, outs, scalars, arrays, aliases=None):
    smem = pl.BlockSpec(memory_space=pltpu.SMEM)
    vmem = pl.BlockSpec(memory_space=pltpu.VMEM)
    return pl.pallas_call(
        kernel,
        out_shape=outs,
        in_specs=[smem] * len(scalars) + [vmem] * len(arrays),
        out_specs=tuple(vmem for _ in outs),
        input_output_aliases=aliases or {},
        cost_estimate=pl.CostEstimate(flops=0, transcendentals=0, bytes_accessed=0),
        compiler_params=pltpu.CompilerParams(vmem_limit_bytes=4 * 1024 * 1024),
    )(*scalars, *arrays)


def on_chip(value):
    return pltpu.with_memory_space_constraint(value, pltpu.VMEM)


def after(value, *needed):
    return lax.optimization_barrier((value,) + needed)[0]


def make_body(n_parts, n_row, n_dp):
    chips = n_row // 2
    group = n_dp // 2

    def core_swap(value):
        return lax.ppermute(value, "row", [(i, i ^ 1) for i in range(n_row)])

    def chip_shift(value, d):
        pairs = [(2 * a + c, 2 * ((a + d) % chips) + c) for a in range(chips) for c in range(2)]
        return lax.ppermute(value, "row", pairs)

    def mate_swap(value):
        return lax.ppermute(value, "dp", [(i, i ^ 1) for i in range(n_dp)])

    def group_shift(value, d):
        pairs = [(2 * a + h, 2 * ((a + d) % group) + h) for a in range(group) for h in range(2)]
        return lax.ppermute(value, "dp", pairs)

    def part_shift(value, d):
        return lax.ppermute(value, "parts", [(i, (i + d) % n_parts) for i in range(n_parts)])

    def body(activations, cotangent, forget_labels, kept_blocks, block_ids, adapter_a, output_adapter):
        tokens, shard_rows = activations.shape
        rank = adapter_a.shape[1]
        feats = cotangent.shape[1]
        slots, tile = kept_blocks.shape[1], kept_blocks.shape[-1]
        row_blocks = shard_rows // tile
        col_blocks = D // tile
        share = col_blocks // n_row
        part = lax.axis_index("parts")
        row_index = lax.axis_index("row")
        dp_index = lax.axis_index("dp")
        where = jnp.stack([
            part, lax.rem(row_index, 2), lax.div(row_index, 2),
            lax.rem(dp_index, 2), lax.div(dp_index, 2), jnp.int32(share),
        ]).astype(jnp.int32)
        blocks = kept_blocks[0]
        ids = block_ids[0]
        labels = forget_labels[None, :]

        held = slots // n_parts
        sizes = [held * k // 32 for k in (16, 10, 6)]
        starts = [sum(sizes[:k]) for k in range(len(sizes))]
        leaving_chunks = [
            lax.dynamic_slice_in_dim(blocks, part * held + start, size, axis=0)
            for start, size in zip(starts, sizes)
        ]
        known = jnp.maximum(ids, 0)
        code = jnp.stack([
            jnp.where(ids >= 0, lax.div(known, col_blocks), -1),
            jnp.where(ids >= 0, lax.rem(known, col_blocks), 0),
        ]).astype(BF16)
        code = jnp.pad(code, ((0, tile - 2), (0, tile - slots)))[None]
        soon = core_swap(after(ids, leaving_chunks[0]))
        leaving_chunks[1] = jnp.concatenate([leaving_chunks[1], code], axis=0)
        leaving_chunks[1:] = [after(chunk, soon) for chunk in leaving_chunks[1:]]
        direct = [
            (group_shift(leaving_chunks[k], d), (d - 1, 0, starts[k], sizes[k]))
            for d in range(1, group) for k in range(len(starts))
        ]
        mate_activations = mate_swap(activations)

        (both,) = call(
            low_rank_kernel, (jax.ShapeDtypeStruct((2 * rank, tokens), F32),), (),
            (activations, after(adapter_a, soon).T, cotangent, after(output_adapter, soon), labels),
        )
        both = both + core_swap(both)
        rounded, kept, pack = call(
            own_grad_kernel,
            (
                jax.ShapeDtypeStruct((2 * rank, tokens), BF16),
                jax.ShapeDtypeStruct((rank, feats // 2), F32),
                jax.ShapeDtypeStruct((rank, feats // 2 + tokens), BF16),
            ),
            (where,), (cotangent, labels, both) + tuple(chip_shift(both, d) for d in range(1, chips)),
        )
        mate_pack = mate_swap(pack)

        def chunk(items, k):
            return [item for item in items if item[1][2] == starts[k]]

        def plan(items):
            return dict(places=[item[1] for item in items], parts=n_parts, held=held, col_blocks=col_blocks)

        def values(items):
            return tuple(item[0] for item in items)

        total_shape = pltpu.VMEM((col_blocks + 1, 2 * tokens, tile), F32)
        total, tiles = call(
            functools.partial(first_kernel, col_blocks=col_blocks),
            (total_shape, pltpu.VMEM((row_blocks, 2 * tokens, tile), BF16)),
            (after(where, rounded, leaving_chunks[-1]), ids), (activations, mate_activations, blocks),
        )
        in_half, both_halves = shard_rows // 2, (shard_rows + feats) // 2
        half_grads, other_grads = call(
            pair_grad_kernel,
            (jax.ShapeDtypeStruct((rank, both_halves), BF16), jax.ShapeDtypeStruct((rank, in_half), BF16)),
            (where,), (rounded, activations, mate_activations, kept, mate_pack),
        )
        far_grads = [group_shift(half_grads, d) for d in range(1, group)]

        (all_ids,) = call(
            functools.partial(ids_kernel, col_blocks=col_blocks),
            (jax.ShapeDtypeStruct((group - 1, tile), jnp.int32),), (),
            tuple(value for value, place in direct if place[2] == starts[1]),
        )
        gates = {starts[0]: (rounded, mate_activations), starts[1]: (total,), starts[2]: (half_grads,)}
        swapped = [
            (part_shift(after(value, *gates[start])[:size], e), (source, e, start, size))
            for value, (source, _, start, size) in direct for e in range(1, n_parts)
        ]
        more = direct + chunk(swapped, 0) + chunk(swapped, 1)
        last = chunk(swapped, 2)

        (total,) = call(
            functools.partial(more_kernel, **plan(more)), (total_shape,), (where, all_ids),
            (on_chip(tiles), on_chip(total)) + values(more), {3: 0},
        )
        small = share // 4
        half = share // 2

        def far_piece(size):
            return pltpu.VMEM((chips - 1, size, tokens, tile), BF16)

        def near_piece(size):
            return pltpu.VMEM((size, tokens, tile), BF16)

        total, *sends = call(
            functools.partial(last_kernel, block_count=len(last), **plan(last)),
            (total_shape,) + (far_piece(small),) * 4 + (near_piece(share),)
            + (far_piece(half),) * 2 + (near_piece(share),),
            (after(where, half_grads), all_ids), (on_chip(tiles), on_chip(total)) + values(last), {3: 0},
        )

        cores = [core_swap(value) for value in sends[:5]]

        def for_chips(pieces, token, block, *needed):
            size = sum(piece.shape[1] for piece in pieces)
            (leaving,) = call(
                functools.partial(chip_kernel, token=token, block=block), (far_piece(size),),
                (after(where, *needed) if needed else where,), (on_chip(total),) + tuple(pieces),
            )
            return leaving, [chip_shift(leaving[d - 1], d) for d in range(1, chips)]

        leaving_first, pieces_first = for_chips(cores[:1], tokens, 0)
        leaving_second, pieces_second = for_chips(cores[1:4], tokens, small, leaving_first)
        cores += [core_swap(after(value, leaving_second)) for value in sends[5:]]
        leaving_own, own_pieces = for_chips(cores[5:7], 0, 0)
        far_grads = [after(value, *pieces_first) for value in far_grads]
        passing = call(
            functools.partial(forward_kernel, in_half=in_half),
            tuple(jax.ShapeDtypeStruct((rank, in_half if d else both_halves), BF16) for d in range(group - 1)),
            (where,), (half_grads,) + tuple(far_grads),
        )
        mate_grads = [mate_swap(value) for value in passing]

        def for_mate(pieces, size, block, *needed):
            (value,) = call(
                functools.partial(mate_kernel, block=block), (near_piece(size),),
                (after(where, *needed) if needed else where,), (on_chip(total), cores[4]) + tuple(pieces),
            )
            return mate_swap(value)

        from_mate_first = for_mate(pieces_first, small, 0)
        from_mate = [
            from_mate_first, for_mate(pieces_second, share - small, small, from_mate_first, *mate_grads),
        ]
        in_grad, out_grad = call(
            grad_sum_kernel,
            (jax.ShapeDtypeStruct((rank, shard_rows), F32), jax.ShapeDtypeStruct((rank, feats), F32)),
            (where,), (half_grads, other_grads) + tuple(far_grads) + tuple(passing) + tuple(mate_grads),
        )
        (near,) = call(
            near_kernel, (pltpu.VMEM((share, tokens, tile), F32),), (where,),
            (rounded, output_adapter, on_chip(total), cores[7]) + tuple(from_mate),
        )
        (projected,) = call(
            final_kernel, (jax.ShapeDtypeStruct((tokens, feats), BF16),), (), (on_chip(near),) + tuple(own_pieces),
        )
        return projected, in_grad.T, out_grad

    return body


def solution(mesh):
    placed = (
        P(("parts", "dp"), "row"),
        P(("parts", "dp"), "row"),
        P(("parts", "dp")),
        P("row", "dp", None, None),
        P("row", "dp"),
        P("row", None),
        P(None, "row"),
    )
    return jax.shard_map(
        make_body(mesh.shape["parts"], mesh.shape["row"], mesh.shape["dp"]),
        mesh=mesh,
        in_specs=placed,
        out_specs=(P(("parts", "dp"), "row"), P(("parts", "row"), None), P("parts", "row")),
        check_vma=False,
    )
```

```python
import functools

import jax
import jax.numpy as jnp
from jax import lax
from jax.experimental import pallas as pl
from jax.experimental.pallas import tpu as pltpu
from jax.sharding import PartitionSpec as P

D = 8192

adapter_scale = 2.0

F32 = jnp.float32
BF16 = jnp.bfloat16


def add_blocks(total_ref, tiles_ref, blocks_ref, count, ident_at, col_blocks):
    unroll = max(u for u in range(1, 9) if count % u == 0)

    def one(step, carry):
        for u in range(unroll):
            k = step * unroll + u
            ident = ident_at(k)
            known = jnp.maximum(ident, 0)
            row = lax.div(known, col_blocks)
            col = jnp.where(ident >= 0, lax.rem(known, col_blocks), col_blocks)
            total_ref[col] += jnp.dot(tiles_ref[row], blocks_ref[k], preferred_element_type=F32)
        return carry

    lax.fori_loop(0, count // unroll, one, 0)


def add_arrivals(where_ref, ids_ref, tiles_ref, blocks, total_ref, places, parts, held, col_blocks):
    for blocks_ref, (source, shift, start, size) in zip(blocks, places):
        base = lax.rem(where_ref[0] + (parts - shift), parts) * held + start
        add_blocks(
            total_ref, tiles_ref, blocks_ref, size, lambda k: ids_ref[source, base + k], col_blocks
        )


def ids_kernel(*refs, col_blocks):
    coded, ids_ref = refs[:-1], refs[-1]
    for source, ref in enumerate(coded):
        code = ref[ref.shape[0] - 1].astype(F32)
        ids_ref[source:source + 1, :] = (code[0:1, :] * col_blocks + code[1:2, :]).astype(jnp.int32)


def first_kernel(where_ref, ids_ref, own_ref, mate_ref, own_blocks_ref, total_ref, tiles_ref, *, col_blocks):
    row_blocks, _, tile = tiles_ref.shape
    tokens = own_ref.shape[0]
    total_ref[...] = jnp.zeros_like(total_ref)
    for i in range(row_blocks):
        tiles_ref[i, :tokens, :] = own_ref[:, i * tile:(i + 1) * tile]
        tiles_ref[i, tokens:, :] = mate_ref[:, i * tile:(i + 1) * tile]
    add_blocks(
        total_ref, tiles_ref, own_blocks_ref, own_blocks_ref.shape[0], lambda k: ids_ref[k], col_blocks
    )


def more_kernel(where_ref, ids_ref, tiles_ref, old_ref, *rest, **plan):
    add_arrivals(where_ref, ids_ref, tiles_ref, rest[:-1], rest[-1], **plan)


def last_kernel(where_ref, ids_ref, tiles_ref, old_ref, *rest, block_count, **plan):
    blocks, total_ref, sends = rest[:block_count], rest[block_count], rest[block_count + 1:]
    add_arrivals(where_ref, ids_ref, tiles_ref, blocks, total_ref, **plan)
    far_mate, near_mate, far_own, near_own = sends[:4], sends[4:6], sends[6:8], sends[8:]
    tokens, share = near_own[0].shape[1], near_own[0].shape[0]
    chips = far_own[0].shape[0] + 1

    def copy(pieces, token, d):
        to_chip = lax.rem(where_ref[2] + d, chips)
        block = (2 * to_chip + 1 - where_ref[1]) * share
        for piece in pieces:
            target = piece.at[d - 1] if d > 0 else piece
            for k in range(target.shape[0]):
                target[k] = total_ref[block + k, token:token + tokens, :].astype(BF16)
            block = block + target.shape[0]

    for d in range(1, chips):
        copy(far_mate, tokens, d)
    copy(near_mate, tokens, 0)
    for d in range(1, chips):
        copy(far_own, 0, d)
    copy(near_own, 0, 0)


def chip_kernel(where_ref, total_ref, *rest, token, block):
    pieces, leaving_ref = rest[:-1], rest[-1]
    others, _, tokens, _ = leaving_ref.shape
    chips = others + 1
    for d in range(1, chips):
        to_chip = lax.rem(where_ref[2] + d, chips)
        first = (2 * to_chip + where_ref[1]) * where_ref[5] + block
        done = 0
        for piece in pieces:
            for k in range(piece.shape[1]):
                value = total_ref[first + done, token:token + tokens, :] + piece[d - 1, k].astype(F32)
                leaving_ref[d - 1, done] = value.astype(BF16)
                done += 1


def mate_kernel(where_ref, total_ref, core_ref, *rest, block):
    pieces, out_ref = rest[:-1], rest[-1]
    size, tokens, _ = out_ref.shape
    first = (2 * where_ref[2] + where_ref[1]) * where_ref[5] + block
    for k in range(size):
        value = total_ref[first + k, tokens:, :] + core_ref[k].astype(F32)
        for piece in pieces:
            value += piece[k].astype(F32)
        out_ref[k] = value.astype(BF16)


def ordered_sum(own, received, place):
    count = len(received) + 1
    if count == 1:
        return own
    if count == 2:
        return own + received[0]
    total = None
    for member in range(count):
        value = own
        for d, other in enumerate(received, 1):
            value = jnp.where(lax.rem(place + (count - d), count) == member, other, value)
        total = value if total is None else total + value
    return total


CONTRACT_LAST = (((1,), (1,)), ((), ()))


def low_rank_kernel(acts_ref, adapter_a_ref, cot_ref, adapter_ref, labels_ref, out_ref):
    rank = adapter_a_ref.shape[0]
    signs = (1 - 2 * labels_ref[...]).astype(F32)
    out_ref[:rank, :] = lax.dot_general(adapter_a_ref[...], acts_ref[...], CONTRACT_LAST, preferred_element_type=F32)
    out_ref[rank:, :] = signs * lax.dot_general(
        adapter_ref[...], cot_ref[...], CONTRACT_LAST, preferred_element_type=F32
    )


def own_grad_kernel(where_ref, cot_ref, labels_ref, both_ref, *rest):
    received, (rounded_ref, kept_ref, pack_ref) = rest[:-3], rest[-3:]
    half = kept_ref.shape[1]
    rounded = ordered_sum(both_ref[...], [ref[...] for ref in received], where_ref[2]).astype(BF16)
    rounded_ref[...] = rounded
    rank = rounded.shape[0] // 2
    signs = (1 - 2 * labels_ref[...]).astype(F32)
    signed_low = (rounded[:rank].astype(F32) * signs).astype(BF16)

    def grad(bit):
        cols = cot_ref[:, bit * half:(bit + 1) * half]
        return adapter_scale * jnp.dot(signed_low, cols, preferred_element_type=F32)

    for bit in range(2):
        @pl.when(where_ref[3] == bit)
        def _():
            kept_ref[...] = grad(bit)
            pack_ref[:, :half] = grad(1 - bit).astype(BF16)
    pack_ref[:, half:] = rounded[rank:]


def pair_grad_kernel(
    where_ref, rounded_ref, acts_ref, mate_acts_ref, kept_ref, mate_pack_ref, half_ref, other_ref
):
    rank, in_half, out_half = rounded_ref.shape[0] // 2, other_ref.shape[1], kept_ref.shape[1]
    back, mate_back = rounded_ref[rank:, :], mate_pack_ref[:, out_half:]

    def grad(bit):
        cols = slice(bit * in_half, (bit + 1) * in_half)
        own = jnp.dot(back, acts_ref[:, cols], preferred_element_type=F32)
        mate = jnp.dot(mate_back, mate_acts_ref[:, cols], preferred_element_type=F32)
        return (adapter_scale * (own + mate)).astype(BF16)

    for bit in range(2):
        @pl.when(where_ref[3] == bit)
        def _():
            half_ref[:, :in_half] = grad(bit)
            other_ref[...] = grad(1 - bit)
    half_ref[:, in_half:] = (kept_ref[...] + mate_pack_ref[:, :out_half].astype(F32)).astype(BF16)


def forward_kernel(where_ref, half_ref, *rest, in_half):
    count = len(rest) // 2
    received, outs = rest[:count], rest[count:]
    for ref, out_ref in zip(received, outs):
        out_ref[:, :in_half] = ref[:, :in_half]
    total = ordered_sum(
        half_ref[:, in_half:].astype(F32), [ref[:, in_half:].astype(F32) for ref in received], where_ref[4]
    )
    outs[0][:, in_half:] = total.astype(BF16)


def grad_sum_kernel(where_ref, half_ref, other_ref, *rest):
    received, (in_ref, out_ref) = rest[:-2], rest[-2:]
    in_half, out_half = in_ref.shape[1] // 2, out_ref.shape[1] // 2
    count = len(received) // 3
    far, sent, passed = received[:count], received[count:2 * count], received[2 * count:]

    def total(own, halves):
        return ordered_sum(own.astype(F32), [ref[:, :in_half].astype(F32) for ref in halves], where_ref[4])

    for bit in range(2):
        @pl.when(where_ref[3] == bit)
        def _():
            mine, others = slice(bit * in_half, (bit + 1) * in_half), slice((1 - bit) * in_half, (2 - bit) * in_half)
            in_ref[:, mine] = total(half_ref[:, :in_half], far)
            in_ref[:, others] = total(other_ref[...], passed)
            out_ref[:, bit * out_half:(bit + 1) * out_half] = sent[0][:, in_half:].astype(F32)
            out_ref[:, (1 - bit) * out_half:(2 - bit) * out_half] = passed[0][:, in_half:].astype(F32)


def near_kernel(where_ref, rounded_ref, adapter_ref, total_ref, core_ref, *rest):
    from_mate, near_ref = rest[:-1], rest[-1]
    share, tokens, tile = core_ref.shape
    rank = rounded_ref.shape[0] // 2
    low = rounded_ref[:rank, :].astype(F32).T.astype(BF16)
    mine = (2 * where_ref[2] + where_ref[1]) * share
    size = from_mate[0].shape[0]
    for q in range(share):
        piece = from_mate[0][q] if q < size else from_mate[1][q - size]
        value = total_ref[mine + q, :tokens, :] + core_ref[q].astype(F32)
        value += piece.astype(F32)
        extra = jnp.dot(low, adapter_ref[:, q * tile:(q + 1) * tile], preferred_element_type=F32)
        near_ref[q] = value + adapter_scale * extra


def final_kernel(near_ref, *rest):
    pieces, out_ref = rest[:-1], rest[-1]
    share, _, tile = near_ref.shape
    for q in range(share):
        value = near_ref[q]
        for piece in pieces:
            value += piece[q].astype(F32)
        out_ref[:, q * tile:(q + 1) * tile] = value.astype(BF16)


def call(kernel, outs, scalars, arrays, aliases=None):
    smem = pl.BlockSpec(memory_space=pltpu.SMEM)
    vmem = pl.BlockSpec(memory_space=pltpu.VMEM)
    return pl.pallas_call(
        kernel,
        out_shape=outs,
        in_specs=[smem] * len(scalars) + [vmem] * len(arrays),
        out_specs=tuple(vmem for _ in outs),
        input_output_aliases=aliases or {},
        cost_estimate=pl.CostEstimate(flops=0, transcendentals=0, bytes_accessed=0),
        compiler_params=pltpu.CompilerParams(vmem_limit_bytes=4 * 1024 * 1024),
    )(*scalars, *arrays)


def on_chip(value):
    return pltpu.with_memory_space_constraint(value, pltpu.VMEM)


def after(value, *needed):
    return lax.optimization_barrier((value,) + needed)[0]


def make_body(n_parts, n_row, n_dp):
    chips = n_row // 2
    group = n_dp // 2

    def core_swap(value):
        return lax.ppermute(value, "row", [(i, i ^ 1) for i in range(n_row)])

    def chip_shift(value, d):
        pairs = [(2 * a + c, 2 * ((a + d) % chips) + c) for a in range(chips) for c in range(2)]
        return lax.ppermute(value, "row", pairs)

    def mate_swap(value):
        return lax.ppermute(value, "dp", [(i, i ^ 1) for i in range(n_dp)])

    def group_shift(value, d):
        pairs = [(2 * a + h, 2 * ((a + d) % group) + h) for a in range(group) for h in range(2)]
        return lax.ppermute(value, "dp", pairs)

    def part_shift(value, d):
        return lax.ppermute(value, "parts", [(i, (i + d) % n_parts) for i in range(n_parts)])

    def body(activations, cotangent, forget_labels, kept_blocks, block_ids, adapter_a, output_adapter):
        tokens, shard_rows = activations.shape
        rank = adapter_a.shape[1]
        feats = cotangent.shape[1]
        slots, tile = kept_blocks.shape[1], kept_blocks.shape[-1]
        row_blocks = shard_rows // tile
        col_blocks = D // tile
        share = col_blocks // n_row
        part = lax.axis_index("parts")
        row_index = lax.axis_index("row")
        dp_index = lax.axis_index("dp")
        where = jnp.stack([
            part, lax.rem(row_index, 2), lax.div(row_index, 2),
            lax.rem(dp_index, 2), lax.div(dp_index, 2), jnp.int32(share),
        ]).astype(jnp.int32)
        blocks = kept_blocks[0]
        ids = block_ids[0]
        labels = forget_labels[None, :]

        held = slots // n_parts
        sizes = [held * k // 32 for k in (16, 10, 6)]
        starts = [sum(sizes[:k]) for k in range(len(sizes))]
        leaving_chunks = [
            lax.dynamic_slice_in_dim(blocks, part * held + start, size, axis=0)
            for start, size in zip(starts, sizes)
        ]
        known = jnp.maximum(ids, 0)
        code = jnp.stack([
            jnp.where(ids >= 0, lax.div(known, col_blocks), -1),
            jnp.where(ids >= 0, lax.rem(known, col_blocks), 0),
        ]).astype(BF16)
        code = jnp.pad(code, ((0, tile - 2), (0, tile - slots)))[None]
        soon = core_swap(ids)
        leaving_chunks[1] = jnp.concatenate([leaving_chunks[1], code], axis=0)
        leaving_chunks = [after(chunk, soon) for chunk in leaving_chunks]
        direct = [
            (group_shift(leaving_chunks[k], d), (d - 1, 0, starts[k], sizes[k]))
            for d in range(1, group) for k in range(len(starts))
        ]
        mate_activations = mate_swap(activations)

        (both,) = call(
            low_rank_kernel, (jax.ShapeDtypeStruct((2 * rank, tokens), F32),), (),
            (activations, after(adapter_a, soon).T, cotangent, after(output_adapter, soon), labels),
        )
        both = both + core_swap(both)
        rounded, kept, pack = call(
            own_grad_kernel,
            (
                jax.ShapeDtypeStruct((2 * rank, tokens), BF16),
                jax.ShapeDtypeStruct((rank, feats // 2), F32),
                jax.ShapeDtypeStruct((rank, feats // 2 + tokens), BF16),
            ),
            (where,), (cotangent, labels, both) + tuple(chip_shift(both, d) for d in range(1, chips)),
        )
        mate_pack = mate_swap(pack)

        def chunk(items, k):
            return [item for item in items if item[1][2] == starts[k]]

        def plan(items):
            return dict(places=[item[1] for item in items], parts=n_parts, held=held, col_blocks=col_blocks)

        def values(items):
            return tuple(item[0] for item in items)

        total_shape = pltpu.VMEM((col_blocks + 1, 2 * tokens, tile), F32)
        total, tiles = call(
            functools.partial(first_kernel, col_blocks=col_blocks),
            (total_shape, pltpu.VMEM((row_blocks, 2 * tokens, tile), BF16)),
            (after(where, rounded, leaving_chunks[-1]), ids), (activations, mate_activations, blocks),
        )
        in_half, both_halves = shard_rows // 2, (shard_rows + feats) // 2
        half_grads, other_grads = call(
            pair_grad_kernel,
            (jax.ShapeDtypeStruct((rank, both_halves), BF16), jax.ShapeDtypeStruct((rank, in_half), BF16)),
            (where,), (rounded, activations, mate_activations, kept, mate_pack),
        )
        far_grads = [group_shift(half_grads, d) for d in range(1, group)]

        (all_ids,) = call(
            functools.partial(ids_kernel, col_blocks=col_blocks),
            (jax.ShapeDtypeStruct((group - 1, tile), jnp.int32),), (),
            tuple(value for value, place in direct if place[2] == starts[1]),
        )
        gates = {starts[0]: (rounded,), starts[1]: (total,), starts[2]: (half_grads,)}
        swapped = [
            (part_shift(after(value, *gates[start])[:size], e), (source, e, start, size))
            for value, (source, _, start, size) in direct for e in range(1, n_parts)
        ]
        more = direct + chunk(swapped, 0) + chunk(swapped, 1)
        last = chunk(swapped, 2)

        (total,) = call(
            functools.partial(more_kernel, **plan(more)), (total_shape,), (where, all_ids),
            (on_chip(tiles), on_chip(total)) + values(more), {3: 0},
        )
        small = max(1, 2 * share // 16)
        rest = share - small
        thirds = (rest - 2 * (rest // 3), rest // 3, rest // 3)
        half = share // 2

        def far_piece(size):
            return pltpu.VMEM((chips - 1, size, tokens, tile), BF16)

        def near_piece(size):
            return pltpu.VMEM((size, tokens, tile), BF16)

        total, *sends = call(
            functools.partial(last_kernel, block_count=len(last), **plan(last)),
            (total_shape, far_piece(small)) + tuple(far_piece(size) for size in thirds)
            + (near_piece(small), near_piece(rest))
            + (far_piece(half),) * 2 + (near_piece(share),),
            (after(where, half_grads), all_ids), (on_chip(tiles), on_chip(total)) + values(last), {3: 0},
        )

        cores = [core_swap(value) for value in sends[:6]]

        def for_chips(pieces, token, block, *needed):
            size = sum(piece.shape[1] for piece in pieces)
            (leaving,) = call(
                functools.partial(chip_kernel, token=token, block=block), (far_piece(size),),
                (after(where, *needed) if needed else where,), (on_chip(total),) + tuple(pieces),
            )
            return leaving, [chip_shift(leaving[d - 1], d) for d in range(1, chips)]

        leaving_first, pieces_first = for_chips(cores[:1], tokens, 0)
        leaving_second, pieces_second = for_chips(cores[1:4], tokens, small, leaving_first)
        cores += [core_swap(after(value, leaving_second)) for value in sends[6:]]
        leaving_own, own_pieces = for_chips(cores[6:8], 0, 0)
        def for_mate(core_got, pieces, block, *needed):
            (value,) = call(
                functools.partial(mate_kernel, block=block), (near_piece(core_got.shape[0]),),
                (after(where, *needed) if needed else where,), (on_chip(total), core_got) + tuple(pieces),
            )
            return mate_swap(value)

        from_mate_first = for_mate(cores[4], pieces_first, 0)
        far_grads = [after(value, from_mate_first) for value in far_grads]
        passing = call(
            functools.partial(forward_kernel, in_half=in_half),
            tuple(jax.ShapeDtypeStruct((rank, in_half if d else both_halves), BF16) for d in range(group - 1)),
            (where,), (half_grads,) + tuple(far_grads),
        )
        mate_grads = [mate_swap(value) for value in passing]
        from_mate = [
            from_mate_first, for_mate(cores[5], pieces_second, small, *mate_grads),
        ]
        in_grad, out_grad = call(
            grad_sum_kernel,
            (jax.ShapeDtypeStruct((rank, shard_rows), F32), jax.ShapeDtypeStruct((rank, feats), F32)),
            (where,), (half_grads, other_grads) + tuple(far_grads) + tuple(passing) + tuple(mate_grads),
        )
        (near,) = call(
            near_kernel, (pltpu.VMEM((share, tokens, tile), F32),), (where,),
            (rounded, output_adapter, on_chip(total), cores[8]) + tuple(from_mate),
        )
        (projected,) = call(
            final_kernel, (jax.ShapeDtypeStruct((tokens, feats), BF16),), (), (on_chip(near),) + tuple(own_pieces),
        )
        return projected, in_grad.T, out_grad

    return body


def solution(mesh):
    placed = (
        P(("parts", "dp"), "row"),
        P(("parts", "dp"), "row"),
        P(("parts", "dp")),
        P("row", "dp", None, None),
        P("row", "dp"),
        P("row", None),
        P(None, "row"),
    )
    return jax.shard_map(
        make_body(mesh.shape["parts"], mesh.shape["row"], mesh.shape["dp"]),
        mesh=mesh,
        in_specs=placed,
        out_specs=(P(("parts", "dp"), "row"), P(("parts", "row"), None), P("parts", "row")),
        check_vma=False,
    )
```

```python
import functools

import jax
import jax.numpy as jnp
from jax import lax
from jax.experimental import pallas as pl
from jax.experimental.pallas import tpu as pltpu
from jax.sharding import PartitionSpec as P

D = 8192

adapter_scale = 2.0

F32 = jnp.float32
BF16 = jnp.bfloat16


def add_blocks(total_ref, tiles_ref, blocks_ref, count, ident_at, col_blocks):
    unroll = max(u for u in range(1, 9) if count % u == 0)

    def one(step, carry):
        for u in range(unroll):
            k = step * unroll + u
            ident = ident_at(k)
            known = jnp.maximum(ident, 0)
            row = lax.div(known, col_blocks)
            col = jnp.where(ident >= 0, lax.rem(known, col_blocks), col_blocks)
            total_ref[col] += jnp.dot(tiles_ref[row], blocks_ref[k], preferred_element_type=F32)
        return carry

    lax.fori_loop(0, count // unroll, one, 0)


def add_arrivals(where_ref, ids_ref, tiles_ref, blocks, total_ref, places, parts, held, col_blocks):
    for blocks_ref, (source, shift, start, size) in zip(blocks, places):
        base = lax.rem(where_ref[0] + (parts - shift), parts) * held + start
        add_blocks(
            total_ref, tiles_ref, blocks_ref, size, lambda k: ids_ref[source, base + k], col_blocks
        )


def ids_kernel(*refs, col_blocks):
    coded, ids_ref = refs[:-1], refs[-1]
    for source, ref in enumerate(coded):
        code = ref[ref.shape[0] - 1].astype(F32)
        ids_ref[source:source + 1, :] = (code[0:1, :] * col_blocks + code[1:2, :]).astype(jnp.int32)


def first_kernel(where_ref, ids_ref, own_ref, mate_ref, own_blocks_ref, total_ref, tiles_ref, *, col_blocks):
    row_blocks, _, tile = tiles_ref.shape
    tokens = own_ref.shape[0]
    total_ref[...] = jnp.zeros_like(total_ref)
    for i in range(row_blocks):
        tiles_ref[i, :tokens, :] = own_ref[:, i * tile:(i + 1) * tile]
        tiles_ref[i, tokens:, :] = mate_ref[:, i * tile:(i + 1) * tile]
    add_blocks(
        total_ref, tiles_ref, own_blocks_ref, own_blocks_ref.shape[0], lambda k: ids_ref[k], col_blocks
    )


def more_kernel(where_ref, ids_ref, tiles_ref, old_ref, *rest, **plan):
    add_arrivals(where_ref, ids_ref, tiles_ref, rest[:-1], rest[-1], **plan)


def last_kernel(where_ref, ids_ref, tiles_ref, old_ref, *rest, block_count, **plan):
    blocks, total_ref, sends = rest[:block_count], rest[block_count], rest[block_count + 1:]
    add_arrivals(where_ref, ids_ref, tiles_ref, blocks, total_ref, **plan)
    far_mate, near_mate, far_own, near_own = sends[:4], sends[4:5], sends[5:7], sends[7:]
    tokens, share = near_own[0].shape[1], near_own[0].shape[0]
    chips = far_own[0].shape[0] + 1

    def copy(pieces, token, d):
        to_chip = lax.rem(where_ref[2] + d, chips)
        block = (2 * to_chip + 1 - where_ref[1]) * share
        for piece in pieces:
            target = piece.at[d - 1] if d > 0 else piece
            for k in range(target.shape[0]):
                target[k] = total_ref[block + k, token:token + tokens, :].astype(BF16)
            block = block + target.shape[0]

    for d in range(1, chips):
        copy(far_mate, tokens, d)
    copy(near_mate, tokens, 0)
    for d in range(1, chips):
        copy(far_own, 0, d)
    copy(near_own, 0, 0)


def chip_kernel(where_ref, total_ref, *rest, token, block):
    pieces, leaving_ref = rest[:-1], rest[-1]
    others, _, tokens, _ = leaving_ref.shape
    chips = others + 1
    for d in range(1, chips):
        to_chip = lax.rem(where_ref[2] + d, chips)
        first = (2 * to_chip + where_ref[1]) * where_ref[5] + block
        done = 0
        for piece in pieces:
            for k in range(piece.shape[1]):
                value = total_ref[first + done, token:token + tokens, :] + piece[d - 1, k].astype(F32)
                leaving_ref[d - 1, done] = value.astype(BF16)
                done += 1


def mate_kernel(where_ref, total_ref, core_ref, *rest, block):
    pieces, out_ref = rest[:-1], rest[-1]
    size, tokens, _ = out_ref.shape
    first = (2 * where_ref[2] + where_ref[1]) * where_ref[5] + block
    for k in range(size):
        value = total_ref[first + k, tokens:, :] + core_ref[block + k].astype(F32)
        for piece in pieces:
            value += piece[k].astype(F32)
        out_ref[k] = value.astype(BF16)


def ordered_sum(own, received, place):
    count = len(received) + 1
    if count == 1:
        return own
    if count == 2:
        return own + received[0]
    total = None
    for member in range(count):
        value = own
        for d, other in enumerate(received, 1):
            value = jnp.where(lax.rem(place + (count - d), count) == member, other, value)
        total = value if total is None else total + value
    return total


CONTRACT_LAST = (((1,), (1,)), ((), ()))


def low_rank_kernel(acts_ref, adapter_a_ref, cot_ref, adapter_ref, labels_ref, out_ref):
    rank = adapter_a_ref.shape[0]
    signs = (1 - 2 * labels_ref[...]).astype(F32)
    out_ref[:rank, :] = lax.dot_general(adapter_a_ref[...], acts_ref[...], CONTRACT_LAST, preferred_element_type=F32)
    out_ref[rank:, :] = signs * lax.dot_general(
        adapter_ref[...], cot_ref[...], CONTRACT_LAST, preferred_element_type=F32
    )


def own_grad_kernel(where_ref, cot_ref, labels_ref, both_ref, *rest):
    received, (rounded_ref, pack_ref) = rest[:-2], rest[-2:]
    feats = cot_ref.shape[1]
    rounded = ordered_sum(both_ref[...], [ref[...] for ref in received], where_ref[2]).astype(BF16)
    rounded_ref[...] = rounded
    rank = rounded.shape[0] // 2
    signs = (1 - 2 * labels_ref[...]).astype(F32)
    signed_low = (rounded[:rank].astype(F32) * signs).astype(BF16)
    grad = jnp.dot(signed_low, cot_ref[...], preferred_element_type=F32)
    pack_ref[:, :feats] = (adapter_scale * grad).astype(BF16)
    pack_ref[:, feats:] = rounded[rank:]


def pair_grad_kernel(
    where_ref, rounded_ref, acts_ref, mate_acts_ref, pack_ref, mate_pack_ref, half_ref, other_ref
):
    rank, shard_rows = rounded_ref.shape[0] // 2, acts_ref.shape[1]
    feats = pack_ref.shape[1] - rounded_ref.shape[1]
    in_half, out_half = shard_rows // 2, feats // 2
    back, mate_back = rounded_ref[rank:, :], mate_pack_ref[:, feats:]

    def fill(bit, out_ref):
        cols = slice(bit * in_half, (bit + 1) * in_half)
        grad = jnp.dot(back, acts_ref[:, cols], preferred_element_type=F32)
        grad = grad + jnp.dot(mate_back, mate_acts_ref[:, cols], preferred_element_type=F32)
        out_ref[:, :in_half] = (adapter_scale * grad).astype(BF16)
        cols = slice(bit * out_half, (bit + 1) * out_half)
        grad = pack_ref[:, cols].astype(F32) + mate_pack_ref[:, cols].astype(F32)
        out_ref[:, in_half:] = grad.astype(BF16)

    for bit in range(2):
        @pl.when(where_ref[3] == bit)
        def _():
            fill(bit, half_ref)
            fill(1 - bit, other_ref)


def grad_sum_kernel(where_ref, half_ref, other_ref, *rest):
    received, (in_ref, out_ref) = rest[:-2], rest[-2:]
    in_half, out_half = in_ref.shape[1] // 2, out_ref.shape[1] // 2
    count = len(received) // 2
    place = where_ref[4]

    def add(bit, own_ref, halves):
        total = ordered_sum(own_ref[...].astype(F32), [ref[...].astype(F32) for ref in halves], place)
        in_ref[:, bit * in_half:(bit + 1) * in_half] = total[:, :in_half]
        out_ref[:, bit * out_half:(bit + 1) * out_half] = total[:, in_half:]

    for bit in range(2):
        @pl.when(where_ref[3] == bit)
        def _():
            add(bit, half_ref, received[:count])
            add(1 - bit, other_ref, received[count:])


def near_kernel(where_ref, rounded_ref, adapter_ref, total_ref, core_ref, *rest):
    from_mate, near_ref = rest[:-1], rest[-1]
    share, tokens, tile = core_ref.shape
    rank = rounded_ref.shape[0] // 2
    low = rounded_ref[:rank, :].astype(F32).T.astype(BF16)
    mine = (2 * where_ref[2] + where_ref[1]) * share
    size = from_mate[0].shape[0]
    for q in range(share):
        piece = from_mate[0][q] if q < size else from_mate[1][q - size]
        value = total_ref[mine + q, :tokens, :] + core_ref[q].astype(F32)
        value += piece.astype(F32)
        extra = jnp.dot(low, adapter_ref[:, q * tile:(q + 1) * tile], preferred_element_type=F32)
        near_ref[q] = value + adapter_scale * extra


def final_kernel(near_ref, *rest):
    pieces, out_ref = rest[:-1], rest[-1]
    share, _, tile = near_ref.shape
    for q in range(share):
        value = near_ref[q]
        for piece in pieces:
            value += piece[q].astype(F32)
        out_ref[:, q * tile:(q + 1) * tile] = value.astype(BF16)


def call(kernel, outs, scalars, arrays, aliases=None):
    smem = pl.BlockSpec(memory_space=pltpu.SMEM)
    vmem = pl.BlockSpec(memory_space=pltpu.VMEM)
    return pl.pallas_call(
        kernel,
        out_shape=outs,
        in_specs=[smem] * len(scalars) + [vmem] * len(arrays),
        out_specs=tuple(vmem for _ in outs),
        input_output_aliases=aliases or {},
        cost_estimate=pl.CostEstimate(flops=0, transcendentals=0, bytes_accessed=0),
        compiler_params=pltpu.CompilerParams(vmem_limit_bytes=4 * 1024 * 1024),
    )(*scalars, *arrays)


def on_chip(value):
    return pltpu.with_memory_space_constraint(value, pltpu.VMEM)


def after(value, *needed):
    return lax.optimization_barrier((value,) + needed)[0]


def make_body(n_parts, n_row, n_dp):
    chips = n_row // 2
    group = n_dp // 2

    def core_swap(value):
        return lax.ppermute(value, "row", [(i, i ^ 1) for i in range(n_row)])

    def chip_shift(value, d):
        pairs = [(2 * a + c, 2 * ((a + d) % chips) + c) for a in range(chips) for c in range(2)]
        return lax.ppermute(value, "row", pairs)

    def mate_swap(value):
        return lax.ppermute(value, "dp", [(i, i ^ 1) for i in range(n_dp)])

    def group_shift(value, d):
        pairs = [(2 * a + h, 2 * ((a + d) % group) + h) for a in range(group) for h in range(2)]
        return lax.ppermute(value, "dp", pairs)

    def part_shift(value, d):
        return lax.ppermute(value, "parts", [(i, (i + d) % n_parts) for i in range(n_parts)])

    def body(activations, cotangent, forget_labels, kept_blocks, block_ids, adapter_a, output_adapter):
        tokens, shard_rows = activations.shape
        rank = adapter_a.shape[1]
        feats = cotangent.shape[1]
        slots, tile = kept_blocks.shape[1], kept_blocks.shape[-1]
        row_blocks = shard_rows // tile
        col_blocks = D // tile
        share = col_blocks // n_row
        part = lax.axis_index("parts")
        row_index = lax.axis_index("row")
        dp_index = lax.axis_index("dp")
        where = jnp.stack([
            part, lax.rem(row_index, 2), lax.div(row_index, 2),
            lax.rem(dp_index, 2), lax.div(dp_index, 2), jnp.int32(share),
        ]).astype(jnp.int32)
        blocks = kept_blocks[0]
        ids = block_ids[0]
        labels = forget_labels[None, :]

        held = slots // n_parts
        sizes = [held * k // 32 for k in (16, 10, 6)]
        starts = [sum(sizes[:k]) for k in range(len(sizes))]
        leaving_chunks = [
            lax.dynamic_slice_in_dim(blocks, part * held + start, size, axis=0)
            for start, size in zip(starts, sizes)
        ]
        known = jnp.maximum(ids, 0)
        code = jnp.stack([
            jnp.where(ids >= 0, lax.div(known, col_blocks), -1),
            jnp.where(ids >= 0, lax.rem(known, col_blocks), 0),
        ]).astype(BF16)
        code = jnp.pad(code, ((0, tile - 2), (0, tile - slots)))[None]
        soon = core_swap(after(ids, leaving_chunks[0]))
        leaving_chunks[1] = jnp.concatenate([leaving_chunks[1], code], axis=0)
        leaving_chunks[1:] = [after(chunk, soon) for chunk in leaving_chunks[1:]]
        direct = [
            (group_shift(leaving_chunks[k], d), (d - 1, 0, starts[k], sizes[k]))
            for d in range(1, group) for k in range(len(starts))
        ]
        mate_activations = mate_swap(activations)

        (both,) = call(
            low_rank_kernel, (jax.ShapeDtypeStruct((2 * rank, tokens), F32),), (),
            (activations, after(adapter_a, soon).T, cotangent, after(output_adapter, soon), labels),
        )
        both = both + core_swap(both)
        rounded, pack = call(
            own_grad_kernel,
            (
                jax.ShapeDtypeStruct((2 * rank, tokens), BF16),
                jax.ShapeDtypeStruct((rank, feats + tokens), BF16),
            ),
            (where,), (cotangent, labels, both) + tuple(chip_shift(both, d) for d in range(1, chips)),
        )
        mate_pack = mate_swap(pack)

        def chunk(items, k):
            return [item for item in items if item[1][2] == starts[k]]

        def plan(items):
            return dict(places=[item[1] for item in items], parts=n_parts, held=held, col_blocks=col_blocks)

        def values(items):
            return tuple(item[0] for item in items)

        total_shape = pltpu.VMEM((col_blocks + 1, 2 * tokens, tile), F32)
        total, tiles = call(
            functools.partial(first_kernel, col_blocks=col_blocks),
            (total_shape, pltpu.VMEM((row_blocks, 2 * tokens, tile), BF16)),
            (after(where, rounded, leaving_chunks[-1]), ids), (activations, mate_activations, blocks),
        )
        half_shape = jax.ShapeDtypeStruct((rank, (shard_rows + feats) // 2), BF16)
        half_grads, other_grads = call(
            pair_grad_kernel, (half_shape, half_shape), (where,), (rounded, activations, mate_activations, pack, mate_pack),
        )
        far_grads = [group_shift(half_grads, d) for d in range(1, group)]

        (all_ids,) = call(
            functools.partial(ids_kernel, col_blocks=col_blocks),
            (jax.ShapeDtypeStruct((group - 1, tile), jnp.int32),), (),
            tuple(value for value, place in direct if place[2] == starts[1]),
        )
        gates = {starts[0]: (rounded, mate_activations), starts[1]: (total,), starts[2]: (half_grads,)}
        swapped = [
            (part_shift(after(value, *gates[start])[:size], e), (source, e, start, size))
            for value, (source, _, start, size) in direct for e in range(1, n_parts)
        ]
        more = direct + chunk(swapped, 0)
        last = chunk(swapped, 1) + chunk(swapped, 2)

        (total,) = call(
            functools.partial(more_kernel, **plan(more)), (total_shape,), (where, all_ids),
            (on_chip(tiles), on_chip(total)) + values(more), {3: 0},
        )
        small = share // 4
        half = share // 2

        def far_piece(size):
            return pltpu.VMEM((chips - 1, size, tokens, tile), BF16)

        def near_piece(size):
            return pltpu.VMEM((size, tokens, tile), BF16)

        total, *sends = call(
            functools.partial(last_kernel, block_count=len(last), **plan(last)),
            (total_shape,) + (far_piece(small),) * 4 + (near_piece(share),)
            + (far_piece(half),) * 2 + (near_piece(share),),
            (after(where, half_grads), all_ids), (on_chip(tiles), on_chip(total)) + values(last), {3: 0},
        )

        cores = [core_swap(value) for value in sends[:5]]

        def for_chips(pieces, token, block, *needed):
            size = sum(piece.shape[1] for piece in pieces)
            (leaving,) = call(
                functools.partial(chip_kernel, token=token, block=block), (far_piece(size),),
                (after(where, *needed) if needed else where,), (on_chip(total),) + tuple(pieces),
            )
            return leaving, [chip_shift(leaving[d - 1], d) for d in range(1, chips)]

        leaving_first, pieces_first = for_chips(cores[:1], tokens, 0)
        leaving_second, pieces_second = for_chips(cores[1:4], tokens, small, leaving_first)
        cores += [core_swap(after(value, leaving_second)) for value in sends[5:]]
        leaving_own, own_pieces = for_chips(cores[5:7], 0, 0)
        far_grads = [after(value, *pieces_first) for value in far_grads]
        mate_grads = [mate_swap(value) for value in far_grads]

        def for_mate(pieces, size, block, *needed):
            (value,) = call(
                functools.partial(mate_kernel, block=block), (near_piece(size),),
                (after(where, *needed) if needed else where,), (on_chip(total), cores[4]) + tuple(pieces),
            )
            return mate_swap(value)

        from_mate_first = for_mate(pieces_first, small, 0)
        from_mate = [
            from_mate_first, for_mate(pieces_second, share - small, small, from_mate_first, *mate_grads),
        ]
        in_grad, out_grad = call(
            grad_sum_kernel,
            (jax.ShapeDtypeStruct((rank, shard_rows), F32), jax.ShapeDtypeStruct((rank, feats), F32)),
            (where,), (half_grads, other_grads) + tuple(far_grads) + tuple(mate_grads),
        )
        (near,) = call(
            near_kernel, (pltpu.VMEM((share, tokens, tile), F32),), (where,),
            (rounded, output_adapter, on_chip(total), cores[7]) + tuple(from_mate),
        )
        (projected,) = call(
            final_kernel, (jax.ShapeDtypeStruct((tokens, feats), BF16),), (), (on_chip(near),) + tuple(own_pieces),
        )
        return projected, in_grad.T, out_grad

    return body


def solution(mesh):
    placed = (
        P(("parts", "dp"), "row"),
        P(("parts", "dp"), "row"),
        P(("parts", "dp")),
        P("row", "dp", None, None),
        P("row", "dp"),
        P("row", None),
        P(None, "row"),
    )
    return jax.shard_map(
        make_body(mesh.shape["parts"], mesh.shape["row"], mesh.shape["dp"]),
        mesh=mesh,
        in_specs=placed,
        out_specs=(P(("parts", "dp"), "row"), P(("parts", "row"), None), P("parts", "row")),
        check_vma=False,
    )
```

```python
import functools

import jax
import jax.numpy as jnp
from jax import lax
from jax.experimental import pallas as pl
from jax.experimental.pallas import tpu as pltpu
from jax.sharding import PartitionSpec as P

D = 8192

adapter_scale = 2.0

F32 = jnp.float32
BF16 = jnp.bfloat16


def add_blocks(total_ref, tiles_ref, blocks_ref, count, ident_at, col_blocks):
    unroll = max(u for u in range(1, 9) if count % u == 0)

    def one(step, carry):
        for u in range(unroll):
            k = step * unroll + u
            ident = ident_at(k)
            known = jnp.maximum(ident, 0)
            row = lax.div(known, col_blocks)
            col = jnp.where(ident >= 0, lax.rem(known, col_blocks), col_blocks)
            total_ref[col] += jnp.dot(tiles_ref[row], blocks_ref[k], preferred_element_type=F32)
        return carry

    lax.fori_loop(0, count // unroll, one, 0)


def add_arrivals(where_ref, ids_ref, tiles_ref, blocks, total_ref, places, parts, held, col_blocks):
    for blocks_ref, (source, shift, start, size) in zip(blocks, places):
        base = lax.rem(where_ref[0] + (parts - shift), parts) * held + start
        add_blocks(
            total_ref, tiles_ref, blocks_ref, size, lambda k: ids_ref[source, base + k], col_blocks
        )


def ids_kernel(*refs, col_blocks):
    coded, ids_ref = refs[:-1], refs[-1]
    for source, ref in enumerate(coded):
        code = ref[ref.shape[0] - 1].astype(F32)
        ids_ref[source:source + 1, :] = (code[0:1, :] * col_blocks + code[1:2, :]).astype(jnp.int32)


def first_kernel(where_ref, ids_ref, own_ref, mate_ref, own_blocks_ref, total_ref, tiles_ref, *, col_blocks):
    row_blocks, _, tile = tiles_ref.shape
    tokens = own_ref.shape[0]
    total_ref[...] = jnp.zeros_like(total_ref)
    for i in range(row_blocks):
        tiles_ref[i, :tokens, :] = own_ref[:, i * tile:(i + 1) * tile]
        tiles_ref[i, tokens:, :] = mate_ref[:, i * tile:(i + 1) * tile]
    add_blocks(
        total_ref, tiles_ref, own_blocks_ref, own_blocks_ref.shape[0], lambda k: ids_ref[k], col_blocks
    )


def more_kernel(where_ref, ids_ref, tiles_ref, old_ref, *rest, **plan):
    add_arrivals(where_ref, ids_ref, tiles_ref, rest[:-1], rest[-1], **plan)


def last_kernel(where_ref, ids_ref, tiles_ref, old_ref, *rest, block_count, **plan):
    blocks, total_ref, sends = rest[:block_count], rest[block_count], rest[block_count + 1:]
    add_arrivals(where_ref, ids_ref, tiles_ref, blocks, total_ref, **plan)
    far_mate, near_mate, far_own, near_own = sends[:4], sends[4:5], sends[5:7], sends[7:]
    tokens, share = near_own[0].shape[1], near_own[0].shape[0]
    chips = far_own[0].shape[0] + 1

    def copy(pieces, token, d):
        to_chip = lax.rem(where_ref[2] + d, chips)
        block = (2 * to_chip + 1 - where_ref[1]) * share
        for piece in pieces:
            target = piece.at[d - 1] if d > 0 else piece
            for k in range(target.shape[0]):
                target[k] = total_ref[block + k, token:token + tokens, :].astype(BF16)
            block = block + target.shape[0]

    for d in range(1, chips):
        copy(far_mate, tokens, d)
    copy(near_mate, tokens, 0)
    for d in range(1, chips):
        copy(far_own, 0, d)
    copy(near_own, 0, 0)


def chip_kernel(where_ref, total_ref, *rest, token, block):
    pieces, leaving_ref = rest[:-1], rest[-1]
    others, _, tokens, _ = leaving_ref.shape
    chips = others + 1
    for d in range(1, chips):
        to_chip = lax.rem(where_ref[2] + d, chips)
        first = (2 * to_chip + where_ref[1]) * where_ref[5] + block
        done = 0
        for piece in pieces:
            for k in range(piece.shape[1]):
                value = total_ref[first + done, token:token + tokens, :] + piece[d - 1, k].astype(F32)
                leaving_ref[d - 1, done] = value.astype(BF16)
                done += 1


def mate_kernel(where_ref, total_ref, core_ref, *rest, block):
    pieces, out_ref = rest[:-1], rest[-1]
    size, tokens, _ = out_ref.shape
    first = (2 * where_ref[2] + where_ref[1]) * where_ref[5] + block
    for k in range(size):
        value = total_ref[first + k, tokens:, :] + core_ref[block + k].astype(F32)
        for piece in pieces:
            value += piece[k].astype(F32)
        out_ref[k] = value.astype(BF16)


def ordered_sum(own, received, place):
    count = len(received) + 1
    if count == 1:
        return own
    if count == 2:
        return own + received[0]
    total = None
    for member in range(count):
        value = own
        for d, other in enumerate(received, 1):
            value = jnp.where(lax.rem(place + (count - d), count) == member, other, value)
        total = value if total is None else total + value
    return total


CONTRACT_LAST = (((1,), (1,)), ((), ()))


def low_rank_kernel(acts_ref, adapter_a_ref, cot_ref, adapter_ref, labels_ref, out_ref):
    rank = adapter_a_ref.shape[0]
    signs = (1 - 2 * labels_ref[...]).astype(F32)
    out_ref[:rank, :] = lax.dot_general(adapter_a_ref[...], acts_ref[...], CONTRACT_LAST, preferred_element_type=F32)
    out_ref[rank:, :] = signs * lax.dot_general(
        adapter_ref[...], cot_ref[...], CONTRACT_LAST, preferred_element_type=F32
    )


def own_grad_kernel(where_ref, cot_ref, labels_ref, both_ref, *rest):
    received, (rounded_ref, pack_ref) = rest[:-2], rest[-2:]
    feats = cot_ref.shape[1]
    rounded = ordered_sum(both_ref[...], [ref[...] for ref in received], where_ref[2]).astype(BF16)
    rounded_ref[...] = rounded
    rank = rounded.shape[0] // 2
    signs = (1 - 2 * labels_ref[...]).astype(F32)
    signed_low = (rounded[:rank].astype(F32) * signs).astype(BF16)
    grad = jnp.dot(signed_low, cot_ref[...], preferred_element_type=F32)
    pack_ref[:, :feats] = (adapter_scale * grad).astype(BF16)
    pack_ref[:, feats:] = rounded[rank:]


def pair_grad_kernel(
    where_ref, rounded_ref, acts_ref, mate_acts_ref, pack_ref, mate_pack_ref, half_ref, other_ref
):
    rank, shard_rows = rounded_ref.shape[0] // 2, acts_ref.shape[1]
    feats = pack_ref.shape[1] - rounded_ref.shape[1]
    in_half, out_half = shard_rows // 2, feats // 2
    back, mate_back = rounded_ref[rank:, :], mate_pack_ref[:, feats:]

    def fill(bit, out_ref):
        cols = slice(bit * in_half, (bit + 1) * in_half)
        grad = jnp.dot(back, acts_ref[:, cols], preferred_element_type=F32)
        grad = grad + jnp.dot(mate_back, mate_acts_ref[:, cols], preferred_element_type=F32)
        out_ref[:, :in_half] = (adapter_scale * grad).astype(BF16)
        cols = slice(bit * out_half, (bit + 1) * out_half)
        grad = pack_ref[:, cols].astype(F32) + mate_pack_ref[:, cols].astype(F32)
        out_ref[:, in_half:] = grad.astype(BF16)

    for bit in range(2):
        @pl.when(where_ref[3] == bit)
        def _():
            fill(bit, half_ref)
            fill(1 - bit, other_ref)


def grad_sum_kernel(where_ref, half_ref, other_ref, *rest):
    received, (in_ref, out_ref) = rest[:-2], rest[-2:]
    in_half, out_half = in_ref.shape[1] // 2, out_ref.shape[1] // 2
    count = len(received) // 2
    place = where_ref[4]

    def add(bit, own_ref, halves):
        total = ordered_sum(own_ref[...].astype(F32), [ref[...].astype(F32) for ref in halves], place)
        in_ref[:, bit * in_half:(bit + 1) * in_half] = total[:, :in_half]
        out_ref[:, bit * out_half:(bit + 1) * out_half] = total[:, in_half:]

    for bit in range(2):
        @pl.when(where_ref[3] == bit)
        def _():
            add(bit, half_ref, received[:count])
            add(1 - bit, other_ref, received[count:])


def near_kernel(where_ref, rounded_ref, adapter_ref, total_ref, core_ref, *rest):
    from_mate, near_ref = rest[:-1], rest[-1]
    share, tokens, tile = core_ref.shape
    rank = rounded_ref.shape[0] // 2
    low = rounded_ref[:rank, :].astype(F32).T.astype(BF16)
    mine = (2 * where_ref[2] + where_ref[1]) * share
    size = from_mate[0].shape[0]
    for q in range(share):
        piece = from_mate[0][q] if q < size else from_mate[1][q - size]
        value = total_ref[mine + q, :tokens, :] + core_ref[q].astype(F32)
        value += piece.astype(F32)
        extra = jnp.dot(low, adapter_ref[:, q * tile:(q + 1) * tile], preferred_element_type=F32)
        near_ref[q] = value + adapter_scale * extra


def final_kernel(near_ref, *rest):
    pieces, out_ref = rest[:-1], rest[-1]
    share, _, tile = near_ref.shape
    for q in range(share):
        value = near_ref[q]
        for piece in pieces:
            value += piece[q].astype(F32)
        out_ref[:, q * tile:(q + 1) * tile] = value.astype(BF16)


def call(kernel, outs, scalars, arrays, aliases=None):
    smem = pl.BlockSpec(memory_space=pltpu.SMEM)
    vmem = pl.BlockSpec(memory_space=pltpu.VMEM)
    return pl.pallas_call(
        kernel,
        out_shape=outs,
        in_specs=[smem] * len(scalars) + [vmem] * len(arrays),
        out_specs=tuple(vmem for _ in outs),
        input_output_aliases=aliases or {},
        cost_estimate=pl.CostEstimate(flops=0, transcendentals=0, bytes_accessed=0),
        compiler_params=pltpu.CompilerParams(vmem_limit_bytes=4 * 1024 * 1024),
    )(*scalars, *arrays)


def on_chip(value):
    return pltpu.with_memory_space_constraint(value, pltpu.VMEM)


def after(value, *needed):
    return lax.optimization_barrier((value,) + needed)[0]


def make_body(n_parts, n_row, n_dp):
    chips = n_row // 2
    group = n_dp // 2

    def core_swap(value):
        return lax.ppermute(value, "row", [(i, i ^ 1) for i in range(n_row)])

    def chip_shift(value, d):
        pairs = [(2 * a + c, 2 * ((a + d) % chips) + c) for a in range(chips) for c in range(2)]
        return lax.ppermute(value, "row", pairs)

    def mate_swap(value):
        return lax.ppermute(value, "dp", [(i, i ^ 1) for i in range(n_dp)])

    def group_shift(value, d):
        pairs = [(2 * a + h, 2 * ((a + d) % group) + h) for a in range(group) for h in range(2)]
        return lax.ppermute(value, "dp", pairs)

    def part_shift(value, d):
        return lax.ppermute(value, "parts", [(i, (i + d) % n_parts) for i in range(n_parts)])

    def body(activations, cotangent, forget_labels, kept_blocks, block_ids, adapter_a, output_adapter):
        tokens, shard_rows = activations.shape
        rank = adapter_a.shape[1]
        feats = cotangent.shape[1]
        slots, tile = kept_blocks.shape[1], kept_blocks.shape[-1]
        row_blocks = shard_rows // tile
        col_blocks = D // tile
        share = col_blocks // n_row
        part = lax.axis_index("parts")
        row_index = lax.axis_index("row")
        dp_index = lax.axis_index("dp")
        where = jnp.stack([
            part, lax.rem(row_index, 2), lax.div(row_index, 2),
            lax.rem(dp_index, 2), lax.div(dp_index, 2), jnp.int32(share),
        ]).astype(jnp.int32)
        blocks = kept_blocks[0]
        ids = block_ids[0]
        labels = forget_labels[None, :]

        held = slots // n_parts
        sizes = [held * k // 32 for k in (16, 10, 6)]
        starts = [sum(sizes[:k]) for k in range(len(sizes))]
        leaving_chunks = [
            lax.dynamic_slice_in_dim(blocks, part * held + start, size, axis=0)
            for start, size in zip(starts, sizes)
        ]
        known = jnp.maximum(ids, 0)
        code = jnp.stack([
            jnp.where(ids >= 0, lax.div(known, col_blocks), -1),
            jnp.where(ids >= 0, lax.rem(known, col_blocks), 0),
        ]).astype(BF16)
        code = jnp.pad(code, ((0, tile - 2), (0, tile - slots)))[None]
        soon = core_swap(after(ids, leaving_chunks[0]))
        leaving_chunks[1] = jnp.concatenate([leaving_chunks[1], code], axis=0)
        leaving_chunks[1:] = [after(chunk, soon) for chunk in leaving_chunks[1:]]
        direct = [
            (group_shift(leaving_chunks[k], d), (d - 1, 0, starts[k], sizes[k]))
            for d in range(1, group) for k in range(len(starts))
        ]
        mate_activations = mate_swap(activations)

        (both,) = call(
            low_rank_kernel, (jax.ShapeDtypeStruct((2 * rank, tokens), F32),), (),
            (activations, after(adapter_a, soon).T, cotangent, after(output_adapter, soon), labels),
        )
        both = both + core_swap(both)
        rounded, pack = call(
            own_grad_kernel,
            (
                jax.ShapeDtypeStruct((2 * rank, tokens), BF16),
                jax.ShapeDtypeStruct((rank, feats + tokens), BF16),
            ),
            (where,), (cotangent, labels, both) + tuple(chip_shift(both, d) for d in range(1, chips)),
        )
        mate_pack = mate_swap(pack)

        def chunk(items, k):
            return [item for item in items if item[1][2] == starts[k]]

        def plan(items):
            return dict(places=[item[1] for item in items], parts=n_parts, held=held, col_blocks=col_blocks)

        def values(items):
            return tuple(item[0] for item in items)

        total_shape = pltpu.VMEM((col_blocks + 1, 2 * tokens, tile), F32)
        total, tiles = call(
            functools.partial(first_kernel, col_blocks=col_blocks),
            (total_shape, pltpu.VMEM((row_blocks, 2 * tokens, tile), BF16)),
            (after(where, rounded, leaving_chunks[-1]), ids), (activations, mate_activations, blocks),
        )
        half_shape = jax.ShapeDtypeStruct((rank, (shard_rows + feats) // 2), BF16)
        half_grads, other_grads = call(
            pair_grad_kernel, (half_shape, half_shape), (where,), (rounded, activations, mate_activations, pack, mate_pack),
        )
        far_grads = [group_shift(half_grads, d) for d in range(1, group)]

        (all_ids,) = call(
            functools.partial(ids_kernel, col_blocks=col_blocks),
            (jax.ShapeDtypeStruct((group - 1, tile), jnp.int32),), (),
            tuple(value for value, place in direct if place[2] == starts[1]),
        )
        gates = {starts[0]: (rounded, mate_activations), starts[1]: (total,), starts[2]: (half_grads,)}
        swapped = [
            (part_shift(after(value, *gates[start])[:size], e), (source, e, start, size))
            for value, (source, _, start, size) in direct for e in range(1, n_parts)
        ]
        more = direct + chunk(swapped, 0)
        last = chunk(swapped, 1) + chunk(swapped, 2)

        (total,) = call(
            functools.partial(more_kernel, **plan(more)), (total_shape,), (where, all_ids),
            (on_chip(tiles), on_chip(total)) + values(more), {3: 0},
        )
        small = share // 4
        half = share // 2

        def far_piece(size):
            return pltpu.VMEM((chips - 1, size, tokens, tile), BF16)

        def near_piece(size):
            return pltpu.VMEM((size, tokens, tile), BF16)

        total, *sends = call(
            functools.partial(last_kernel, block_count=len(last), **plan(last)),
            (total_shape,) + (far_piece(small),) * 4 + (near_piece(share),)
            + (far_piece(half),) * 2 + (near_piece(share),),
            (after(where, half_grads), all_ids), (on_chip(tiles), on_chip(total)) + values(last), {3: 0},
        )

        cores = [core_swap(value) for value in sends[:5]]

        def for_chips(pieces, token, block, *needed):
            size = sum(piece.shape[1] for piece in pieces)
            (leaving,) = call(
                functools.partial(chip_kernel, token=token, block=block), (far_piece(size),),
                (after(where, *needed) if needed else where,), (on_chip(total),) + tuple(pieces),
            )
            return leaving, [chip_shift(leaving[d - 1], d) for d in range(1, chips)]

        leaving_first, pieces_first = for_chips(cores[:1], tokens, 0)
        leaving_second, pieces_second = for_chips(cores[1:4], tokens, small, leaving_first)
        cores += [core_swap(after(value, leaving_second)) for value in sends[5:]]
        leaving_own, own_pieces = for_chips(cores[5:7], 0, 0)
        far_grads = [after(value, *pieces_first) for value in far_grads]
        mate_grads = [mate_swap(value) for value in far_grads]

        def for_mate(pieces, size, block, *needed):
            (value,) = call(
                functools.partial(mate_kernel, block=block), (near_piece(size),),
                (after(where, *needed) if needed else where,), (on_chip(total), cores[4]) + tuple(pieces),
            )
            return mate_swap(value)

        from_mate_first = for_mate(pieces_first, small, 0)
        from_mate = [
            from_mate_first, for_mate(pieces_second, share - small, small, *mate_grads),
        ]
        in_grad, out_grad = call(
            grad_sum_kernel,
            (jax.ShapeDtypeStruct((rank, shard_rows), F32), jax.ShapeDtypeStruct((rank, feats), F32)),
            (where,), (half_grads, other_grads) + tuple(far_grads) + tuple(mate_grads),
        )
        (near,) = call(
            near_kernel, (pltpu.VMEM((share, tokens, tile), F32),), (where,),
            (rounded, output_adapter, on_chip(total), cores[7]) + tuple(from_mate),
        )
        (projected,) = call(
            final_kernel, (jax.ShapeDtypeStruct((tokens, feats), BF16),), (), (on_chip(near),) + tuple(own_pieces),
        )
        return projected, in_grad.T, out_grad

    return body


def solution(mesh):
    placed = (
        P(("parts", "dp"), "row"),
        P(("parts", "dp"), "row"),
        P(("parts", "dp")),
        P("row", "dp", None, None),
        P("row", "dp"),
        P("row", None),
        P(None, "row"),
    )
    return jax.shard_map(
        make_body(mesh.shape["parts"], mesh.shape["row"], mesh.shape["dp"]),
        mesh=mesh,
        in_specs=placed,
        out_specs=(P(("parts", "dp"), "row"), P(("parts", "row"), None), P("parts", "row")),
        check_vma=False,
    )
```
